32 devices in a mesh: groups: 2 (over y), sub: 16 (over z, x, core).
Axes of the slice: x: 2, y: 2, z: 4, core: 2. Of those that a mesh axis runs over, the one named last changes fastest.
Arguments:
- samples: bfloat16 [16896, 512], P(('groups', 'sub')), parts along dimension 0, may hold values from -6 to 6
- channel_order: int32 [512], replicated, may hold values from 0 to 511, each once
- merge_table: int32 [9, 3, 256], replicated, may hold values from 0 to 128, as said below
Outputs:
- spectra: float32 [512, 4096], P(('groups', 'sub')), parts along dimension 0
The draws below stay inside these ranges and needn't reach their ends.
There are 2 independent parts, one for each index of `groups`. The reference program is written for one: setup_inputs(seed, part) draws one part's arguments, and reference() takes and returns one part's arrays. A program takes and returns all parts, laid end to end along the dimension named above; an argument that names none is the same for every part. Nothing has to cross between parts.
Inputs may be any that keep to these rules, and one draw needn't show every extreme that they name: `channel_order`: a permutation of the 512 channels. `merge_table`: for level l, entry j is row d = j % 2**(l-1) of merged subband j // 2**(l-1); with C = max(1, 2**(l-2)) and e = 8, entries 0 and 1 lie in [e * (d // (2 e)), e * (d // (2 e)) + min(C, e)), and entry 2 equals entry 0 or entry 0 plus 1.
All inputs are finite; a program needn't handle non-finite values.
Results may differ from the reference program's by a relative error of at most 0.012.
Values may be sent and summed in bfloat16 or wider, within the bound.
A program may use at most 64 MiB of HBM per device.

```python
import math
import jax
import jax.numpy as jnp
from jax import lax

CH_DEV = 32
CROSS = 4
CHANNELS = 512
LEVELS = 9
DMAX = 256
SAMPLES = 8192
SPAN = 8448
N_SUB = 16


def draw_merge_table(key, part):
    quarter = CH_DEV // 4
    owned_rows = CH_DEV // 2
    stacked = []
    for level_num in range(1, LEVELS + 1):
        span_rows = 2 ** (level_num - 1)
        child_rows = max(1, 2 ** (level_num - 2))
        choices_wide = min(child_rows, quarter)
        entry_index = jnp.arange(DMAX, dtype=jnp.int32)
        row_base = entry_index % span_rows // owned_rows * quarter
        key_lower, key_upper, key_shift = jax.random.split(jax.random.fold_in(key, 7919 + level_num), 3)
        lower_rows = row_base + jax.random.randint(key_lower, (DMAX,), 0, choices_wide, dtype=jnp.int32)
        upper_rows = row_base + jax.random.randint(key_upper, (DMAX,), 0, choices_wide, dtype=jnp.int32)
        shifts = lower_rows + jax.random.randint(key_shift, (DMAX,), 0, 2, dtype=jnp.int32)
        stacked.append(jnp.stack([lower_rows, upper_rows, shifts], axis=0))
    return jnp.stack(stacked, axis=0)


def levels(key, extent, pieces, least, high):
    level = 1.0
    for axis_at, blocks in pieces:
        draws = jax.random.uniform(jax.random.fold_in(jax.random.fold_in(key, 6), axis_at), (blocks,), jnp.float32, least / len(pieces), high / len(pieces))
        level = level * jnp.repeat(jnp.exp(draws), extent[axis_at] // blocks).reshape((-1,) + (1,) * (len(extent) - 1 - axis_at))
    return level


def bell_draw(key, dims, deviation, most, cuts=(), kind=jnp.bfloat16):
    result = deviation * jax.random.normal(key, dims, jnp.float32)
    if cuts:
        result = result * levels(key, dims, cuts, -0.22, 0.18)
    return jnp.clip(result, -most, most).astype(kind)


def setup_inputs(seed: int = 0, part: int = 0) -> dict:
    streams_of = jax.random.split(jax.random.key(seed), 4)
    part_keys = jax.random.split(jax.random.fold_in(streams_of[3], part), 4)
    samples = bell_draw(part_keys[0], (SPAN, CHANNELS), 1.0, 6.0, ((0, 16),))
    channel_order = jax.random.permutation(streams_of[1], CHANNELS).astype(jnp.int32)
    merge_table = draw_merge_table(jax.random.fold_in(streams_of[3], 71), part)
    return dict(samples=samples, channel_order=channel_order, merge_table=merge_table)


def delay_rows(values, shifts, margin, time_axis):
    length = values.shape[time_axis]
    if time_axis == 1:
        padded = jnp.pad(values, ((0, 0), (0, margin)))
        return jax.vmap(lambda series, offset: lax.dynamic_slice_in_dim(series, offset, length))(padded, shifts)
    padded = jnp.pad(values, ((0, margin), (0, 0)))
    return jax.vmap(lambda series, offset: lax.dynamic_slice_in_dim(series, offset, length), in_axes=(1, 0), out_axes=1)(padded, shifts)


def merge_level(current, entries, child_rows, span_rows, time_axis):
    outputs = jnp.arange(entries.shape[1], dtype=jnp.int32)
    starts = 2 * child_rows * (outputs // span_rows)
    lower_rows = jnp.take(current, starts + entries[0], axis=1 - time_axis)
    upper_rows = jnp.take(current, starts + child_rows + entries[1], axis=1 - time_axis)
    moved_rows = delay_rows(upper_rows, entries[2], child_rows, time_axis)
    return (lower_rows.astype(jnp.float32) + moved_rows.astype(jnp.float32)).astype(jnp.bfloat16)


def spectrum(delays, channels):
    row_count = delays.shape[0]
    length = delays.shape[1]
    fold_size = length // 128
    first_index = jnp.arange(fold_size, dtype=jnp.int32)
    lane_index = jnp.arange(128, dtype=jnp.int32)
    half_index = jnp.arange(64, dtype=jnp.int32)
    angle_one = (2.0 * math.pi / fold_size) * ((first_index[:, None] * first_index[None, :]) % fold_size).astype(jnp.float32)
    cos_one = jnp.cos(angle_one).astype(jnp.bfloat16).astype(jnp.float32)
    sin_one = jnp.sin(angle_one).astype(jnp.bfloat16).astype(jnp.float32)
    angle_two = (2.0 * math.pi / length) * ((first_index[:, None] * lane_index[None, :]) % length).astype(jnp.float32)
    twist_cos = jnp.cos(angle_two)
    twist_sin = jnp.sin(angle_two)
    angle_three = (2.0 * math.pi / 128) * ((lane_index[:, None] * half_index[None, :]) % 128).astype(jnp.float32)
    cos_three = jnp.cos(angle_three).astype(jnp.bfloat16).astype(jnp.float32)
    sin_three = jnp.sin(angle_three).astype(jnp.bfloat16).astype(jnp.float32)
    series = delays.reshape(row_count, fold_size, 128).astype(jnp.float32)
    highest = lax.Precision.HIGHEST
    first_re = jnp.einsum("kn,rnm->rkm", cos_one, series, precision=highest)
    first_im = -jnp.einsum("kn,rnm->rkm", sin_one, series, precision=highest)
    twisted_re = (first_re * twist_cos + first_im * twist_sin).astype(jnp.bfloat16).astype(jnp.float32)
    twisted_im = (first_im * twist_cos - first_re * twist_sin).astype(jnp.bfloat16).astype(jnp.float32)
    out_re = jnp.einsum("rkn,nj->rjk", twisted_re, cos_three, precision=highest) + jnp.einsum("rkn,nj->rjk", twisted_im, sin_three, precision=highest)
    out_im = jnp.einsum("rkn,nj->rjk", twisted_im, cos_three, precision=highest) - jnp.einsum("rkn,nj->rjk", twisted_re, sin_three, precision=highest)
    power = (out_re * out_re + out_im * out_im) / (length * channels)
    return power.reshape(row_count, 64 * fold_size)


def reference(samples, channel_order, merge_table):
    current = jnp.take(samples, channel_order, axis=1).T
    for level_num in range(1, LEVELS + 1):
        current = merge_level(current, merge_table[level_num - 1], max(1, 2 ** (level_num - 2)), 2 ** (level_num - 1), 1)
    owned_rows = CH_DEV // 2
    reversal = []
    for position in range(N_SUB):
        flipped = 0
        for bit_num in range(CROSS):
            flipped = flipped | (((position >> bit_num) & 1) << (CROSS - 1 - bit_num))
        reversal.append(flipped)
    blocks = current.reshape(N_SUB, owned_rows, SPAN)
    blocks = jnp.take(blocks, jnp.array(reversal, dtype=jnp.int32), axis=0).reshape(DMAX, SPAN)
    return spectrum(blocks[:, :SAMPLES], CHANNELS)
```

```python
import functools
import math

import jax
import jax.numpy as jnp
import numpy as np
from jax import lax
from jax.experimental import pallas as pl
from jax.experimental.pallas import tpu as pltpu
from jax.sharding import PartitionSpec as P

LOCAL = 5
MESH = pl.DeviceIdType.MESH
CH_DEV = 32
SAMPLES = 8192


def from_partner(block, axis, apart):
    count = lax.axis_size(axis)
    route = []
    for low in range(count):
        high = low | 1 << apart
        if high != low and high < count:
            route += [(low, high), (high, low)]
    return lax.ppermute(block, axis, route)


def delay_rows(values, shifts, margin, time_axis):
    length = values.shape[time_axis]
    moved = values
    for bit_num in range(max(1, margin.bit_length())):
        offset = 2**bit_num
        rolled = jnp.pad(moved[:, offset:], ((0, 0), (0, offset)))
        flagged = shifts >> bit_num & 1 == 1
        flagged = flagged[:, None]
        moved = jnp.where(flagged, rolled, moved)
    return moved


def merge_level(current, entries, child_rows, span_rows, time_axis):
    outputs = jnp.arange(entries.shape[1], dtype=jnp.int32)
    starts = 2 * child_rows * (outputs // span_rows)
    lower_rows = jnp.take(current, starts + entries[0], axis=1 - time_axis)
    upper_rows = jnp.take(current, starts + child_rows + entries[1], axis=1 - time_axis)
    moved_rows = delay_rows(upper_rows, entries[2], child_rows, time_axis)
    return (lower_rows.astype(jnp.float32) + moved_rows.astype(jnp.float32)).astype(jnp.bfloat16)


def spectrum(delays, channels):
    row_count = delays.shape[0]
    length = delays.shape[1]
    fold_size = length // 128
    first_index = jnp.arange(fold_size, dtype=jnp.int32)
    lane_index = jnp.arange(128, dtype=jnp.int32)
    half_index = jnp.arange(64, dtype=jnp.int32)
    angle_one = (
        2.0
        * math.pi
        / fold_size
        * (first_index[:, None] * first_index[None, :] % fold_size).astype(jnp.float32)
    )
    cos_one = jnp.cos(angle_one).astype(jnp.bfloat16)
    sin_one = jnp.sin(angle_one).astype(jnp.bfloat16)
    angle_two = (
        2.0
        * math.pi
        / length
        * (first_index[:, None] * lane_index[None, :] % length).astype(jnp.float32)
    )
    twist_cos = jnp.cos(angle_two)
    twist_sin = jnp.sin(angle_two)
    angle_three = (
        2.0 * math.pi / 128 * (lane_index[:, None] * half_index[None, :] % 128).astype(jnp.float32)
    )
    cos_three = jnp.cos(angle_three).astype(jnp.bfloat16)
    sin_three = jnp.sin(angle_three).astype(jnp.bfloat16)
    series = delays.reshape(row_count, fold_size, 128)
    first_re = jnp.einsum("kn,rnm->rkm", cos_one, series, preferred_element_type=jnp.float32)
    first_im = -jnp.einsum("kn,rnm->rkm", sin_one, series, preferred_element_type=jnp.float32)
    twisted_re = (first_re * twist_cos + first_im * twist_sin).astype(jnp.bfloat16)
    twisted_im = (first_im * twist_cos - first_re * twist_sin).astype(jnp.bfloat16)
    out_re = jnp.einsum(
        "rkn,nj->rjk", twisted_re, cos_three, preferred_element_type=jnp.float32
    ) + jnp.einsum("rkn,nj->rjk", twisted_im, sin_three, preferred_element_type=jnp.float32)
    out_im = jnp.einsum(
        "rkn,nj->rjk", twisted_im, cos_three, preferred_element_type=jnp.float32
    ) - jnp.einsum("rkn,nj->rjk", twisted_re, sin_three, preferred_element_type=jnp.float32)
    power = (out_re * out_re + out_im * out_im) / (length * channels)
    return power.reshape(row_count, 64 * fold_size)


def local(samples, channel_order, merge_table):
    owners = lax.axis_size("sub")
    owner_index = lax.axis_index("sub")
    owned_rows = CH_DEV // 2
    quarter = CH_DEV // 4
    window = samples.shape[0]
    channels = samples.shape[1]
    ordered = jnp.take(samples, channel_order, axis=1).T.reshape(owners, CH_DEV, window)
    current = lax.all_to_all(ordered, "sub", split_axis=0, concat_axis=2, tiled=True).reshape(
        CH_DEV, window * owners
    )
    for level_num in range(1, LOCAL + 1):
        entries = lax.dynamic_slice_in_dim(
            merge_table[level_num - 1], owner_index * owned_rows, owned_rows, 1
        )
        current = merge_level(
            current, entries, max(1, 2 ** (level_num - 2)), 2 ** (level_num - 1), 1
        )
    block_index = jnp.zeros((), jnp.int32)
    for bit_num in range(owners.bit_length() - 1):
        level_num = LOCAL + bit_num + 1
        half_bit = owner_index >> bit_num & 1
        block_index = block_index * 2 + half_bit
        span_rows = owned_rows * 2 ** (bit_num + 1)
        child_rows = span_rows // 2
        subband = owner_index >> bit_num + 1
        entries = lax.dynamic_slice_in_dim(
            merge_table[level_num - 1],
            subband * span_rows + owned_rows * block_index,
            owned_rows,
            1,
        )
        kept_rows = lax.dynamic_slice_in_dim(current, half_bit * quarter, quarter, 0)
        sent_rows = lax.dynamic_slice_in_dim(current, (1 - half_bit) * quarter, quarter, 0)
        partner = from_partner(sent_rows, "sub", bit_num)
        row_base = quarter * block_index
        is_low = half_bit == 0
        lower_part = jnp.where(is_low, kept_rows, partner)
        upper_part = jnp.where(is_low, partner, kept_rows)
        lower_rows = jnp.take(lower_part, entries[0] - row_base, axis=0)
        upper_rows = jnp.take(upper_part, entries[1] - row_base, axis=0)
        moved_rows = delay_rows(upper_rows, entries[2], child_rows, 1)
        current = (lower_rows.astype(jnp.float32) + moved_rows.astype(jnp.float32)).astype(
            jnp.bfloat16
        )
    return spectrum(current[:, :SAMPLES], channels)


LANES = 128
GROUP = 8


def reversed_index(index, bits):
    flipped = 0
    for bit_num in range(bits):
        flipped = flipped * 2 + index // 2**bit_num % 2
    return flipped


def widest_shift(level_num):
    return max(1, 2 ** (level_num - 2))


def still_to_come(level_num, levels):
    return sum(widest_shift(later) for later in range(level_num + 1, levels + 1))


def rounded(values):
    return values.astype(jnp.bfloat16).astype(jnp.float32)


def transform_tables(fold_size, length):
    first_index = np.arange(fold_size)
    lane_index = np.arange(LANES)
    half_index = np.concatenate([np.arange(0, 64, 2), np.arange(1, 64, 2)])
    unit = np.float32(2.0 * math.pi)

    def angles(left, right, period):
        turns = (left[:, None] * right[None, :]) % period
        return (unit / np.float32(period)) * turns.astype(np.float32)

    one = angles(first_index, first_index, fold_size)
    first_table = np.concatenate([np.cos(one), -np.sin(one)], axis=0)
    two = angles(first_index, lane_index, length)
    twist = np.stack([np.cos(two), np.sin(two)])
    three = angles(half_index, lane_index, LANES)
    cos_three, sin_three = np.cos(three), np.sin(three)
    third_table = np.concatenate(
        [
            np.concatenate([cos_three, sin_three], axis=1),
            np.concatenate([-sin_three, cos_three], axis=1),
        ],
        axis=0,
    )
    return (
        jnp.asarray(first_table, jnp.bfloat16),
        jnp.asarray(twist, jnp.float32),
        jnp.asarray(third_table, jnp.bfloat16),
    )


def merge_kernel(
    owners,
    length,
    order_hbm,
    table_hbm,
    own_hbm,
    first_hbm,
    twist_hbm,
    third_hbm,
    out_ref,
    order_ref,
    table_ref,
    own_ref,
    first_ref,
    twist_ref,
    third_ref,
    order_wide,
    table_flat,
    choose,
    lower_at,
    upper_at,
    lane_at,
    picked,
    tables,
    halo_out,
    halo_in,
    early_out,
    late_out,
    early_in,
    late_in,
    folded,
    twisted,
    powers,
    halo_sem,
    early_send,
    early_recv,
    late_send,
    late_recv,
    load_sem,
):
    levels, _, rows = table_ref.shape
    window, channels = own_ref.shape
    held = rows // owners
    pad = -window % LANES
    own_tiles = (window + pad) // LANES
    halo_tiles = rows // LANES
    all_tiles = own_tiles + halo_tiles
    early_tiles = own_tiles - halo_tiles
    fold_size = length // LANES
    turn = window % LANES
    me = lax.axis_index("sub")
    bits = owners.bit_length() - 1

    barrier = pltpu.get_barrier_semaphore()
    for apart in range(1, owners):
        pl.semaphore_signal(
            barrier, inc=1, device_id={"sub": lax.rem(me + apart, owners)}, device_id_type=MESH
        )
    loads = [
        pltpu.make_async_copy(source, target, load_sem.at[place])
        for place, (source, target) in enumerate(
            [
                (order_hbm, order_ref),
                (own_hbm, own_ref),
                (table_hbm, table_ref),
                (first_hbm, first_ref),
                (twist_hbm, twist_ref),
                (third_hbm, third_ref),
            ]
        )
    ]
    for load in loads:
        load.start()

    lane = lax.broadcasted_iota(jnp.int32, (GROUP, LANES), 1)
    lane_rows = lax.broadcasted_iota(jnp.int32, (rows, LANES), 1)

    loads[0].wait()
    order_rows = jnp.broadcast_to(order_ref[...].astype(jnp.float32), (GROUP, channels))
    order_wide[...] = jnp.broadcast_to(order_rows.T[:, 0:1], (channels, LANES))
    lane_float = lane_rows.astype(jnp.float32)
    for half in range(2):
        wanted = order_wide[pl.ds(half, rows, stride=2), :]
        for base in range(0, channels, LANES):
            hit = (wanted == lane_float + float(base)).astype(jnp.float32)
            choose[half * rows : (half + 1) * rows, base : base + LANES] = hit.astype(jnp.bfloat16)

    loads[2].wait()
    table_flat[...] = jnp.zeros_like(table_flat)
    for level_num in range(levels):
        table_flat[3 * level_num : 3 * level_num + 3, :] = table_ref[level_num].astype(jnp.float32)
    turned = table_flat[...].T
    shifted = lane_rows + jnp.broadcast_to(turned[:, 2:3], (rows, LANES)).astype(jnp.int32)
    lane_at[0] = shifted

    def level_one(begin, end):
        size = end - begin
        both = lax.dot_general(
            choose[...],
            own_ref[begin:end, :],
            (((1,), (1,)), ((), ())),
            preferred_element_type=jnp.float32,
        )
        whole = -(-size // LANES) * LANES
        picked[:, begin : begin + size] = both
        return whole // LANES

    def summed(tile, last):
        at = tile * LANES
        near = jnp.take_along_axis(picked[rows:, at : at + LANES], shifted & (LANES - 1), axis=1)
        return near

    loads[1].wait()
    first_tiles = level_one(0, rows)
    near = [summed(tile, False) for tile in range(halo_tiles)]
    level_tiles = []
    for tile in range(halo_tiles):
        at = tile * LANES
        if tile + 1 < halo_tiles:
            moved = jnp.where(shifted < LANES, near[tile], near[tile + 1])
            sent = rounded(picked[0:rows, at : at + LANES] + moved)
        else:
            moved = near[tile]
            sent = rounded(picked[0:rows, at : at + LANES] + moved)
            edge = pltpu.roll(picked[rows:, 0:LANES], LANES - 1, axis=1)
            sent = jnp.where(lane_rows == LANES - 1, edge, sent)
        halo_out[:, at : at + LANES] = sent.astype(jnp.bfloat16)

    pl.semaphore_wait(barrier, owners - 1)
    back = pltpu.make_async_remote_copy(
        src_ref=halo_out,
        dst_ref=halo_in,
        send_sem=halo_sem.at[0],
        recv_sem=halo_sem.at[1],
        device_id={"sub": lax.rem(me + owners - 1, owners)},
        device_id_type=MESH,
    )

    @pl.when(me > 0)
    def _():
        back.start()

    level_one(rows, window)
    count = -(-window // LANES)
    near = [summed(tile, False) for tile in range(count)]
    previous = None
    for tile in range(count):
        at = tile * LANES
        if tile + 1 < count:
            moved = jnp.where(shifted < LANES, near[tile], near[tile + 1])
        else:
            inside = shifted < window - at
            moved = jnp.where(inside, near[tile], 0.0)
        done = rounded(picked[0:rows, at : at + LANES] + moved)
        done = pltpu.roll(done, pad, axis=1)
        if tile == 0:
            tables[0, :, 0:LANES] = done
        else:
            tables[0, :, at : at + LANES] = jnp.where(lane_rows < pad, previous, done)
        previous = done

    sublane = lax.broadcasted_iota(jnp.int32, (rows, LANES), 0)
    for level_num in range(2, levels + 1):
        span_rows = 2 ** (level_num - 1)
        child_rows = widest_shift(level_num)
        column = 3 * (level_num - 1)
        starts = 2 * child_rows * (sublane >> (level_num - 1))
        lower = jnp.broadcast_to(turned[:, column : column + 1], (rows, LANES)).astype(jnp.int32)
        upper = jnp.broadcast_to(turned[:, column + 1 : column + 2], (rows, LANES))
        amount = jnp.broadcast_to(turned[:, column + 2 : column + 3], (rows, LANES))
        lower_at[level_num - 2] = (starts + lower) & (GROUP - 1)
        upper_at[level_num - 2] = (starts + child_rows + upper.astype(jnp.int32)) & (GROUP - 1)
        lane_at[level_num - 1] = lane_rows + amount.astype(jnp.int32)

    def merge(level_num, begin, end, given, keep):
        span_rows = 2 ** (level_num - 1)
        pairs = 2 * GROUP

        def one(row, low, high):
            at_low = lower_at[level_num - 2, pl.ds(row, GROUP), :]
            at_high = upper_at[level_num - 2, pl.ds(row, GROUP), :]
            reach = lane_at[level_num - 1, pl.ds(row, GROUP), :]
            inside = reach < LANES
            within = reach & (LANES - 1)
            sources = min(end + 1, given) - begin
            moved = []
            for tile in range(begin, begin + sources):
                at = tile * LANES
                value = tables[level_num - 2, pl.ds(high, GROUP), at : at + LANES]
                value = jnp.take_along_axis(value, at_high, axis=0)
                moved.append(jnp.take_along_axis(value, within, axis=1))
            results = []
            for tile in range(begin, end):
                at = tile * LANES
                value = tables[level_num - 2, pl.ds(low, GROUP), at : at + LANES]
                value = jnp.take_along_axis(value, at_low, axis=0)
                here = moved[tile - begin]
                after = moved[min(tile - begin + 1, sources - 1)]
                results.append(value + jnp.where(inside, here, after))
            return results

        def step(index, carry):
            row = pl.multiple_of(index * pairs, pairs)
            if span_rows < pairs:
                places = [(row, row), (row + GROUP, row + GROUP)]
            else:
                wide = span_rows // pairs
                low = (index // wide) * span_rows + (index % wide) * GROUP
                high = low + span_rows // 2
                low = pl.multiple_of(low, GROUP)
                high = pl.multiple_of(high, GROUP)
                places = [(low, high), (low, high)]
            results = [
                one(pl.multiple_of(row + part * GROUP, GROUP), low, high)
                for part, (low, high) in enumerate(places)
            ]
            for tile in range(begin, end):
                keep(row, tile, results[0][tile - begin], results[1][tile - begin])
            return carry

        lax.fori_loop(0, rows // pairs, step, 0, unroll=2)

    def to_table(level_num):
        def keep(row, tile, upper_half, lower_half):
            at = tile * LANES
            tables[level_num - 1, pl.ds(row, GROUP), at : at + LANES] = rounded(upper_half)
            tables[level_num - 1, pl.ds(row + GROUP, GROUP), at : at + LANES] = rounded(lower_half)

        return keep

    def to_output(target, first_tile):
        def keep(row, tile, upper_half, lower_half):
            at = (tile - first_tile) * LANES
            block = jnp.concatenate([upper_half, lower_half], axis=0)
            target[pl.ds(row, 2 * GROUP), at : at + LANES] = block.astype(jnp.bfloat16)

        return keep

    edge = early_tiles * LANES
    given = own_tiles
    for level_num in range(2, levels + 1):
        need = -(-(edge + still_to_come(level_num, levels)) // LANES)
        last = level_num == levels
        merge(
            level_num, 0, need, given, to_output(early_out, 0) if last else to_table(level_num)
        )
        given = need

    def spread(source, target, send_sem, recv_sem, some):
        copies = []
        for apart in range(1, owners):
            to = lax.rem(me + apart, owners)
            base = pl.multiple_of(reversed_index(to, bits) * held, held)
            copy = pltpu.make_async_remote_copy(
                src_ref=source.at[pl.ds(base, held)],
                dst_ref=target.at[me],
                send_sem=send_sem.at[apart],
                recv_sem=recv_sem.at[apart],
                device_id={"sub": to},
                device_id_type=MESH,
            )
            copies.append((copy, apart))

            if some:

                @pl.when(me < owners - 1)
                def _():
                    copy.start()

            else:
                copy.start()
        base = pl.multiple_of(reversed_index(me, bits) * held, held)
        target[me] = source[pl.ds(base, held), :]
        return copies

    early = spread(early_out, early_in, early_send, early_recv, False)

    @pl.when(me < owners - 1)
    def _():
        back.wait_recv()

    @pl.when(me > 0)
    def _():
        back.wait_send()

    for tile in range(halo_tiles):
        at = (own_tiles + tile) * LANES
        tables[0, :, at : at + LANES] = halo_in[:, tile * LANES : (tile + 1) * LANES].astype(
            jnp.float32
        )
    at = (own_tiles - 1) * LANES
    extra = jnp.where(
        lane_at[0] >= LANES, halo_in[:, (halo_tiles - 1) * LANES :].astype(jnp.float32), 0.0
    )
    tables[0, :, at : at + LANES] = rounded(tables[0, :, at : at + LANES] + extra)
    given = all_tiles
    for level_num in range(2, levels + 1):
        coming = still_to_come(level_num, levels)
        begin = (edge + coming) // LANES
        end = -(-(own_tiles * LANES + coming) // LANES)
        last = level_num == levels
        merge(
            level_num,
            begin,
            end,
            given,
            to_output(late_out, early_tiles) if last else to_table(level_num),
        )
        given = end
    late = spread(late_out, late_in, late_send, late_recv, True)

    for load in loads[3:]:
        load.wait()
    for copy, apart in early:
        copy.wait()
    for copy, apart in late:

        @pl.when(me < owners - 1)
        def _():
            copy.wait_send()

        @pl.when(lax.rem(me + owners - apart, owners) < owners - 1)
        def _():
            copy.wait_recv()

    wide_lane = lax.broadcasted_iota(jnp.int32, (held, LANES), 1)
    pieces = [[] for _ in range(fold_size)]
    for source in range(owners):
        offset = window * source - pad
        whole, part = offset // LANES, offset % LANES
        for tile in range(own_tiles):
            spots = []
            from_lane = pad if tile == 0 else 0
            spots.append((whole + tile, max(part, from_lane + part), LANES))
            spots.append((whole + tile + 1, max(0, from_lane + part - LANES), part))
            for fold, begin, end in spots:
                if 0 <= fold < fold_size and begin < end:
                    pieces[fold].append((begin, source, tile, part))
    rolled = {}

    def rolled_tile(source, tile, part):
        if (source, tile) not in rolled:
            if tile < early_tiles:
                value = early_in[source, :, tile * LANES : (tile + 1) * LANES]
            else:
                at = (tile - early_tiles) * LANES
                value = late_in[source, :, at : at + LANES]
            value = value.astype(jnp.float32)
            if part:
                value = pltpu.roll(value, part, axis=1)
            rolled[source, tile] = value
        return rolled[source, tile]

    for fold in range(fold_size):
        value = None
        for begin, source, tile, part in sorted(pieces[fold]):
            piece = rolled_tile(source, tile, part)
            value = piece if value is None else jnp.where(wide_lane < begin, value, piece)
        folded[fold * held : (fold + 1) * held, :] = value

    cosine, sine = twist_ref[0], twist_ref[1]
    for series in range(0, held, 2):
        pair = jnp.concatenate(
            [folded[pl.ds(series + side, fold_size, stride=held), :] for side in range(2)], axis=1
        )
        spun = jnp.dot(
            first_ref[...], pair.astype(jnp.bfloat16), preferred_element_type=jnp.float32
        )
        for side in range(2):
            real = spun[0:fold_size, side * LANES : (side + 1) * LANES]
            imag = spun[fold_size:, side * LANES : (side + 1) * LANES]
            at = (series + side) * fold_size
            twisted[at : at + fold_size, 0:LANES] = (real * cosine + imag * sine).astype(
                jnp.bfloat16
            )
            twisted[at : at + fold_size, LANES:] = (imag * cosine - real * sine).astype(
                jnp.bfloat16
            )
    half = fold_size
    scale = 1.0 / (length * channels)
    small_lane = lax.broadcasted_iota(jnp.int32, (half // 2, LANES), 1)
    for series in range(0, held, 4):
        at = series * fold_size
        waves = lax.dot_general(
            third_ref[...],
            twisted[at : at + 4 * fold_size, :],
            (((1,), (1,)), ((), ())),
            preferred_element_type=jnp.float32,
        )
        power = (waves[0:half] * waves[0:half] + waves[half:] * waves[half:]) * scale
        for side in range(2):
            even = power[0 : half // 2, side * LANES : (side + 1) * LANES]
            odd = power[half // 2 :, side * LANES : (side + 1) * LANES]
            left = jnp.where(small_lane < fold_size, even, pltpu.roll(odd, fold_size, axis=1))
            right = jnp.where(small_lane < fold_size, pltpu.roll(even, fold_size, axis=1), odd)
            spot = (series + 2 * side) * (half // 2)
            powers[spot : spot + half // 2, :] = left
            powers[spot + half // 2 : spot + half, :] = right
    for block in range(0, held, GROUP):
        for tile in range(half // 2):
            out_ref[block : block + GROUP, tile * LANES : (tile + 1) * LANES] = powers[
                pl.ds(block * (half // 2) + tile, GROUP, stride=half // 2), :
            ]


def local_sliced(samples, channel_order, merge_table):
    owners = lax.axis_size("sub")
    window, channels = samples.shape
    levels, _, rows = merge_table.shape
    held = rows // owners
    length = owners * (window - held)
    fold_size = length // LANES
    pad = -window % LANES
    own_tiles = (window + pad) // LANES
    halo_tiles = rows // LANES
    early_tiles = own_tiles - halo_tiles
    order = channel_order.reshape(1, channels)
    first_table, twist, third_table = transform_tables(fold_size, length)
    return pl.pallas_call(
        functools.partial(merge_kernel, owners, length),
        out_shape=jax.ShapeDtypeStruct((held, 64 * fold_size), jnp.float32),
        in_specs=[pl.BlockSpec(memory_space=pl.ANY)] * 6,
        out_specs=pl.BlockSpec(memory_space=pltpu.VMEM),
        scratch_shapes=[
            pltpu.VMEM((1, channels), jnp.int32),
            pltpu.VMEM((levels, 3, rows), jnp.int32),
            pltpu.VMEM((window, channels), jnp.bfloat16),
            pltpu.VMEM(first_table.shape, jnp.bfloat16),
            pltpu.VMEM(twist.shape, jnp.float32),
            pltpu.VMEM(third_table.shape, jnp.bfloat16),
            pltpu.VMEM((channels, LANES), jnp.float32),
            pltpu.VMEM((-(-3 * levels // 8) * 8, rows), jnp.float32),
            pltpu.VMEM((channels, channels), jnp.bfloat16),
            pltpu.VMEM((levels - 1, rows, LANES), jnp.int32),
            pltpu.VMEM((levels - 1, rows, LANES), jnp.int32),
            pltpu.VMEM((levels, rows, LANES), jnp.int32),
            pltpu.VMEM((channels, own_tiles * LANES), jnp.float32),
            pltpu.VMEM((levels - 1, rows, (own_tiles + halo_tiles) * LANES), jnp.float32),
            pltpu.VMEM((rows, rows), jnp.bfloat16),
            pltpu.VMEM((rows, rows), jnp.bfloat16),
            pltpu.VMEM((rows, early_tiles * LANES), jnp.bfloat16),
            pltpu.VMEM((rows, rows), jnp.bfloat16),
            pltpu.VMEM((owners, held, early_tiles * LANES), jnp.bfloat16),
            pltpu.VMEM((owners, held, rows), jnp.bfloat16),
            pltpu.VMEM((held * fold_size, LANES), jnp.float32),
            pltpu.VMEM((held * fold_size, 2 * LANES), jnp.bfloat16),
            pltpu.VMEM((held * fold_size // 2, LANES), jnp.float32),
            pltpu.SemaphoreType.DMA((2,)),
            pltpu.SemaphoreType.DMA((owners,)),
            pltpu.SemaphoreType.DMA((owners,)),
            pltpu.SemaphoreType.DMA((owners,)),
            pltpu.SemaphoreType.DMA((owners,)),
            pltpu.SemaphoreType.DMA((6,)),
        ],
        compiler_params=pltpu.CompilerParams(
            vmem_limit_bytes=48 * 1024 * 1024, collective_id=0, has_side_effects=True
        ),
        name="merge_rows",
    )(order, merge_table, samples, first_table, twist, third_table)


def is_sliced(window, channels, owners, rows, levels):
    held = rows // owners
    length = owners * (window - held)
    return (
        held == 16
        and window % 16 == 0
        and rows % LANES == 0
        and channels == 2 * rows
        and rows == 2 ** (levels - 1)
        and length == 64 * LANES
        and window > 2 * rows
    )


def local_any(samples, channel_order, merge_table):
    window, channels = samples.shape
    levels, _, rows = merge_table.shape
    if is_sliced(window, channels, lax.axis_size("sub"), rows, levels):
        return local_sliced(samples, channel_order, merge_table)
    return local(samples, channel_order, merge_table)


def solution(mesh):
    in_specs = (P(("groups", "sub"), None), P(), P())
    out_specs = P(("groups", "sub"), None)
    return jax.shard_map(local_any, mesh=mesh, in_specs=in_specs, out_specs=out_specs, check_vma=False)
```

```python
import functools
import math

import jax
import jax.numpy as jnp
import numpy as np
from jax import lax
from jax.experimental import pallas as pl
from jax.experimental.pallas import tpu as pltpu
from jax.sharding import PartitionSpec as P

LOCAL = 5
MESH = pl.DeviceIdType.MESH
CH_DEV = 32
SAMPLES = 8192


def from_partner(block, axis, apart):
    count = lax.axis_size(axis)
    route = []
    for low in range(count):
        high = low | 1 << apart
        if high != low and high < count:
            route += [(low, high), (high, low)]
    return lax.ppermute(block, axis, route)


def delay_rows(values, shifts, margin, time_axis):
    length = values.shape[time_axis]
    moved = values
    for bit_num in range(max(1, margin.bit_length())):
        offset = 2**bit_num
        rolled = jnp.pad(moved[:, offset:], ((0, 0), (0, offset)))
        flagged = shifts >> bit_num & 1 == 1
        flagged = flagged[:, None]
        moved = jnp.where(flagged, rolled, moved)
    return moved


def merge_level(current, entries, child_rows, span_rows, time_axis):
    outputs = jnp.arange(entries.shape[1], dtype=jnp.int32)
    starts = 2 * child_rows * (outputs // span_rows)
    lower_rows = jnp.take(current, starts + entries[0], axis=1 - time_axis)
    upper_rows = jnp.take(current, starts + child_rows + entries[1], axis=1 - time_axis)
    moved_rows = delay_rows(upper_rows, entries[2], child_rows, time_axis)
    return (lower_rows.astype(jnp.float32) + moved_rows.astype(jnp.float32)).astype(jnp.bfloat16)


def spectrum(delays, channels):
    row_count = delays.shape[0]
    length = delays.shape[1]
    fold_size = length // 128
    first_index = jnp.arange(fold_size, dtype=jnp.int32)
    lane_index = jnp.arange(128, dtype=jnp.int32)
    half_index = jnp.arange(64, dtype=jnp.int32)
    angle_one = (
        2.0
        * math.pi
        / fold_size
        * (first_index[:, None] * first_index[None, :] % fold_size).astype(jnp.float32)
    )
    cos_one = jnp.cos(angle_one).astype(jnp.bfloat16)
    sin_one = jnp.sin(angle_one).astype(jnp.bfloat16)
    angle_two = (
        2.0
        * math.pi
        / length
        * (first_index[:, None] * lane_index[None, :] % length).astype(jnp.float32)
    )
    twist_cos = jnp.cos(angle_two)
    twist_sin = jnp.sin(angle_two)
    angle_three = (
        2.0 * math.pi / 128 * (lane_index[:, None] * half_index[None, :] % 128).astype(jnp.float32)
    )
    cos_three = jnp.cos(angle_three).astype(jnp.bfloat16)
    sin_three = jnp.sin(angle_three).astype(jnp.bfloat16)
    series = delays.reshape(row_count, fold_size, 128)
    first_re = jnp.einsum("kn,rnm->rkm", cos_one, series, preferred_element_type=jnp.float32)
    first_im = -jnp.einsum("kn,rnm->rkm", sin_one, series, preferred_element_type=jnp.float32)
    twisted_re = (first_re * twist_cos + first_im * twist_sin).astype(jnp.bfloat16)
    twisted_im = (first_im * twist_cos - first_re * twist_sin).astype(jnp.bfloat16)
    out_re = jnp.einsum(
        "rkn,nj->rjk", twisted_re, cos_three, preferred_element_type=jnp.float32
    ) + jnp.einsum("rkn,nj->rjk", twisted_im, sin_three, preferred_element_type=jnp.float32)
    out_im = jnp.einsum(
        "rkn,nj->rjk", twisted_im, cos_three, preferred_element_type=jnp.float32
    ) - jnp.einsum("rkn,nj->rjk", twisted_re, sin_three, preferred_element_type=jnp.float32)
    power = (out_re * out_re + out_im * out_im) / (length * channels)
    return power.reshape(row_count, 64 * fold_size)


def local(samples, channel_order, merge_table):
    owners = lax.axis_size("sub")
    owner_index = lax.axis_index("sub")
    owned_rows = CH_DEV // 2
    quarter = CH_DEV // 4
    window = samples.shape[0]
    channels = samples.shape[1]
    ordered = jnp.take(samples, channel_order, axis=1).T.reshape(owners, CH_DEV, window)
    current = lax.all_to_all(ordered, "sub", split_axis=0, concat_axis=2, tiled=True).reshape(
        CH_DEV, window * owners
    )
    for level_num in range(1, LOCAL + 1):
        entries = lax.dynamic_slice_in_dim(
            merge_table[level_num - 1], owner_index * owned_rows, owned_rows, 1
        )
        current = merge_level(
            current, entries, max(1, 2 ** (level_num - 2)), 2 ** (level_num - 1), 1
        )
    block_index = jnp.zeros((), jnp.int32)
    for bit_num in range(owners.bit_length() - 1):
        level_num = LOCAL + bit_num + 1
        half_bit = owner_index >> bit_num & 1
        block_index = block_index * 2 + half_bit
        span_rows = owned_rows * 2 ** (bit_num + 1)
        child_rows = span_rows // 2
        subband = owner_index >> bit_num + 1
        entries = lax.dynamic_slice_in_dim(
            merge_table[level_num - 1],
            subband * span_rows + owned_rows * block_index,
            owned_rows,
            1,
        )
        kept_rows = lax.dynamic_slice_in_dim(current, half_bit * quarter, quarter, 0)
        sent_rows = lax.dynamic_slice_in_dim(current, (1 - half_bit) * quarter, quarter, 0)
        partner = from_partner(sent_rows, "sub", bit_num)
        row_base = quarter * block_index
        is_low = half_bit == 0
        lower_part = jnp.where(is_low, kept_rows, partner)
        upper_part = jnp.where(is_low, partner, kept_rows)
        lower_rows = jnp.take(lower_part, entries[0] - row_base, axis=0)
        upper_rows = jnp.take(upper_part, entries[1] - row_base, axis=0)
        moved_rows = delay_rows(upper_rows, entries[2], child_rows, 1)
        current = (lower_rows.astype(jnp.float32) + moved_rows.astype(jnp.float32)).astype(
            jnp.bfloat16
        )
    return spectrum(current[:, :SAMPLES], channels)


LANES = 128
GROUP = 8


def widest_shift(level_num):
    return max(1, 2 ** (level_num - 2))


def still_to_come(level_num, levels):
    return sum(widest_shift(later) for later in range(level_num + 1, levels + 1))


def gathered(values, places, axis):
    other = 1 - axis
    numbers = lax.GatherDimensionNumbers(
        offset_dims=(),
        collapsed_slice_dims=(axis,),
        start_index_map=(axis,),
        operand_batching_dims=(other,),
        start_indices_batching_dims=(other,),
    )
    return lax.gather(
        values,
        places[..., None],
        numbers,
        slice_sizes=(1, 1),
        mode=lax.GatherScatterMode.PROMISE_IN_BOUNDS,
    )


def transform_tables(fold_size, length):
    first_index = np.arange(fold_size)
    lane_index = np.arange(LANES)
    half_index = np.concatenate([np.arange(0, 64, 2), np.arange(1, 64, 2)])
    unit = np.float32(2.0 * math.pi)

    def angles(left, right, period):
        turns = (left[:, None] * right[None, :]) % period
        return (unit / np.float32(period)) * turns.astype(np.float32)

    one = angles(first_index, first_index, fold_size)
    first_table = np.concatenate([np.cos(one), -np.sin(one)], axis=0)
    two = angles(first_index, lane_index, length)
    twist = np.stack([np.cos(two), np.sin(two)])
    three = angles(half_index, lane_index, LANES)
    cos_three, sin_three = np.cos(three), np.sin(three)
    third_table = np.concatenate(
        [
            np.concatenate([cos_three, sin_three], axis=1),
            np.concatenate([-sin_three, cos_three], axis=1),
        ],
        axis=0,
    )
    return (
        jnp.asarray(first_table, jnp.bfloat16),
        jnp.asarray(twist, jnp.float32),
        jnp.asarray(third_table, jnp.bfloat16),
    )


def one_hot(row_index, depth):
    rows = lax.broadcasted_iota(jnp.int32, (depth, row_index.shape[1]), 0)
    return (rows == row_index).astype(jnp.float32).astype(jnp.bfloat16)


def floor_16(count):
    return count // 16 * 16


def ceil_16(count):
    return -(-count // 16) * 16


def merge_kernel(
    owners,
    length,
    order_hbm,
    table_hbm,
    own_hbm,
    first_hbm,
    twist_hbm,
    third_hbm,
    out_ref,
    order_ref,
    table_ref,
    own_ref,
    first_ref,
    twist_ref,
    third_ref,
    split,
    choose,
    choices,
    picked,
    tables,
    halo_out,
    placed,
    early_out,
    late_out,
    early_in,
    late_in,
    folded,
    twisted,
    powers,
    halo_sem,
    early_send,
    early_recv,
    late_send,
    late_recv,
    load_sem,
):
    levels, _, rows = table_ref.shape
    window, channels = own_ref.shape
    held = rows // owners
    fold_size = length // LANES
    me = lax.axis_index("sub")
    bits = owners.bit_length() - 1

    loads = [
        pltpu.make_async_copy(source, target, load_sem.at[place])
        for place, (source, target) in enumerate(
            [
                (order_hbm, order_ref),
                (table_hbm, table_ref),
                (own_hbm, own_ref),
                (first_hbm, first_ref),
                (twist_hbm, twist_ref),
                (third_hbm, third_ref),
            ]
        )
    ]
    for load in loads:
        load.start()
    barrier = pltpu.get_barrier_semaphore()
    for apart in range(1, owners):
        pl.semaphore_signal(
            barrier, inc=1, device_id={"sub": lax.rem(me + apart, owners)}, device_id_type=MESH
        )

    column = lax.broadcasted_iota(jnp.int32, (1, channels), 1)
    split[...] = one_hot(
        jnp.where(column < rows, 2 * column, 2 * (column - rows) + 1), channels
    )
    loads[0].wait()
    order = jnp.broadcast_to(order_ref[...], (16, channels))
    side = lax.broadcasted_iota(jnp.int32, (16, channels), 0)
    digits = jnp.where(side == 0, order >> 6, order & 63).astype(jnp.float32)
    digits = jnp.dot(
        digits.astype(jnp.bfloat16), split[...], preferred_element_type=jnp.float32
    ).astype(jnp.int32)
    choose[...] = one_hot(digits[0:1] * 64 + digits[1:2], channels)

    lane = lax.broadcasted_iota(jnp.int32, (1, LANES), 1)
    sublane = lax.broadcasted_iota(jnp.int32, (GROUP, LANES), 0)

    def combine(level_num, begin, end, given):
        span_rows = 2 ** (level_num - 1)
        columns = []
        for base in range(0, rows, LANES):
            place = (lane + base) % span_rows // 16
            static = base % span_rows // 16
            amount = table_ref[level_num - 1][2:3, base : base + LANES]
            reach = sublane + (amount - GROUP * place)
            inside = reach < GROUP
            turn = reach & (GROUP - 1)
            steps = max(0, min(span_rows, LANES).bit_length() - 5)
            top = end + GROUP + GROUP * (static + 2**steps - 1)
            bottom = begin + GROUP * static
            upper = picked[level_num - 1][bottom : min(top, given), rows + base : rows + base + LANES]
            if top > given:
                filler = jnp.zeros((top - given, LANES), jnp.float32)
                upper = jnp.concatenate([upper, filler], axis=0)
            for step in range(steps):
                offset = GROUP * 2**step
                flagged = (place - static) >> step & 1 == 1
                size = upper.shape[0]
                flagged = jnp.broadcast_to(flagged, (size - offset, LANES))
                upper = jnp.where(flagged, upper[offset:], upper[: size - offset])
            count = (end - begin) // GROUP
            spun = [
                gathered(upper[GROUP * part : GROUP * (part + 1)], turn, 0)
                for part in range(count + 1)
            ]
            moved = [jnp.where(inside, spun[part], spun[part + 1]) for part in range(count)]
            lower = picked[level_num - 1][begin:end, base : base + LANES]
            columns.append(lower + jnp.concatenate(moved, axis=0))
        return jnp.concatenate(columns, axis=1)

    loads[1].wait()
    loads[2].wait()
    ahead = ceil_16(rows + GROUP)
    picked[0][0:ahead, :] = jnp.dot(
        own_ref[0:ahead, :], choose[...], preferred_element_type=jnp.float32
    )
    near = combine(1, 0, rows, ahead)
    tables[0][0:rows, :] = near.astype(jnp.bfloat16)
    halo_out[0 : rows - 16, :] = near[0 : rows - 16].astype(jnp.bfloat16)
    edge = jnp.broadcast_to(picked[0][0:1, rows:], (16, rows))
    last_row = lax.broadcasted_iota(jnp.int32, (16, rows), 0) == 15
    halo_out[rows - 16 :, :] = jnp.where(last_row, edge, near[rows - 16 :]).astype(jnp.bfloat16)

    pl.semaphore_wait(barrier, owners - 1)
    back = pltpu.make_async_remote_copy(
        src_ref=halo_out,
        dst_ref=tables[0].at[window : window + rows],
        send_sem=halo_sem.at[0],
        recv_sem=halo_sem.at[1],
        device_id={"sub": lax.rem(me + owners - 1, owners)},
        device_id_type=MESH,
    )

    @pl.when(me > 0)
    def _():
        back.start()

    picked[0][ahead:window, :] = jnp.dot(
        own_ref[ahead:window, :], choose[...], preferred_element_type=jnp.float32
    )
    tables[0][rows:window, :] = combine(1, rows, window, window).astype(jnp.bfloat16)

    lanes = lax.broadcasted_iota(jnp.int32, (1, rows), 1)

    def prepare(level_num):
        child_rows = widest_shift(level_num)
        entries = table_ref[level_num - 1]
        starts = 2 * child_rows * (lanes >> (level_num - 1))
        choices[level_num - 2, :, 0:rows] = one_hot(starts + entries[0:1], rows)
        choices[level_num - 2, :, rows:] = one_hot(starts + child_rows + entries[1:2], rows)

    def advance(level_num, source_begin, source_end, begin, end):
        picked[level_num - 1][source_begin:source_end, :] = jnp.dot(
            tables[level_num - 2][source_begin:source_end, :],
            choices[level_num - 2],
            preferred_element_type=jnp.float32,
        )
        tables[level_num - 1][begin:end, :] = combine(
            level_num, begin, end, source_end
        ).astype(jnp.bfloat16)

    valid = window - 1
    ready = window
    starts_late = [floor_16(valid)]
    for level_num in range(2, levels + 1):
        prepare(level_num)
        valid -= widest_shift(level_num)
        end = ceil_16(valid)
        advance(level_num, 0, ready, 0, end)
        ready = end
        starts_late.append(floor_16(valid))
    early = ready

    spots = lax.broadcasted_iota(jnp.int32, (rows, rows), 0)
    shift = held.bit_length() - 1
    wanted = jnp.zeros_like(spots)
    for bit_num in range(bits):
        wanted = wanted | ((spots >> (shift + bit_num) & 1) << (bits - 1 - bit_num))
    wanted = (wanted << shift) + (spots & (held - 1))
    placed[...] = (
        (lax.broadcasted_iota(jnp.int32, (rows, rows), 1) == wanted)
        .astype(jnp.float32)
        .astype(jnp.bfloat16)
    )

    def turn_over(begin, end):
        return lax.dot_general(
            placed[...],
            tables[levels - 1][begin:end, :],
            (((1,), (1,)), ((), ())),
            preferred_element_type=jnp.float32,
        ).astype(jnp.bfloat16)

    def spread(source, target, send_sem, recv_sem, some):
        copies = []
        for apart in range(1, owners):
            to = lax.rem(me + apart, owners)
            copy = pltpu.make_async_remote_copy(
                src_ref=source.at[pl.ds(pl.multiple_of(to * held, held), held)],
                dst_ref=target.at[me],
                send_sem=send_sem.at[apart],
                recv_sem=recv_sem.at[apart],
                device_id={"sub": to},
                device_id_type=MESH,
            )
            copies.append((copy, apart))

            if some:

                @pl.when(me < owners - 1)
                def _():
                    copy.start()

            else:
                copy.start()
        target[me] = source[pl.ds(pl.multiple_of(me * held, held), held), :]
        return copies

    early_out[:, 0:early] = turn_over(0, early)
    early_copies = spread(early_out, early_in, early_send, early_recv, False)

    @pl.when(me < owners - 1)
    def _():
        back.wait_recv()

    @pl.when(me > 0)
    def _():
        back.wait_send()

    fill = tables[0][window - 16 : window, :].astype(jnp.float32)
    edge = tables[0][window + rows - 16 : window + rows, :].astype(jnp.float32)[15:16]
    amount = jnp.broadcast_to(table_ref[0][2:3, :], (16, rows))
    fill = fill + jnp.where(last_row & (amount > 0), jnp.broadcast_to(edge, (16, rows)), 0.0)
    tables[0][window - 16 : window, :] = fill.astype(jnp.bfloat16)
    ready = window + rows
    for level_num in range(2, levels + 1):
        end = ceil_16(window + still_to_come(level_num, levels))
        advance(
            level_num, starts_late[level_num - 2], ready, starts_late[level_num - 1], end
        )
        ready = end
    late_out[...] = turn_over(early, window)
    late_copies = spread(late_out, late_in, late_send, late_recv, True)

    for load in loads[3:]:
        load.wait()
    for copy, apart in early_copies:
        copy.wait()
    for copy, apart in late_copies:

        @pl.when(me < owners - 1)
        def _():
            copy.wait_send()

        @pl.when(lax.rem(me + owners - apart, owners) < owners - 1)
        def _():
            copy.wait_recv()

    wide_lane = lax.broadcasted_iota(jnp.int32, (held, LANES), 1)
    pieces = [[] for _ in range(fold_size)]
    for source in range(owners):
        for late, begin, end in ((False, 0, early), (True, early, window)):
            for at in range(begin, end, LANES):
                fold, part = divmod(window * source + at, LANES)
                count = min(LANES, end - at)
                for where, low, high in (
                    (fold, part, min(LANES, part + count)),
                    (fold + 1, 0, part + count - LANES),
                ):
                    if where < fold_size and low < high:
                        pieces[where].append((low, source, late, at - begin, part))
    rolled = {}

    def rolled_tile(source, late, at, part):
        if (source, late, at) not in rolled:
            value = (late_in if late else early_in)[source, :, at : at + LANES]
            value = value.astype(jnp.float32)
            if part:
                value = pltpu.roll(value, part, axis=1)
            rolled[source, late, at] = value
        return rolled[source, late, at]

    for fold in range(fold_size):
        value = None
        for low, source, late, at, part in sorted(pieces[fold]):
            piece = rolled_tile(source, late, at, part)
            value = piece if value is None else jnp.where(wide_lane < low, value, piece)
        folded[fold * held : (fold + 1) * held, :] = value

    cosine, sine = twist_ref[0], twist_ref[1]
    for series in range(0, held, 2):
        pair = jnp.concatenate(
            [folded[pl.ds(series + side, fold_size, stride=held), :] for side in range(2)], axis=1
        )
        spun = jnp.dot(
            first_ref[...], pair.astype(jnp.bfloat16), preferred_element_type=jnp.float32
        )
        for side in range(2):
            real = spun[0:fold_size, side * LANES : (side + 1) * LANES]
            imag = spun[fold_size:, side * LANES : (side + 1) * LANES]
            at = (series + side) * fold_size
            twisted[at : at + fold_size, 0:LANES] = (real * cosine + imag * sine).astype(
                jnp.bfloat16
            )
            twisted[at : at + fold_size, LANES:] = (imag * cosine - real * sine).astype(
                jnp.bfloat16
            )
    half = fold_size
    scale = 1.0 / (length * channels)
    small_lane = lax.broadcasted_iota(jnp.int32, (half // 2, LANES), 1)
    for series in range(0, held, 4):
        at = series * fold_size
        waves = lax.dot_general(
            third_ref[...],
            twisted[at : at + 4 * fold_size, :],
            (((1,), (1,)), ((), ())),
            preferred_element_type=jnp.float32,
        )
        power = (waves[0:half] * waves[0:half] + waves[half:] * waves[half:]) * scale
        for side in range(2):
            even = power[0 : half // 2, side * LANES : (side + 1) * LANES]
            odd = power[half // 2 :, side * LANES : (side + 1) * LANES]
            left = jnp.where(small_lane < fold_size, even, pltpu.roll(odd, fold_size, axis=1))
            right = jnp.where(small_lane < fold_size, pltpu.roll(even, fold_size, axis=1), odd)
            spot = (series + 2 * side) * (half // 2)
            powers[spot : spot + half // 2, :] = left
            powers[spot + half // 2 : spot + half, :] = right
    for block in range(0, held, GROUP):
        for tile in range(half // 2):
            out_ref[block : block + GROUP, tile * LANES : (tile + 1) * LANES] = powers[
                pl.ds(block * (half // 2) + tile, GROUP, stride=half // 2), :
            ]


def local_sliced(samples, channel_order, merge_table):
    owners = lax.axis_size("sub")
    window, channels = samples.shape
    levels, _, rows = merge_table.shape
    held = rows // owners
    length = owners * (window - held)
    fold_size = length // LANES
    early = window - rows
    whole = window + rows
    order = channel_order.reshape(1, channels)
    first_table, twist, third_table = transform_tables(fold_size, length)
    return pl.pallas_call(
        functools.partial(merge_kernel, owners, length),
        out_shape=jax.ShapeDtypeStruct((held, 64 * fold_size), jnp.float32),
        in_specs=[pl.BlockSpec(memory_space=pl.ANY)] * 6,
        out_specs=pl.BlockSpec(memory_space=pltpu.VMEM),
        scratch_shapes=[
            pltpu.VMEM((1, channels), jnp.int32),
            pltpu.VMEM((levels, 3, rows), jnp.int32),
            pltpu.VMEM((window, channels), jnp.bfloat16),
            pltpu.VMEM(first_table.shape, jnp.bfloat16),
            pltpu.VMEM(twist.shape, jnp.float32),
            pltpu.VMEM(third_table.shape, jnp.bfloat16),
            pltpu.VMEM((channels, channels), jnp.bfloat16),
            pltpu.VMEM((channels, channels), jnp.bfloat16),
            pltpu.VMEM((levels - 1, rows, 2 * rows), jnp.bfloat16),
            [pltpu.VMEM((whole, 2 * rows), jnp.float32)] * levels,
            [pltpu.VMEM((whole, rows), jnp.bfloat16)] * levels,
            pltpu.VMEM((rows, rows), jnp.bfloat16),
            pltpu.VMEM((rows, rows), jnp.bfloat16),
            pltpu.VMEM((rows, -(-early // LANES) * LANES), jnp.bfloat16),
            pltpu.VMEM((rows, rows), jnp.bfloat16),
            pltpu.VMEM((owners, held, -(-early // LANES) * LANES), jnp.bfloat16),
            pltpu.VMEM((owners, held, rows), jnp.bfloat16),
            pltpu.VMEM((held * fold_size, LANES), jnp.float32),
            pltpu.VMEM((held * fold_size, 2 * LANES), jnp.bfloat16),
            pltpu.VMEM((held * fold_size // 2, LANES), jnp.float32),
            pltpu.SemaphoreType.DMA((2,)),
            pltpu.SemaphoreType.DMA((owners,)),
            pltpu.SemaphoreType.DMA((owners,)),
            pltpu.SemaphoreType.DMA((owners,)),
            pltpu.SemaphoreType.DMA((owners,)),
            pltpu.SemaphoreType.DMA((6,)),
        ],
        compiler_params=pltpu.CompilerParams(
            vmem_limit_bytes=62 * 1024 * 1024, collective_id=0, has_side_effects=True
        ),
        name="merge_rows",
    )(order, merge_table, samples, first_table, twist, third_table)


def is_sliced(window, channels, owners, rows, levels):
    held = rows // owners
    length = owners * (window - held)
    return (
        held == 16
        and window % 16 == 0
        and rows % LANES == 0
        and channels == 2 * rows
        and rows == 2 ** (levels - 1)
        and length == 64 * LANES
        and window > 2 * rows
    )


def local_any(samples, channel_order, merge_table):
    window, channels = samples.shape
    levels, _, rows = merge_table.shape
    if is_sliced(window, channels, lax.axis_size("sub"), rows, levels):
        return local_sliced(samples, channel_order, merge_table)
    return local(samples, channel_order, merge_table)


def solution(mesh):
    in_specs = (P(("groups", "sub"), None), P(), P())
    out_specs = P(("groups", "sub"), None)
    return jax.shard_map(local_any, mesh=mesh, in_specs=in_specs, out_specs=out_specs, check_vma=False)
```

```python
import functools
import math

import jax
import jax.numpy as jnp
import numpy as np
from jax import lax
from jax.experimental import pallas as pl
from jax.experimental.pallas import tpu as pltpu
from jax.sharding import PartitionSpec as P

LOCAL = 5
MESH = pl.DeviceIdType.MESH
CH_DEV = 32
SAMPLES = 8192


def from_partner(block, axis, apart):
    count = lax.axis_size(axis)
    route = []
    for low in range(count):
        high = low | 1 << apart
        if high != low and high < count:
            route += [(low, high), (high, low)]
    return lax.ppermute(block, axis, route)


def delay_rows(values, shifts, margin, time_axis):
    length = values.shape[time_axis]
    moved = values
    for bit_num in range(max(1, margin.bit_length())):
        offset = 2**bit_num
        rolled = jnp.pad(moved[:, offset:], ((0, 0), (0, offset)))
        flagged = shifts >> bit_num & 1 == 1
        flagged = flagged[:, None]
        moved = jnp.where(flagged, rolled, moved)
    return moved


def merge_level(current, entries, child_rows, span_rows, time_axis):
    outputs = jnp.arange(entries.shape[1], dtype=jnp.int32)
    starts = 2 * child_rows * (outputs // span_rows)
    lower_rows = jnp.take(current, starts + entries[0], axis=1 - time_axis)
    upper_rows = jnp.take(current, starts + child_rows + entries[1], axis=1 - time_axis)
    moved_rows = delay_rows(upper_rows, entries[2], child_rows, time_axis)
    return (lower_rows.astype(jnp.float32) + moved_rows.astype(jnp.float32)).astype(jnp.bfloat16)


def spectrum(delays, channels):
    row_count = delays.shape[0]
    length = delays.shape[1]
    fold_size = length // 128
    first_index = jnp.arange(fold_size, dtype=jnp.int32)
    lane_index = jnp.arange(128, dtype=jnp.int32)
    half_index = jnp.arange(64, dtype=jnp.int32)
    angle_one = (
        2.0
        * math.pi
        / fold_size
        * (first_index[:, None] * first_index[None, :] % fold_size).astype(jnp.float32)
    )
    cos_one = jnp.cos(angle_one).astype(jnp.bfloat16)
    sin_one = jnp.sin(angle_one).astype(jnp.bfloat16)
    angle_two = (
        2.0
        * math.pi
        / length
        * (first_index[:, None] * lane_index[None, :] % length).astype(jnp.float32)
    )
    twist_cos = jnp.cos(angle_two)
    twist_sin = jnp.sin(angle_two)
    angle_three = (
        2.0 * math.pi / 128 * (lane_index[:, None] * half_index[None, :] % 128).astype(jnp.float32)
    )
    cos_three = jnp.cos(angle_three).astype(jnp.bfloat16)
    sin_three = jnp.sin(angle_three).astype(jnp.bfloat16)
    series = delays.reshape(row_count, fold_size, 128)
    first_re = jnp.einsum("kn,rnm->rkm", cos_one, series, preferred_element_type=jnp.float32)
    first_im = -jnp.einsum("kn,rnm->rkm", sin_one, series, preferred_element_type=jnp.float32)
    twisted_re = (first_re * twist_cos + first_im * twist_sin).astype(jnp.bfloat16)
    twisted_im = (first_im * twist_cos - first_re * twist_sin).astype(jnp.bfloat16)
    out_re = jnp.einsum(
        "rkn,nj->rjk", twisted_re, cos_three, preferred_element_type=jnp.float32
    ) + jnp.einsum("rkn,nj->rjk", twisted_im, sin_three, preferred_element_type=jnp.float32)
    out_im = jnp.einsum(
        "rkn,nj->rjk", twisted_im, cos_three, preferred_element_type=jnp.float32
    ) - jnp.einsum("rkn,nj->rjk", twisted_re, sin_three, preferred_element_type=jnp.float32)
    power = (out_re * out_re + out_im * out_im) / (length * channels)
    return power.reshape(row_count, 64 * fold_size)


def local(samples, channel_order, merge_table):
    owners = lax.axis_size("sub")
    owner_index = lax.axis_index("sub")
    owned_rows = CH_DEV // 2
    quarter = CH_DEV // 4
    window = samples.shape[0]
    channels = samples.shape[1]
    ordered = jnp.take(samples, channel_order, axis=1).T.reshape(owners, CH_DEV, window)
    current = lax.all_to_all(ordered, "sub", split_axis=0, concat_axis=2, tiled=True).reshape(
        CH_DEV, window * owners
    )
    for level_num in range(1, LOCAL + 1):
        entries = lax.dynamic_slice_in_dim(
            merge_table[level_num - 1], owner_index * owned_rows, owned_rows, 1
        )
        current = merge_level(
            current, entries, max(1, 2 ** (level_num - 2)), 2 ** (level_num - 1), 1
        )
    block_index = jnp.zeros((), jnp.int32)
    for bit_num in range(owners.bit_length() - 1):
        level_num = LOCAL + bit_num + 1
        half_bit = owner_index >> bit_num & 1
        block_index = block_index * 2 + half_bit
        span_rows = owned_rows * 2 ** (bit_num + 1)
        child_rows = span_rows // 2
        subband = owner_index >> bit_num + 1
        entries = lax.dynamic_slice_in_dim(
            merge_table[level_num - 1],
            subband * span_rows + owned_rows * block_index,
            owned_rows,
            1,
        )
        kept_rows = lax.dynamic_slice_in_dim(current, half_bit * quarter, quarter, 0)
        sent_rows = lax.dynamic_slice_in_dim(current, (1 - half_bit) * quarter, quarter, 0)
        partner = from_partner(sent_rows, "sub", bit_num)
        row_base = quarter * block_index
        is_low = half_bit == 0
        lower_part = jnp.where(is_low, kept_rows, partner)
        upper_part = jnp.where(is_low, partner, kept_rows)
        lower_rows = jnp.take(lower_part, entries[0] - row_base, axis=0)
        upper_rows = jnp.take(upper_part, entries[1] - row_base, axis=0)
        moved_rows = delay_rows(upper_rows, entries[2], child_rows, 1)
        current = (lower_rows.astype(jnp.float32) + moved_rows.astype(jnp.float32)).astype(
            jnp.bfloat16
        )
    return spectrum(current[:, :SAMPLES], channels)


LANES = 128
GROUP = 8
FOLD_PITCH = 24
POWER_PITCH = 40


def widest_shift(level_num):
    return max(1, 2 ** (level_num - 2))


def still_to_come(level_num, levels):
    return sum(widest_shift(later) for later in range(level_num + 1, levels + 1))


def gathered(values, places, axis):
    other = 1 - axis
    numbers = lax.GatherDimensionNumbers(
        offset_dims=(),
        collapsed_slice_dims=(axis,),
        start_index_map=(axis,),
        operand_batching_dims=(other,),
        start_indices_batching_dims=(other,),
    )
    return lax.gather(
        values,
        places[..., None],
        numbers,
        slice_sizes=(1, 1),
        mode=lax.GatherScatterMode.PROMISE_IN_BOUNDS,
    )


def transform_tables(fold_size, length):
    first_index = np.arange(fold_size)
    lane_index = np.arange(LANES)
    half_index = np.concatenate([np.arange(0, 64, 2), np.arange(1, 64, 2)])
    unit = np.float32(2.0 * math.pi)

    def angles(left, right, period):
        turns = (left[:, None] * right[None, :]) % period
        return (unit / np.float32(period)) * turns.astype(np.float32)

    one = angles(first_index, first_index, fold_size)
    first_table = np.concatenate([np.cos(one), -np.sin(one)], axis=0)
    two = angles(first_index, lane_index, length)
    twist = np.stack([np.cos(two), np.sin(two)])
    three = angles(half_index, lane_index, LANES)
    cos_three, sin_three = np.cos(three), np.sin(three)
    third_table = np.concatenate(
        [
            np.concatenate([cos_three, sin_three], axis=1),
            np.concatenate([-sin_three, cos_three], axis=1),
        ],
        axis=0,
    )
    return (
        jnp.asarray(first_table, jnp.bfloat16),
        jnp.asarray(twist, jnp.float32),
        jnp.asarray(third_table, jnp.bfloat16),
    )


def one_hot(row_index, depth):
    rows = lax.broadcasted_iota(jnp.int32, (depth, row_index.shape[1]), 0)
    return (rows == row_index).astype(jnp.float32).astype(jnp.bfloat16)


def floor_16(count):
    return count // 16 * 16


def ceil_16(count):
    return -(-count // 16) * 16


def merge_kernel(
    owners,
    length,
    order_hbm,
    table_hbm,
    own_hbm,
    first_hbm,
    twist_hbm,
    third_hbm,
    out_ref,
    order_ref,
    table_ref,
    own_ref,
    first_ref,
    twist_ref,
    third_ref,
    split,
    choose,
    choices,
    picked,
    tables,
    halo_out,
    placed,
    early_out,
    late_out,
    early_in,
    late_in,
    folded,
    twisted,
    powers,
    halo_sem,
    early_send,
    early_recv,
    late_send,
    late_recv,
    load_sem,
):
    levels, _, rows = table_ref.shape
    window, channels = own_ref.shape
    held = rows // owners
    fold_size = length // LANES
    me = lax.axis_index("sub")
    bits = owners.bit_length() - 1

    loads = [
        pltpu.make_async_copy(source, target, load_sem.at[place])
        for place, (source, target) in enumerate(
            [
                (order_hbm, order_ref),
                (table_hbm, table_ref),
                (own_hbm, own_ref),
                (first_hbm, first_ref),
                (twist_hbm, twist_ref),
                (third_hbm, third_ref),
            ]
        )
    ]
    for load in loads:
        load.start()
    barrier = pltpu.get_barrier_semaphore()
    column = lax.broadcasted_iota(jnp.int32, (1, channels), 1)
    paired = jnp.where(column < rows, 2 * column, 2 * (column - rows) + 1)
    stripe = channels // owners
    for apart in range(owners):
        if apart:
            pl.semaphore_signal(
                barrier,
                inc=1,
                device_id={"sub": lax.rem(me + apart, owners)},
                device_id_type=MESH,
            )
        split[apart * stripe : (apart + 1) * stripe, :] = one_hot(paired - apart * stripe, stripe)
    half_rows = rows // 2
    for level_num in range(1, levels):
        end = ceil_16(window + still_to_come(level_num, levels))
        tables[level_num - 1][floor_16(end - half_rows) : end, 0:half_rows] = jnp.zeros(
            (end - floor_16(end - half_rows), half_rows), jnp.bfloat16
        )
    loads[0].wait()
    order = jnp.broadcast_to(order_ref[...], (16, channels))
    side = lax.broadcasted_iota(jnp.int32, (16, channels), 0)
    digits = jnp.where(side == 0, order >> 6, order & 63).astype(jnp.float32)
    digits = jnp.dot(
        digits.astype(jnp.bfloat16), split[...], preferred_element_type=jnp.float32
    ).astype(jnp.int32)
    choose[...] = one_hot(digits[0:1] * 64 + digits[1:2], channels)

    lane = lax.broadcasted_iota(jnp.int32, (1, LANES), 1)
    sublane = lax.broadcasted_iota(jnp.int32, (GROUP, LANES), 0)

    def combine(level_num, begin, ends, given):
        ends = ends if isinstance(ends, list) else [ends] * (rows // LANES)
        span_rows = 2 ** (level_num - 1)
        columns = []
        for base in range(0, rows, LANES):
            end = ends[base // LANES]
            count = (end - begin) // GROUP
            place = (lane + base) % span_rows // 16
            static = base % span_rows // 16
            amount = table_ref[level_num - 1][2:3, base : base + LANES]
            reach = sublane + (amount - GROUP * place)
            inside = reach < GROUP
            turn = reach & (GROUP - 1)
            steps = max(0, min(span_rows, LANES).bit_length() - 5)
            top = end + GROUP + GROUP * (static + 2**steps - 1)
            bottom = begin + GROUP * static
            upper = picked[level_num - 1][bottom : min(top, given), rows + base : rows + base + LANES]
            if top > given:
                filler = jnp.zeros((top - given, LANES), jnp.float32)
                upper = jnp.concatenate([upper, filler], axis=0)
            for step in range(steps):
                offset = GROUP * 2**step
                flagged = (place - static) >> step & 1 == 1
                size = upper.shape[0]
                flagged = jnp.broadcast_to(flagged, (size - offset, LANES))
                upper = jnp.where(flagged, upper[offset:], upper[: size - offset])
            spun = [
                gathered(upper[GROUP * part : GROUP * (part + 1)], turn, 0)
                for part in range(count + 1)
            ]
            moved = [jnp.where(inside, spun[part], spun[part + 1]) for part in range(count)]
            lower = picked[level_num - 1][begin:end, base : base + LANES]
            columns.append(lower + jnp.concatenate(moved, axis=0))
        return columns

    loads[1].wait()
    loads[2].wait()
    ahead = ceil_16(rows + GROUP)
    picked[0][0:ahead, :] = jnp.dot(
        own_ref[0:ahead, :], choose[...], preferred_element_type=jnp.float32
    )
    near = combine(1, 0, rows, ahead)
    last_row = lax.broadcasted_iota(jnp.int32, (16, half_rows), 0) == 15
    for part, values in enumerate(near):
        at = part * half_rows
        tables[0][0:rows, at : at + half_rows] = values.astype(jnp.bfloat16)
        top = (part + 1) * half_rows
        halo_out[0 : top - 16, at : at + half_rows] = values[0 : top - 16].astype(jnp.bfloat16)
        edge = jnp.broadcast_to(picked[0][0:1, rows + at : rows + at + half_rows], (16, half_rows))
        halo_out[top - 16 : top, at : at + half_rows] = jnp.where(
            last_row, edge, values[top - 16 : top]
        ).astype(jnp.bfloat16)

    pl.semaphore_wait(barrier, owners - 1)
    backs = [
        pltpu.make_async_remote_copy(
            src_ref=halo_out.at[0:count, first : first + half_rows],
            dst_ref=tables[0].at[window : window + count, first : first + half_rows],
            send_sem=halo_sem.at[part],
            recv_sem=halo_sem.at[2 + part],
            device_id={"sub": lax.rem(me + owners - 1, owners)},
            device_id_type=MESH,
        )
        for part, (count, first) in enumerate(((rows, half_rows), (half_rows, 0)))
    ]

    @pl.when(me > 0)
    def _():
        for back in backs:
            back.start()

    picked[0][ahead:window, :] = jnp.dot(
        own_ref[ahead:window, :], choose[...], preferred_element_type=jnp.float32
    )
    for part, values in enumerate(combine(1, rows, window, window)):
        at = part * half_rows
        tables[0][rows:window, at : at + half_rows] = values.astype(jnp.bfloat16)

    lanes = lax.broadcasted_iota(jnp.int32, (1, rows), 1)

    def prepare(level_num):
        child_rows = widest_shift(level_num)
        entries = table_ref[level_num - 1]
        starts = 2 * child_rows * (lanes >> (level_num - 1))
        choices[level_num - 2, :, 0:rows] = one_hot(starts + entries[0:1], rows)
        choices[level_num - 2, :, rows:] = one_hot(starts + child_rows + entries[1:2], rows)

    def advance(level_num, source_begin, source_end, begin, ends):
        picked[level_num - 1][source_begin:source_end, :] = jnp.dot(
            tables[level_num - 2][source_begin:source_end, :],
            choices[level_num - 2],
            preferred_element_type=jnp.float32,
        )
        for part, values in enumerate(combine(level_num, begin, ends, source_end)):
            at = part * half_rows
            tables[level_num - 1][begin : begin + values.shape[0], at : at + half_rows] = (
                values.astype(jnp.bfloat16)
            )

    valid = window - 1
    ready = window
    starts_late = [floor_16(valid)]
    for level_num in range(2, levels + 1):
        prepare(level_num)
        valid -= widest_shift(level_num)
        end = ceil_16(valid)
        advance(level_num, 0, ready, 0, end)
        ready = end
        starts_late.append(floor_16(valid))
    early = ready

    spots = lax.broadcasted_iota(jnp.int32, (rows, rows), 0)
    shift = held.bit_length() - 1
    wanted = jnp.zeros_like(spots)
    for bit_num in range(bits):
        wanted = wanted | ((spots >> (shift + bit_num) & 1) << (bits - 1 - bit_num))
    wanted = (wanted << shift) + (spots & (held - 1))
    placed[...] = (
        (lax.broadcasted_iota(jnp.int32, (rows, rows), 1) == wanted)
        .astype(jnp.float32)
        .astype(jnp.bfloat16)
    )

    def turn_over(begin, end):
        return lax.dot_general(
            placed[...],
            tables[levels - 1][begin:end, :],
            (((1,), (1,)), ((), ())),
            preferred_element_type=jnp.float32,
        ).astype(jnp.bfloat16)

    def spread(source, target, send_sem, recv_sem, some):
        copies = []
        for apart in range(1, owners):
            to = lax.rem(me + apart, owners)
            copy = pltpu.make_async_remote_copy(
                src_ref=source.at[pl.ds(pl.multiple_of(to * held, held), held)],
                dst_ref=target.at[me],
                send_sem=send_sem.at[apart],
                recv_sem=recv_sem.at[apart],
                device_id={"sub": to},
                device_id_type=MESH,
            )
            copies.append((copy, apart))

            if some:

                @pl.when(me < owners - 1)
                def _():
                    copy.start()

            else:
                copy.start()
        target[me] = source[pl.ds(pl.multiple_of(me * held, held), held), :]
        return copies

    early_out[:, 0:early] = turn_over(0, early)
    early_copies = spread(early_out, early_in, early_send, early_recv, False)

    @pl.when(me < owners - 1)
    def _():
        for back in backs:
            back.wait_recv()

    @pl.when(me > 0)
    def _():
        for back in backs:
            back.wait_send()

    for part in range(2):
        at = part * half_rows
        top = window + (part + 1) * half_rows
        fill = tables[0][window - 16 : window, at : at + half_rows].astype(jnp.float32)
        edge = tables[0][top - 16 : top, at : at + half_rows].astype(jnp.float32)[15:16]
        amount = table_ref[0][2:3, at : at + half_rows]
        late_edge = last_row & jnp.broadcast_to(amount > 0, (16, half_rows))
        fill = fill + jnp.where(late_edge, jnp.broadcast_to(edge, (16, half_rows)), 0.0)
        tables[0][window - 16 : window, at : at + half_rows] = fill.astype(jnp.bfloat16)
    ready = window + rows
    for level_num in range(2, levels + 1):
        end = ceil_16(window + still_to_come(level_num, levels))
        ends = [end if level_num == levels else ceil_16(end - half_rows), end]
        advance(
            level_num, starts_late[level_num - 2], ready, starts_late[level_num - 1], ends
        )
        ready = end
    late_out[...] = turn_over(early, window)
    late_copies = spread(late_out, late_in, late_send, late_recv, True)

    wide_lane = lax.broadcasted_iota(jnp.int32, (held, LANES), 1)
    pieces = [[] for _ in range(fold_size)]
    for source in range(owners):
        for late, begin, end in ((False, 0, early), (True, early, window)):
            for at in range(begin, end, LANES):
                fold, part = divmod(window * source + at, LANES)
                count = min(LANES, end - at)
                for where, low, high in (
                    (fold, part, min(LANES, part + count)),
                    (fold + 1, 0, part + count - LANES),
                ):
                    if where < fold_size and low < high:
                        pieces[where].append((low, high, source, late, at - begin, part))
    rolled = {}

    def rolled_tile(source, late, at, part):
        if (source, late, at) not in rolled:
            value = (late_in if late else early_in)[source, :, at : at + LANES]
            value = value.astype(jnp.float32)
            if part:
                value = pltpu.roll(value, part, axis=1)
            rolled[source, late, at] = value
        return rolled[source, late, at]

    def assemble(which):
        for fold in range(fold_size):
            some = [piece for piece in sorted(pieces[fold]) if piece[3] == which]
            if not some:
                continue
            where = slice(fold * FOLD_PITCH, fold * FOLD_PITCH + held)
            value = None
            if which and len(some) < len(pieces[fold]):
                value = folded[where, :]
            for low, high, source, late, at, part in some:
                piece = rolled_tile(source, late, at, part)
                if value is None:
                    value = piece
                elif high == LANES:
                    value = jnp.where(wide_lane < low, value, piece)
                elif low == 0:
                    value = jnp.where(wide_lane < high, piece, value)
                else:
                    value = jnp.where((wide_lane >= low) & (wide_lane < high), piece, value)
            folded[where, :] = value

    for copy, apart in early_copies:
        copy.wait()
    assemble(False)
    for load in loads[3:]:
        load.wait()
    for copy, apart in late_copies:

        @pl.when(me < owners - 1)
        def _():
            copy.wait_send()

        @pl.when(lax.rem(me + owners - apart, owners) < owners - 1)
        def _():
            copy.wait_recv()

    assemble(True)

    cosine, sine = twist_ref[0], twist_ref[1]
    for series in range(0, held, 2):
        pair = jnp.concatenate(
            [folded[pl.ds(series + side, fold_size, stride=FOLD_PITCH), :] for side in range(2)], axis=1
        )
        spun = jnp.dot(
            first_ref[...], pair.astype(jnp.bfloat16), preferred_element_type=jnp.float32
        )
        for side in range(2):
            real = spun[0:fold_size, side * LANES : (side + 1) * LANES]
            imag = spun[fold_size:, side * LANES : (side + 1) * LANES]
            at = (series + side) * fold_size
            twisted[at : at + fold_size, 0:LANES] = (real * cosine + imag * sine).astype(
                jnp.bfloat16
            )
            twisted[at : at + fold_size, LANES:] = (imag * cosine - real * sine).astype(
                jnp.bfloat16
            )
    half = fold_size
    scale = 1.0 / (length * channels)
    small_lane = lax.broadcasted_iota(jnp.int32, (half // 2, LANES), 1)
    for series in range(0, held, 4):
        at = series * fold_size
        waves = lax.dot_general(
            third_ref[...],
            twisted[at : at + 4 * fold_size, :],
            (((1,), (1,)), ((), ())),
            preferred_element_type=jnp.float32,
        )
        power = (waves[0:half] * waves[0:half] + waves[half:] * waves[half:]) * scale
        for side in range(2):
            even = power[0 : half // 2, side * LANES : (side + 1) * LANES]
            odd = power[half // 2 :, side * LANES : (side + 1) * LANES]
            left = jnp.where(small_lane < fold_size, even, pltpu.roll(odd, fold_size, axis=1))
            right = jnp.where(small_lane < fold_size, pltpu.roll(even, fold_size, axis=1), odd)
            spot = (series + 2 * side) * POWER_PITCH
            powers[spot : spot + half // 2, :] = left
            powers[spot + POWER_PITCH : spot + POWER_PITCH + half // 2, :] = right
    for block in range(0, held, GROUP):
        for tile in range(half // 2):
            out_ref[block : block + GROUP, tile * LANES : (tile + 1) * LANES] = powers[
                pl.ds(block * POWER_PITCH + tile, GROUP, stride=POWER_PITCH), :
            ]


def in_place(*operands):
    return [pltpu.with_memory_space_constraint(operand, pltpu.HBM) for operand in operands]


def local_sliced(samples, channel_order, merge_table):
    owners = lax.axis_size("sub")
    window, channels = samples.shape
    levels, _, rows = merge_table.shape
    held = rows // owners
    length = owners * (window - held)
    fold_size = length // LANES
    early = window - rows
    whole = window + rows
    order = channel_order.reshape(1, channels)
    first_table, twist, third_table = transform_tables(fold_size, length)
    return pl.pallas_call(
        functools.partial(merge_kernel, owners, length),
        out_shape=pltpu.VMEM((held, 64 * fold_size), jnp.float32),
        in_specs=[pl.BlockSpec(memory_space=pl.ANY)] * 6,
        out_specs=pl.BlockSpec(memory_space=pltpu.VMEM),
        scratch_shapes=[
            pltpu.VMEM((1, channels), jnp.int32),
            pltpu.VMEM((levels, 3, rows), jnp.int32),
            pltpu.VMEM((window, channels), jnp.bfloat16),
            pltpu.VMEM(first_table.shape, jnp.bfloat16),
            pltpu.VMEM(twist.shape, jnp.float32),
            pltpu.VMEM(third_table.shape, jnp.bfloat16),
            pltpu.VMEM((channels, channels), jnp.bfloat16),
            pltpu.VMEM((channels, channels), jnp.bfloat16),
            pltpu.VMEM((levels - 1, rows, 2 * rows), jnp.bfloat16),
            [pltpu.VMEM((whole, 2 * rows), jnp.float32)] * levels,
            [pltpu.VMEM((whole, rows), jnp.bfloat16)] * levels,
            pltpu.VMEM((rows, rows), jnp.bfloat16),
            pltpu.VMEM((rows, rows), jnp.bfloat16),
            pltpu.VMEM((rows, -(-early // LANES) * LANES), jnp.bfloat16),
            pltpu.VMEM((rows, rows), jnp.bfloat16),
            pltpu.VMEM((owners, held, -(-early // LANES) * LANES), jnp.bfloat16),
            pltpu.VMEM((owners, held, rows), jnp.bfloat16),
            pltpu.VMEM((FOLD_PITCH * fold_size, LANES), jnp.float32),
            pltpu.VMEM((held * fold_size, 2 * LANES), jnp.bfloat16),
            pltpu.VMEM((POWER_PITCH * held, LANES), jnp.float32),
            pltpu.SemaphoreType.DMA((4,)),
            pltpu.SemaphoreType.DMA((owners,)),
            pltpu.SemaphoreType.DMA((owners,)),
            pltpu.SemaphoreType.DMA((owners,)),
            pltpu.SemaphoreType.DMA((owners,)),
            pltpu.SemaphoreType.DMA((6,)),
        ],
        compiler_params=pltpu.CompilerParams(
            vmem_limit_bytes=40 * 1024 * 1024, collective_id=0, has_side_effects=True
        ),
        name="merge_rows",
    )(*in_place(order, merge_table, samples, first_table, twist, third_table))


def is_sliced(window, channels, owners, rows, levels):
    held = rows // owners
    length = owners * (window - held)
    return (
        held == 16
        and window % 16 == 0
        and rows == 2 * LANES
        and channels == 2 * rows
        and rows == 2 ** (levels - 1)
        and length == 64 * LANES
        and window > 2 * rows
    )


def local_any(samples, channel_order, merge_table):
    window, channels = samples.shape
    levels, _, rows = merge_table.shape
    if is_sliced(window, channels, lax.axis_size("sub"), rows, levels):
        return local_sliced(samples, channel_order, merge_table)
    return local(samples, channel_order, merge_table)


def solution(mesh):
    in_specs = (P(("groups", "sub"), None), P(), P())
    out_specs = P(("groups", "sub"), None)
    return jax.shard_map(local_any, mesh=mesh, in_specs=in_specs, out_specs=out_specs, check_vma=False)
```

```python
import functools
import math

import jax
import jax.numpy as jnp
import numpy as np
from jax import lax
from jax.experimental import pallas as pl
from jax.experimental.pallas import tpu as pltpu
from jax.sharding import PartitionSpec as P

LOCAL = 5
MESH = pl.DeviceIdType.MESH
CH_DEV = 32
SAMPLES = 8192


def from_partner(block, axis, apart):
    count = lax.axis_size(axis)
    route = []
    for low in range(count):
        high = low | 1 << apart
        if high != low and high < count:
            route += [(low, high), (high, low)]
    return lax.ppermute(block, axis, route)


def delay_rows(values, shifts, margin, time_axis):
    length = values.shape[time_axis]
    moved = values
    for bit_num in range(max(1, margin.bit_length())):
        offset = 2**bit_num
        rolled = jnp.pad(moved[:, offset:], ((0, 0), (0, offset)))
        flagged = shifts >> bit_num & 1 == 1
        flagged = flagged[:, None]
        moved = jnp.where(flagged, rolled, moved)
    return moved


def merge_level(current, entries, child_rows, span_rows, time_axis):
    outputs = jnp.arange(entries.shape[1], dtype=jnp.int32)
    starts = 2 * child_rows * (outputs // span_rows)
    lower_rows = jnp.take(current, starts + entries[0], axis=1 - time_axis)
    upper_rows = jnp.take(current, starts + child_rows + entries[1], axis=1 - time_axis)
    moved_rows = delay_rows(upper_rows, entries[2], child_rows, time_axis)
    return (lower_rows.astype(jnp.float32) + moved_rows.astype(jnp.float32)).astype(jnp.bfloat16)


def spectrum(delays, channels):
    row_count = delays.shape[0]
    length = delays.shape[1]
    fold_size = length // 128
    first_index = jnp.arange(fold_size, dtype=jnp.int32)
    lane_index = jnp.arange(128, dtype=jnp.int32)
    half_index = jnp.arange(64, dtype=jnp.int32)
    angle_one = (
        2.0
        * math.pi
        / fold_size
        * (first_index[:, None] * first_index[None, :] % fold_size).astype(jnp.float32)
    )
    cos_one = jnp.cos(angle_one).astype(jnp.bfloat16)
    sin_one = jnp.sin(angle_one).astype(jnp.bfloat16)
    angle_two = (
        2.0
        * math.pi
        / length
        * (first_index[:, None] * lane_index[None, :] % length).astype(jnp.float32)
    )
    twist_cos = jnp.cos(angle_two)
    twist_sin = jnp.sin(angle_two)
    angle_three = (
        2.0 * math.pi / 128 * (lane_index[:, None] * half_index[None, :] % 128).astype(jnp.float32)
    )
    cos_three = jnp.cos(angle_three).astype(jnp.bfloat16)
    sin_three = jnp.sin(angle_three).astype(jnp.bfloat16)
    series = delays.reshape(row_count, fold_size, 128)
    first_re = jnp.einsum("kn,rnm->rkm", cos_one, series, preferred_element_type=jnp.float32)
    first_im = -jnp.einsum("kn,rnm->rkm", sin_one, series, preferred_element_type=jnp.float32)
    twisted_re = (first_re * twist_cos + first_im * twist_sin).astype(jnp.bfloat16)
    twisted_im = (first_im * twist_cos - first_re * twist_sin).astype(jnp.bfloat16)
    out_re = jnp.einsum(
        "rkn,nj->rjk", twisted_re, cos_three, preferred_element_type=jnp.float32
    ) + jnp.einsum("rkn,nj->rjk", twisted_im, sin_three, preferred_element_type=jnp.float32)
    out_im = jnp.einsum(
        "rkn,nj->rjk", twisted_im, cos_three, preferred_element_type=jnp.float32
    ) - jnp.einsum("rkn,nj->rjk", twisted_re, sin_three, preferred_element_type=jnp.float32)
    power = (out_re * out_re + out_im * out_im) / (length * channels)
    return power.reshape(row_count, 64 * fold_size)


def local(samples, channel_order, merge_table):
    owners = lax.axis_size("sub")
    owner_index = lax.axis_index("sub")
    owned_rows = CH_DEV // 2
    quarter = CH_DEV // 4
    window = samples.shape[0]
    channels = samples.shape[1]
    ordered = jnp.take(samples, channel_order, axis=1).T.reshape(owners, CH_DEV, window)
    current = lax.all_to_all(ordered, "sub", split_axis=0, concat_axis=2, tiled=True).reshape(
        CH_DEV, window * owners
    )
    for level_num in range(1, LOCAL + 1):
        entries = lax.dynamic_slice_in_dim(
            merge_table[level_num - 1], owner_index * owned_rows, owned_rows, 1
        )
        current = merge_level(
            current, entries, max(1, 2 ** (level_num - 2)), 2 ** (level_num - 1), 1
        )
    block_index = jnp.zeros((), jnp.int32)
    for bit_num in range(owners.bit_length() - 1):
        level_num = LOCAL + bit_num + 1
        half_bit = owner_index >> bit_num & 1
        block_index = block_index * 2 + half_bit
        span_rows = owned_rows * 2 ** (bit_num + 1)
        child_rows = span_rows // 2
        subband = owner_index >> bit_num + 1
        entries = lax.dynamic_slice_in_dim(
            merge_table[level_num - 1],
            subband * span_rows + owned_rows * block_index,
            owned_rows,
            1,
        )
        kept_rows = lax.dynamic_slice_in_dim(current, half_bit * quarter, quarter, 0)
        sent_rows = lax.dynamic_slice_in_dim(current, (1 - half_bit) * quarter, quarter, 0)
        partner = from_partner(sent_rows, "sub", bit_num)
        row_base = quarter * block_index
        is_low = half_bit == 0
        lower_part = jnp.where(is_low, kept_rows, partner)
        upper_part = jnp.where(is_low, partner, kept_rows)
        lower_rows = jnp.take(lower_part, entries[0] - row_base, axis=0)
        upper_rows = jnp.take(upper_part, entries[1] - row_base, axis=0)
        moved_rows = delay_rows(upper_rows, entries[2], child_rows, 1)
        current = (lower_rows.astype(jnp.float32) + moved_rows.astype(jnp.float32)).astype(
            jnp.bfloat16
        )
    return spectrum(current[:, :SAMPLES], channels)


LANES = 128
GROUP = 8
FOLD_PITCH = 24
POWER_PITCH = 40


def widest_shift(level_num):
    return max(1, 2 ** (level_num - 2))


def still_to_come(level_num, levels):
    return sum(widest_shift(later) for later in range(level_num + 1, levels + 1))


def gathered(values, places, axis):
    other = 1 - axis
    numbers = lax.GatherDimensionNumbers(
        offset_dims=(),
        collapsed_slice_dims=(axis,),
        start_index_map=(axis,),
        operand_batching_dims=(other,),
        start_indices_batching_dims=(other,),
    )
    return lax.gather(
        values,
        places[..., None],
        numbers,
        slice_sizes=(1, 1),
        mode=lax.GatherScatterMode.PROMISE_IN_BOUNDS,
    )


def transform_tables(fold_size, length):
    first_index = np.arange(fold_size)
    lane_index = np.arange(LANES)
    half_index = np.concatenate([np.arange(0, 64, 2), np.arange(1, 64, 2)])
    unit = np.float32(2.0 * math.pi)

    def angles(left, right, period):
        turns = (left[:, None] * right[None, :]) % period
        return (unit / np.float32(period)) * turns.astype(np.float32)

    one = angles(first_index, first_index, fold_size)
    first_table = np.concatenate([np.cos(one), -np.sin(one)], axis=0)
    two = angles(first_index, lane_index, length)
    twist = np.stack([np.cos(two), np.sin(two)])
    three = angles(half_index, lane_index, LANES)
    cos_three, sin_three = np.cos(three), np.sin(three)
    third_table = np.concatenate(
        [
            np.concatenate([cos_three, sin_three], axis=1),
            np.concatenate([-sin_three, cos_three], axis=1),
        ],
        axis=0,
    )
    return (
        jnp.asarray(first_table, jnp.bfloat16),
        jnp.asarray(twist, jnp.float32),
        jnp.asarray(third_table, jnp.bfloat16),
    )


def one_hot(row_index, depth):
    rows = lax.broadcasted_iota(jnp.int32, (depth, row_index.shape[1]), 0)
    return (rows == row_index).astype(jnp.float32).astype(jnp.bfloat16)


def floor_16(count):
    return count // 16 * 16


def ceil_16(count):
    return -(-count // 16) * 16


def merge_kernel(
    owners,
    length,
    order_hbm,
    table_hbm,
    own_hbm,
    first_hbm,
    twist_hbm,
    third_hbm,
    out_ref,
    order_ref,
    table_ref,
    own_ref,
    first_ref,
    twist_ref,
    third_ref,
    split,
    choose,
    choices,
    first_picked,
    picked,
    tables,
    halo_out,
    placed,
    early_out,
    late_out,
    early_in,
    late_in,
    folded,
    twisted,
    powers,
    halo_sem,
    early_send,
    early_recv,
    late_send,
    late_recv,
    load_sem,
):
    levels, _, rows = table_ref.shape
    window, channels = own_ref.shape
    held = rows // owners
    fold_size = length // LANES
    me = lax.axis_index("sub")
    bits = owners.bit_length() - 1

    loads = [
        pltpu.make_async_copy(source, target, load_sem.at[place])
        for place, (source, target) in enumerate(
            [
                (order_hbm, order_ref),
                (table_hbm, table_ref),
                (own_hbm, own_ref),
                (first_hbm, first_ref),
                (twist_hbm, twist_ref),
                (third_hbm, third_ref),
            ]
        )
    ]
    for load in loads:
        load.start()
    barrier = pltpu.get_barrier_semaphore()
    column = lax.broadcasted_iota(jnp.int32, (1, channels), 1)
    paired = jnp.where(column < rows, 2 * column, 2 * (column - rows) + 1)
    stripe = channels // owners
    for apart in range(owners):
        if apart:
            pl.semaphore_signal(
                barrier,
                inc=1,
                device_id={"sub": lax.rem(me + apart, owners)},
                device_id_type=MESH,
            )
        split[apart * stripe : (apart + 1) * stripe, :] = one_hot(paired - apart * stripe, stripe)
    half_rows = rows // 2

    @pl.when(me == owners - 1)
    def _():
        tables[0][window:, :] = jnp.zeros((rows, rows), jnp.bfloat16)

    loads[0].wait()
    order = jnp.broadcast_to(order_ref[...], (16, channels))
    side = lax.broadcasted_iota(jnp.int32, (16, channels), 0)
    digits = jnp.where(side == 0, order >> 6, order & 63).astype(jnp.float32)
    digits = jnp.dot(
        digits.astype(jnp.bfloat16), split[...], preferred_element_type=jnp.float32
    ).astype(jnp.int32)
    choose[...] = one_hot(digits[0:1] * 64 + digits[1:2], channels)

    lane = lax.broadcasted_iota(jnp.int32, (1, LANES), 1)
    sublane = lax.broadcasted_iota(jnp.int32, (GROUP, LANES), 0)

    def combine(level_num, half, begin, end, lower_ref, upper_ref, given):
        span_rows = 2 ** (level_num - 1)
        base = half * half_rows
        count = (end - begin) // GROUP
        place = (lane + base) % span_rows // 16
        static = base % span_rows // 16
        amount = table_ref[level_num - 1][2:3, base : base + half_rows]
        reach = sublane + (amount - GROUP * place)
        inside = reach < GROUP
        turn = reach & (GROUP - 1)
        steps = max(0, min(span_rows, half_rows).bit_length() - 5)
        top = end + GROUP + GROUP * (static + 2**steps - 1)
        bottom = begin + GROUP * static
        upper = upper_ref[bottom : min(top, given), :]
        if top > given:
            filler = jnp.zeros((top - given, half_rows), jnp.float32)
            upper = jnp.concatenate([upper, filler], axis=0)
        for step in range(steps):
            offset = GROUP * 2**step
            flagged = (place - static) >> step & 1 == 1
            size = upper.shape[0]
            flagged = jnp.broadcast_to(flagged, (size - offset, half_rows))
            upper = jnp.where(flagged, upper[offset:], upper[: size - offset])
        spun = [
            gathered(upper[GROUP * part : GROUP * (part + 1)], turn, 0) for part in range(count + 1)
        ]
        moved = [jnp.where(inside, spun[part], spun[part + 1]) for part in range(count)]
        return lower_ref[begin:end, :] + jnp.concatenate(moved, axis=0)

    def combine_first(half, begin, end, given):
        at = half * half_rows
        return combine(
            1,
            half,
            begin,
            end,
            first_picked.at[:, at : at + half_rows],
            first_picked.at[:, rows + at : rows + at + half_rows],
            given,
        )

    loads[1].wait()
    loads[2].wait()
    ahead = ceil_16(rows + GROUP)
    first_picked[0:ahead, :] = jnp.dot(
        own_ref[0:ahead, :], choose[...], preferred_element_type=jnp.float32
    )
    last_row = lax.broadcasted_iota(jnp.int32, (16, half_rows), 0) == 15
    for part in range(2):
        values = combine_first(part, 0, rows, ahead)
        at = part * half_rows
        tables[0][0:rows, at : at + half_rows] = values.astype(jnp.bfloat16)
        top = (part + 1) * half_rows
        halo_out[0 : top - 16, at : at + half_rows] = values[0 : top - 16].astype(jnp.bfloat16)
        edge = jnp.broadcast_to(first_picked[0:1, rows + at : rows + at + half_rows], (16, half_rows))
        halo_out[top - 16 : top, at : at + half_rows] = jnp.where(
            last_row, edge, values[top - 16 : top]
        ).astype(jnp.bfloat16)

    pl.semaphore_wait(barrier, owners - 1)
    backs = [
        pltpu.make_async_remote_copy(
            src_ref=halo_out.at[0:count, first : first + half_rows],
            dst_ref=tables[0].at[window : window + count, first : first + half_rows],
            send_sem=halo_sem.at[part],
            recv_sem=halo_sem.at[2 + part],
            device_id={"sub": lax.rem(me + owners - 1, owners)},
            device_id_type=MESH,
        )
        for part, (count, first) in enumerate(((rows, half_rows), (half_rows, 0)))
    ]

    @pl.when(me > 0)
    def _():
        for back in backs:
            back.start()

    first_picked[ahead:window, :] = jnp.dot(
        own_ref[ahead:window, :], choose[...], preferred_element_type=jnp.float32
    )
    for part in range(2):
        values = combine_first(part, rows, window, window)
        at = part * half_rows
        tables[0][rows:window, at : at + half_rows] = values.astype(jnp.bfloat16)

    lanes = lax.broadcasted_iota(jnp.int32, (1, rows), 1)

    def prepare(level_num):
        child_rows = widest_shift(level_num)
        entries = table_ref[level_num - 1]
        if level_num == levels:
            choices[level_num - 2, 0] = one_hot(entries[0:1], half_rows)
            choices[level_num - 2, 1] = one_hot(entries[1:2], half_rows)
            return
        starts = 2 * child_rows * (lanes >> (level_num - 1))
        lower = starts + entries[0:1]
        upper = starts + child_rows + entries[1:2]
        for half in range(2):
            at = half * half_rows
            choices[level_num - 2, half, :, 0:half_rows] = one_hot(
                lower[:, at : at + half_rows] - at, half_rows
            )
            choices[level_num - 2, half, :, half_rows:] = one_hot(
                upper[:, at : at + half_rows] - at, half_rows
            )

    def advance(level_num, half, source_begin, source_end):
        at = half * half_rows
        picked[level_num - 2][half, source_begin:source_end, :] = jnp.dot(
            tables[level_num - 2][source_begin:source_end, at : at + half_rows],
            choices[level_num - 2, half],
            preferred_element_type=jnp.float32,
        )

    def finish(level_num, half, begin, end, given):
        at = half * half_rows
        lower, upper = (0, 1) if level_num == levels else (half, half)
        low_at, high_at = (at, at) if level_num == levels else (0, half_rows)
        tables[level_num - 1][begin:end, at : at + half_rows] = combine(
            level_num,
            half,
            begin,
            end,
            picked[level_num - 2].at[lower, :, low_at : low_at + half_rows],
            picked[level_num - 2].at[upper, :, high_at : high_at + half_rows],
            given,
        ).astype(jnp.bfloat16)

    def needed(level_num, half, edge):
        lag = 0 if half or level_num == levels else half_rows
        return edge + still_to_come(level_num, levels) - lag

    early = rows
    for level_num in range(2, levels + 1):
        prepare(level_num)
        ends = [ceil_16(needed(level_num - 1, half, early)) for half in range(2)]
        for half in range(2):
            advance(level_num, half, 0, ends[half])
        for half in range(2):
            given = ends[1] if level_num == levels else ends[half]
            finish(level_num, half, 0, ceil_16(needed(level_num, half, early)), given)

    spots = lax.broadcasted_iota(jnp.int32, (rows, rows), 0)
    shift = held.bit_length() - 1
    wanted = jnp.zeros_like(spots)
    for bit_num in range(bits):
        wanted = wanted | ((spots >> (shift + bit_num) & 1) << (bits - 1 - bit_num))
    wanted = (wanted << shift) + (spots & (held - 1))
    placed[...] = (
        (lax.broadcasted_iota(jnp.int32, (rows, rows), 1) == wanted)
        .astype(jnp.float32)
        .astype(jnp.bfloat16)
    )

    def turn_over(values):
        return lax.dot_general(
            placed[...],
            values,
            (((1,), (1,)), ((), ())),
            preferred_element_type=jnp.float32,
        )

    def put_blocks(target, begin):
        blocks = turn_over(tables[levels - 1][begin : begin + rows, :]).astype(jnp.bfloat16)
        for tile in range(rows // LANES):
            for owner in range(owners):
                target[owner, tile * held : (tile + 1) * held, :] = blocks[
                    owner * held : (owner + 1) * held, tile * LANES : (tile + 1) * LANES
                ]

    def spread(source, target, size, send_sem, recv_sem):
        copies = []
        for apart in range(1, owners):
            to = lax.rem(me + apart, owners)
            copy = pltpu.make_async_remote_copy(
                src_ref=source.at[to, 0:size],
                dst_ref=target.at[me, 0:size],
                send_sem=send_sem.at[apart],
                recv_sem=recv_sem.at[apart],
                device_id={"sub": to},
                device_id_type=MESH,
            )
            copies.append(copy)
            copy.start()
        target[me] = source[me]
        return copies

    put_blocks(early_out, 0)
    early_copies = spread(early_out, early_in, 2 * held, early_send, early_recv)

    @pl.when(me < owners - 1)
    def _():
        for back in backs:
            back.wait_recv()

    @pl.when(me > 0)
    def _():
        for back in backs:
            back.wait_send()

    for part in range(2):
        at = part * half_rows
        top = window + (part + 1) * half_rows
        fill = tables[0][window - 16 : window, at : at + half_rows].astype(jnp.float32)
        edge = tables[0][top - 16 : top, at : at + half_rows].astype(jnp.float32)[15:16]
        amount = table_ref[0][2:3, at : at + half_rows]
        late_edge = last_row & jnp.broadcast_to(amount > 0, (16, half_rows))
        fill = fill + jnp.where(late_edge, jnp.broadcast_to(edge, (16, half_rows)), 0.0)
        tables[0][window - 16 : window, at : at + half_rows] = fill.astype(jnp.bfloat16)
    for level_num in range(2, levels + 1):
        begins = [floor_16(needed(level_num - 1, half, early)) for half in range(2)]
        ends = [ceil_16(needed(level_num - 1, half, window)) for half in range(2)]
        for half in range(2):
            advance(level_num, half, begins[half], ends[half])
        for half in range(2):
            given = ends[1] if level_num == levels else ends[half]
            finish(
                level_num,
                half,
                floor_16(needed(level_num, half, early)),
                ceil_16(needed(level_num, half, window)),
                given,
            )
    put_blocks(late_out, early)
    rest = window - 2 * rows
    tail = tables[levels - 1][2 * rows : window, :]
    tail = turn_over(jnp.concatenate([tail] * (LANES // rest), axis=0))
    row_spot = lax.broadcasted_iota(jnp.int32, (rows, LANES), 0)
    turned = window * me // rest % (LANES // rest)
    lane_spot = lax.broadcasted_iota(jnp.int32, (rows, LANES), 1) // rest
    tail = jnp.where((row_spot + lane_spot) % (LANES // rest) == turned, tail, 0.0).astype(jnp.bfloat16)
    packed_rows = rows * rest // LANES
    gather_rows = (
        lax.broadcasted_iota(jnp.int32, (packed_rows, rows), 1) // (LANES // rest)
        == lax.broadcasted_iota(jnp.int32, (packed_rows, rows), 0)
    )
    tail = jnp.dot(
        gather_rows.astype(jnp.float32).astype(jnp.bfloat16),
        tail,
        preferred_element_type=jnp.float32,
    ).astype(jnp.bfloat16)
    extra = packed_rows // owners
    for owner in range(owners):
        late_out[owner, 2 * held : 2 * held + extra, :] = tail[
            owner * extra : (owner + 1) * extra
        ]
    late_copies = spread(late_out, late_in, 2 * held + extra, late_send, late_recv)

    wide_lane = lax.broadcasted_iota(jnp.int32, (held, LANES), 1)
    pieces = [[] for _ in range(fold_size)]
    for source in range(owners):
        for at in range(0, window, LANES):
            fold, part = divmod(window * source + at, LANES)
            count = min(LANES, window - at)
            for where, low, high in (
                (fold, part, min(LANES, part + count)),
                (fold + 1, 0, part + count - LANES),
            ):
                if where < fold_size and low < high:
                    pieces[where].append((low, high, source, at >= early, at, part))
    rolled = {}

    def rolled_tile(source, late, at, part):
        if (source, at) not in rolled:
            if at < 2 * rows:
                place = (at - early if late else at) // LANES * held
                value = (late_in if late else early_in)[source, place : place + held, :]
                value = value.astype(jnp.float32)
                if part:
                    value = pltpu.roll(value, part, axis=1)
            else:
                value = late_in[source, 2 * held : 3 * held, :].astype(jnp.float32)
                value = jnp.concatenate(
                    [
                        pltpu.roll(
                            jnp.broadcast_to(value[row : row + 1], (LANES // rest, LANES)),
                            0,
                            axis=1,
                            stride=rest,
                            stride_axis=0,
                        )
                        for row in range(extra)
                    ],
                    axis=0,
                )
            rolled[source, at] = value
        return rolled[source, at]

    def assemble(which):
        for fold in range(fold_size):
            some = [piece for piece in sorted(pieces[fold]) if piece[3] == which]
            if not some:
                continue
            where = slice(fold * FOLD_PITCH, fold * FOLD_PITCH + held)
            value = None
            if which and len(some) < len(pieces[fold]):
                value = folded[where, :]
            for low, high, source, late, at, part in some:
                piece = rolled_tile(source, late, at, part)
                if value is None:
                    value = piece
                elif high == LANES:
                    value = jnp.where(wide_lane < low, value, piece)
                elif low == 0:
                    value = jnp.where(wide_lane < high, piece, value)
                else:
                    value = jnp.where((wide_lane >= low) & (wide_lane < high), piece, value)
            folded[where, :] = value

    for copy in early_copies:
        copy.wait()
    assemble(False)
    for load in loads[3:]:
        load.wait()
    for copy in late_copies:
        copy.wait()

    assemble(True)

    cosine, sine = twist_ref[0], twist_ref[1]
    for series in range(0, held, 2):
        pair = jnp.concatenate(
            [folded[pl.ds(series + side, fold_size, stride=FOLD_PITCH), :] for side in range(2)], axis=1
        )
        spun = jnp.dot(
            first_ref[...], pair.astype(jnp.bfloat16), preferred_element_type=jnp.float32
        )
        for side in range(2):
            real = spun[0:fold_size, side * LANES : (side + 1) * LANES]
            imag = spun[fold_size:, side * LANES : (side + 1) * LANES]
            at = (series + side) * fold_size
            twisted[at : at + fold_size, 0:LANES] = (real * cosine + imag * sine).astype(
                jnp.bfloat16
            )
            twisted[at : at + fold_size, LANES:] = (imag * cosine - real * sine).astype(
                jnp.bfloat16
            )
    half = fold_size
    scale = 1.0 / (length * channels)
    small_lane = lax.broadcasted_iota(jnp.int32, (half // 2, LANES), 1)
    for series in range(0, held, 4):
        at = series * fold_size
        waves = lax.dot_general(
            third_ref[...],
            twisted[at : at + 4 * fold_size, :],
            (((1,), (1,)), ((), ())),
            preferred_element_type=jnp.float32,
        )
        power = (waves[0:half] * waves[0:half] + waves[half:] * waves[half:]) * scale
        for side in range(2):
            even = power[0 : half // 2, side * LANES : (side + 1) * LANES]
            odd = power[half // 2 :, side * LANES : (side + 1) * LANES]
            left = jnp.where(small_lane < fold_size, even, pltpu.roll(odd, fold_size, axis=1))
            right = jnp.where(small_lane < fold_size, pltpu.roll(even, fold_size, axis=1), odd)
            spot = (series + 2 * side) * POWER_PITCH
            powers[spot : spot + half // 2, :] = left
            powers[spot + POWER_PITCH : spot + POWER_PITCH + half // 2, :] = right
    for block in range(0, held, GROUP):
        for tile in range(half // 2):
            out_ref[block : block + GROUP, tile * LANES : (tile + 1) * LANES] = powers[
                pl.ds(block * POWER_PITCH + tile, GROUP, stride=POWER_PITCH), :
            ]


def in_place(*operands):
    return [pltpu.with_memory_space_constraint(operand, pltpu.HBM) for operand in operands]


def local_sliced(samples, channel_order, merge_table):
    owners = lax.axis_size("sub")
    window, channels = samples.shape
    levels, _, rows = merge_table.shape
    held = rows // owners
    length = owners * (window - held)
    fold_size = length // LANES
    whole = window + rows
    order = channel_order.reshape(1, channels)
    first_table, twist, third_table = transform_tables(fold_size, length)
    return pl.pallas_call(
        functools.partial(merge_kernel, owners, length),
        out_shape=pltpu.VMEM((held, 64 * fold_size), jnp.float32),
        in_specs=[pl.BlockSpec(memory_space=pl.ANY)] * 6,
        out_specs=pl.BlockSpec(memory_space=pltpu.VMEM),
        scratch_shapes=[
            pltpu.VMEM((1, channels), jnp.int32),
            pltpu.VMEM((levels, 3, rows), jnp.int32),
            pltpu.VMEM((window, channels), jnp.bfloat16),
            pltpu.VMEM(first_table.shape, jnp.bfloat16),
            pltpu.VMEM(twist.shape, jnp.float32),
            pltpu.VMEM(third_table.shape, jnp.bfloat16),
            pltpu.VMEM((channels, channels), jnp.bfloat16),
            pltpu.VMEM((channels, channels), jnp.bfloat16),
            pltpu.VMEM((levels - 1, 2, rows // 2, rows), jnp.bfloat16),
            pltpu.VMEM((window, channels), jnp.float32),
            [pltpu.VMEM((2, whole, rows), jnp.float32)] * (levels - 1),
            [pltpu.VMEM((whole, rows), jnp.bfloat16)] * levels,
            pltpu.VMEM((rows, rows), jnp.bfloat16),
            pltpu.VMEM((rows, rows), jnp.bfloat16),
            pltpu.VMEM((owners, 2 * held, LANES), jnp.bfloat16),
            pltpu.VMEM((owners, 3 * held, LANES), jnp.bfloat16),
            pltpu.VMEM((owners, 2 * held, LANES), jnp.bfloat16),
            pltpu.VMEM((owners, 3 * held, LANES), jnp.bfloat16),
            pltpu.VMEM((FOLD_PITCH * fold_size, LANES), jnp.float32),
            pltpu.VMEM((held * fold_size, 2 * LANES), jnp.bfloat16),
            pltpu.VMEM((POWER_PITCH * held, LANES), jnp.float32),
            pltpu.SemaphoreType.DMA((4,)),
            pltpu.SemaphoreType.DMA((owners,)),
            pltpu.SemaphoreType.DMA((owners,)),
            pltpu.SemaphoreType.DMA((owners,)),
            pltpu.SemaphoreType.DMA((owners,)),
            pltpu.SemaphoreType.DMA((6,)),
        ],
        compiler_params=pltpu.CompilerParams(
            vmem_limit_bytes=40 * 1024 * 1024, collective_id=0, has_side_effects=True
        ),
        name="merge_rows",
    )(*in_place(order, merge_table, samples, first_table, twist, third_table))


def is_sliced(window, channels, owners, rows, levels):
    held = rows // owners
    length = owners * (window - held)
    return (
        held == 16
        and window % 16 == 0
        and rows == 2 * LANES
        and channels == 2 * rows
        and rows == 2 ** (levels - 1)
        and length == 64 * LANES
        and window == 2 * rows + 16
        and owners == 16
    )


def local_any(samples, channel_order, merge_table):
    window, channels = samples.shape
    levels, _, rows = merge_table.shape
    if is_sliced(window, channels, lax.axis_size("sub"), rows, levels):
        return local_sliced(samples, channel_order, merge_table)
    return local(samples, channel_order, merge_table)


def solution(mesh):
    in_specs = (P(("groups", "sub"), None), P(), P())
    out_specs = P(("groups", "sub"), None)
    return jax.shard_map(local_any, mesh=mesh, in_specs=in_specs, out_specs=out_specs, check_vma=False)
```

```python
import functools
import math

import jax
import jax.numpy as jnp
import numpy as np
from jax import lax
from jax.experimental import pallas as pl
from jax.experimental.pallas import tpu as pltpu
from jax.sharding import PartitionSpec as P

LOCAL = 5
MESH = pl.DeviceIdType.MESH
CH_DEV = 32
SAMPLES = 8192


def from_partner(block, axis, apart):
    count = lax.axis_size(axis)
    route = []
    for low in range(count):
        high = low | 1 << apart
        if high != low and high < count:
            route += [(low, high), (high, low)]
    return lax.ppermute(block, axis, route)


def delay_rows(values, shifts, margin, time_axis):
    length = values.shape[time_axis]
    moved = values
    for bit_num in range(max(1, margin.bit_length())):
        offset = 2**bit_num
        rolled = jnp.pad(moved[:, offset:], ((0, 0), (0, offset)))
        flagged = shifts >> bit_num & 1 == 1
        flagged = flagged[:, None]
        moved = jnp.where(flagged, rolled, moved)
    return moved


def merge_level(current, entries, child_rows, span_rows, time_axis):
    outputs = jnp.arange(entries.shape[1], dtype=jnp.int32)
    starts = 2 * child_rows * (outputs // span_rows)
    lower_rows = jnp.take(current, starts + entries[0], axis=1 - time_axis)
    upper_rows = jnp.take(current, starts + child_rows + entries[1], axis=1 - time_axis)
    moved_rows = delay_rows(upper_rows, entries[2], child_rows, time_axis)
    return (lower_rows.astype(jnp.float32) + moved_rows.astype(jnp.float32)).astype(jnp.bfloat16)


def spectrum(delays, channels):
    row_count = delays.shape[0]
    length = delays.shape[1]
    fold_size = length // 128
    first_index = jnp.arange(fold_size, dtype=jnp.int32)
    lane_index = jnp.arange(128, dtype=jnp.int32)
    half_index = jnp.arange(64, dtype=jnp.int32)
    angle_one = (
        2.0
        * math.pi
        / fold_size
        * (first_index[:, None] * first_index[None, :] % fold_size).astype(jnp.float32)
    )
    cos_one = jnp.cos(angle_one).astype(jnp.bfloat16)
    sin_one = jnp.sin(angle_one).astype(jnp.bfloat16)
    angle_two = (
        2.0
        * math.pi
        / length
        * (first_index[:, None] * lane_index[None, :] % length).astype(jnp.float32)
    )
    twist_cos = jnp.cos(angle_two)
    twist_sin = jnp.sin(angle_two)
    angle_three = (
        2.0 * math.pi / 128 * (lane_index[:, None] * half_index[None, :] % 128).astype(jnp.float32)
    )
    cos_three = jnp.cos(angle_three).astype(jnp.bfloat16)
    sin_three = jnp.sin(angle_three).astype(jnp.bfloat16)
    series = delays.reshape(row_count, fold_size, 128)
    first_re = jnp.einsum("kn,rnm->rkm", cos_one, series, preferred_element_type=jnp.float32)
    first_im = -jnp.einsum("kn,rnm->rkm", sin_one, series, preferred_element_type=jnp.float32)
    twisted_re = (first_re * twist_cos + first_im * twist_sin).astype(jnp.bfloat16)
    twisted_im = (first_im * twist_cos - first_re * twist_sin).astype(jnp.bfloat16)
    out_re = jnp.einsum(
        "rkn,nj->rjk", twisted_re, cos_three, preferred_element_type=jnp.float32
    ) + jnp.einsum("rkn,nj->rjk", twisted_im, sin_three, preferred_element_type=jnp.float32)
    out_im = jnp.einsum(
        "rkn,nj->rjk", twisted_im, cos_three, preferred_element_type=jnp.float32
    ) - jnp.einsum("rkn,nj->rjk", twisted_re, sin_three, preferred_element_type=jnp.float32)
    power = (out_re * out_re + out_im * out_im) / (length * channels)
    return power.reshape(row_count, 64 * fold_size)


def local(samples, channel_order, merge_table):
    owners = lax.axis_size("sub")
    owner_index = lax.axis_index("sub")
    owned_rows = CH_DEV // 2
    quarter = CH_DEV // 4
    window = samples.shape[0]
    channels = samples.shape[1]
    ordered = jnp.take(samples, channel_order, axis=1).T.reshape(owners, CH_DEV, window)
    current = lax.all_to_all(ordered, "sub", split_axis=0, concat_axis=2, tiled=True).reshape(
        CH_DEV, window * owners
    )
    for level_num in range(1, LOCAL + 1):
        entries = lax.dynamic_slice_in_dim(
            merge_table[level_num - 1], owner_index * owned_rows, owned_rows, 1
        )
        current = merge_level(
            current, entries, max(1, 2 ** (level_num - 2)), 2 ** (level_num - 1), 1
        )
    block_index = jnp.zeros((), jnp.int32)
    for bit_num in range(owners.bit_length() - 1):
        level_num = LOCAL + bit_num + 1
        half_bit = owner_index >> bit_num & 1
        block_index = block_index * 2 + half_bit
        span_rows = owned_rows * 2 ** (bit_num + 1)
        child_rows = span_rows // 2
        subband = owner_index >> bit_num + 1
        entries = lax.dynamic_slice_in_dim(
            merge_table[level_num - 1],
            subband * span_rows + owned_rows * block_index,
            owned_rows,
            1,
        )
        kept_rows = lax.dynamic_slice_in_dim(current, half_bit * quarter, quarter, 0)
        sent_rows = lax.dynamic_slice_in_dim(current, (1 - half_bit) * quarter, quarter, 0)
        partner = from_partner(sent_rows, "sub", bit_num)
        row_base = quarter * block_index
        is_low = half_bit == 0
        lower_part = jnp.where(is_low, kept_rows, partner)
        upper_part = jnp.where(is_low, partner, kept_rows)
        lower_rows = jnp.take(lower_part, entries[0] - row_base, axis=0)
        upper_rows = jnp.take(upper_part, entries[1] - row_base, axis=0)
        moved_rows = delay_rows(upper_rows, entries[2], child_rows, 1)
        current = (lower_rows.astype(jnp.float32) + moved_rows.astype(jnp.float32)).astype(
            jnp.bfloat16
        )
    return spectrum(current[:, :SAMPLES], channels)


LANES = 128
GROUP = 8
FOLD_PITCH = 24
POWER_PITCH = 40


def widest_shift(level_num):
    return max(1, 2 ** (level_num - 2))


def still_to_come(level_num, levels):
    return sum(widest_shift(later) for later in range(level_num + 1, levels + 1))


def gathered(values, places, axis):
    other = 1 - axis
    numbers = lax.GatherDimensionNumbers(
        offset_dims=(),
        collapsed_slice_dims=(axis,),
        start_index_map=(axis,),
        operand_batching_dims=(other,),
        start_indices_batching_dims=(other,),
    )
    return lax.gather(
        values,
        places[..., None],
        numbers,
        slice_sizes=(1, 1),
        mode=lax.GatherScatterMode.PROMISE_IN_BOUNDS,
    )


def transform_tables(fold_size, length):
    first_index = np.arange(fold_size)
    lane_index = np.arange(LANES)
    half_index = np.concatenate([np.arange(0, 64, 2), np.arange(1, 64, 2)])
    unit = np.float32(2.0 * math.pi)

    def angles(left, right, period):
        turns = (left[:, None] * right[None, :]) % period
        return (unit / np.float32(period)) * turns.astype(np.float32)

    one = angles(first_index, first_index, fold_size)
    first_table = np.concatenate([np.cos(one), -np.sin(one)], axis=0)
    two = angles(first_index, lane_index, length)
    twist = np.stack([np.cos(two), np.sin(two)])
    three = angles(half_index, lane_index, LANES)
    cos_three, sin_three = np.cos(three), np.sin(three)
    third_table = np.concatenate(
        [
            np.concatenate([cos_three, sin_three], axis=1),
            np.concatenate([-sin_three, cos_three], axis=1),
        ],
        axis=0,
    )
    return (
        jnp.asarray(first_table, jnp.bfloat16),
        jnp.asarray(twist, jnp.float32),
        jnp.asarray(third_table, jnp.bfloat16),
    )


def one_hot(row_index, depth):
    rows = lax.broadcasted_iota(jnp.int32, (depth, row_index.shape[1]), 0)
    return (rows == row_index).astype(jnp.float32).astype(jnp.bfloat16)


def floor_16(count):
    return count // 16 * 16


def ceil_16(count):
    return -(-count // 16) * 16


def merge_kernel(
    owners,
    length,
    order_hbm,
    table_hbm,
    own_hbm,
    first_hbm,
    twist_hbm,
    third_hbm,
    out_ref,
    order_ref,
    table_ref,
    own_ref,
    first_ref,
    twist_ref,
    third_ref,
    split,
    choose,
    choices,
    first_picked,
    picked,
    tables,
    halo_out,
    placed,
    early_out,
    late_out,
    early_in,
    late_in,
    folded,
    twisted,
    powers,
    halo_sem,
    early_send,
    early_recv,
    late_send,
    late_recv,
    load_sem,
):
    levels, _, rows = table_ref.shape
    window, channels = own_ref.shape
    held = rows // owners
    fold_size = length // LANES
    me = lax.axis_index("sub")
    bits = owners.bit_length() - 1

    loads = [
        pltpu.make_async_copy(source, target, load_sem.at[place])
        for place, (source, target) in enumerate(
            [
                (order_hbm, order_ref),
                (table_hbm, table_ref),
                (own_hbm, own_ref),
                (first_hbm, first_ref),
                (twist_hbm, twist_ref),
                (third_hbm, third_ref),
            ]
        )
    ]
    for load in loads:
        load.start()
    barrier = pltpu.get_barrier_semaphore()
    column = lax.broadcasted_iota(jnp.int32, (1, channels), 1)
    paired = jnp.where(column < rows, 2 * column, 2 * (column - rows) + 1)
    stripe = channels // owners
    for apart in range(owners):
        if apart:
            pl.semaphore_signal(
                barrier,
                inc=1,
                device_id={"sub": lax.rem(me + apart, owners)},
                device_id_type=MESH,
            )
        split[apart * stripe : (apart + 1) * stripe, :] = one_hot(paired - apart * stripe, stripe)
    half_rows = rows // 2

    @pl.when(me == owners - 1)
    def _():
        tables[0][window:, :] = jnp.zeros((rows, rows), jnp.bfloat16)

    loads[0].wait()
    order = jnp.broadcast_to(order_ref[...], (16, channels))
    side = lax.broadcasted_iota(jnp.int32, (16, channels), 0)
    digits = jnp.where(side == 0, order >> 6, order & 63).astype(jnp.float32)
    digits = jnp.dot(
        digits.astype(jnp.bfloat16), split[...], preferred_element_type=jnp.float32
    ).astype(jnp.int32)
    choose[...] = one_hot(digits[0:1] * 64 + digits[1:2], channels)

    lane = lax.broadcasted_iota(jnp.int32, (1, LANES), 1)
    sublane = lax.broadcasted_iota(jnp.int32, (GROUP, LANES), 0)

    def combine(level_num, half, begin, end, lower_ref, upper_ref, given):
        span_rows = 2 ** (level_num - 1)
        base = half * half_rows
        count = (end - begin) // GROUP
        place = (lane + base) % span_rows // 16
        static = base % span_rows // 16
        amount = table_ref[level_num - 1][2:3, base : base + half_rows]
        reach = sublane + (amount - GROUP * place)
        inside = reach < GROUP
        turn = reach & (GROUP - 1)
        steps = max(0, min(span_rows, half_rows).bit_length() - 5)
        top = end + GROUP + GROUP * (static + 2**steps - 1)
        bottom = begin + GROUP * static
        upper = upper_ref[bottom : min(top, given), :]
        if top > given:
            filler = jnp.zeros((top - given, half_rows), jnp.float32)
            upper = jnp.concatenate([upper, filler], axis=0)
        for step in range(steps):
            offset = GROUP * 2**step
            flagged = (place - static) >> step & 1 == 1
            size = upper.shape[0]
            flagged = jnp.broadcast_to(flagged, (size - offset, half_rows))
            upper = jnp.where(flagged, upper[offset:], upper[: size - offset])
        spun = [
            gathered(upper[GROUP * part : GROUP * (part + 1)], turn, 0) for part in range(count + 1)
        ]
        moved = [jnp.where(inside, spun[part], spun[part + 1]) for part in range(count)]
        return lower_ref[begin:end, :] + jnp.concatenate(moved, axis=0)

    def combine_first(half, begin, end, given):
        at = half * half_rows
        return combine(
            1,
            half,
            begin,
            end,
            first_picked.at[:, at : at + half_rows],
            first_picked.at[:, rows + at : rows + at + half_rows],
            given,
        )

    loads[1].wait()
    lanes = lax.broadcasted_iota(jnp.int32, (1, rows), 1)

    def prepare(level_num):
        child_rows = widest_shift(level_num)
        entries = table_ref[level_num - 1]
        if level_num == levels:
            choices[level_num - 2, 0] = one_hot(entries[0:1], half_rows)
            choices[level_num - 2, 1] = one_hot(entries[1:2], half_rows)
            return
        starts = 2 * child_rows * (lanes >> (level_num - 1))
        lower = starts + entries[0:1]
        upper = starts + child_rows + entries[1:2]
        for half in range(2):
            at = half * half_rows
            choices[level_num - 2, half, :, 0:half_rows] = one_hot(
                lower[:, at : at + half_rows] - at, half_rows
            )
            choices[level_num - 2, half, :, half_rows:] = one_hot(
                upper[:, at : at + half_rows] - at, half_rows
            )

    for level_num in range(2, levels + 1):
        prepare(level_num)

    loads[2].wait()
    ahead = ceil_16(rows + GROUP)
    first_picked[0:ahead, :] = jnp.dot(
        own_ref[0:ahead, :], choose[...], preferred_element_type=jnp.float32
    )
    last_row = lax.broadcasted_iota(jnp.int32, (16, half_rows), 0) == 15
    for part in range(2):
        values = combine_first(part, 0, rows, ahead)
        at = part * half_rows
        tables[0][0:rows, at : at + half_rows] = values.astype(jnp.bfloat16)
        top = (part + 1) * half_rows
        halo_out[0 : top - 16, at : at + half_rows] = values[0 : top - 16].astype(jnp.bfloat16)
        edge = jnp.broadcast_to(first_picked[0:1, rows + at : rows + at + half_rows], (16, half_rows))
        halo_out[top - 16 : top, at : at + half_rows] = jnp.where(
            last_row, edge, values[top - 16 : top]
        ).astype(jnp.bfloat16)

    first_picked[ahead:window, :] = jnp.dot(
        own_ref[ahead:window, :], choose[...], preferred_element_type=jnp.float32
    )
    for part in range(2):
        values = combine_first(part, rows, window, window)
        at = part * half_rows
        tables[0][rows:window, at : at + half_rows] = values.astype(jnp.bfloat16)

    def advance(level_num, half, source_begin, source_end):
        at = half * half_rows
        picked[level_num - 2][half, source_begin:source_end, :] = jnp.dot(
            tables[level_num - 2][source_begin:source_end, at : at + half_rows],
            choices[level_num - 2, half],
            preferred_element_type=jnp.float32,
        )

    def finish(level_num, half, begin, end, given):
        at = half * half_rows
        lower, upper = (0, 1) if level_num == levels else (half, half)
        low_at, high_at = (at, at) if level_num == levels else (0, half_rows)
        tables[level_num - 1][begin:end, at : at + half_rows] = combine(
            level_num,
            half,
            begin,
            end,
            picked[level_num - 2].at[lower, :, low_at : low_at + half_rows],
            picked[level_num - 2].at[upper, :, high_at : high_at + half_rows],
            given,
        ).astype(jnp.bfloat16)

    def needed(level_num, half, edge):
        lag = 0 if half or level_num == levels else half_rows
        return edge + still_to_come(level_num, levels) - lag

    early = rows
    pl.semaphore_wait(barrier, owners - 1)
    backs = [
        pltpu.make_async_remote_copy(
            src_ref=halo_out.at[0:count, first : first + half_rows],
            dst_ref=tables[0].at[window : window + count, first : first + half_rows],
            send_sem=halo_sem.at[part],
            recv_sem=halo_sem.at[2 + part],
            device_id={"sub": lax.rem(me + owners - 1, owners)},
            device_id_type=MESH,
        )
        for part, (count, first) in enumerate(((rows, half_rows), (half_rows, 0)))
    ]

    @pl.when(me > 0)
    def _():
        for back in backs:
            back.start()

    for level_num in range(1 + 1, levels + 1):
        ends = [ceil_16(needed(level_num - 1, half, early)) for half in range(2)]
        for half in range(2):
            advance(level_num, half, 0, ends[half])
        for half in range(2):
            given = ends[1] if level_num == levels else ends[half]
            finish(level_num, half, 0, ceil_16(needed(level_num, half, early)), given)

    spots = lax.broadcasted_iota(jnp.int32, (rows, rows), 0)
    shift = held.bit_length() - 1
    wanted = jnp.zeros_like(spots)
    for bit_num in range(bits):
        wanted = wanted | ((spots >> (shift + bit_num) & 1) << (bits - 1 - bit_num))
    wanted = (wanted << shift) + (spots & (held - 1))
    placed[...] = (
        (lax.broadcasted_iota(jnp.int32, (rows, rows), 1) == wanted)
        .astype(jnp.float32)
        .astype(jnp.bfloat16)
    )

    def turn_over(values):
        return lax.dot_general(
            placed[...],
            values,
            (((1,), (1,)), ((), ())),
            preferred_element_type=jnp.float32,
        )

    def put_blocks(target, begin):
        blocks = turn_over(tables[levels - 1][begin : begin + rows, :]).astype(jnp.bfloat16)
        for tile in range(rows // LANES):
            for owner in range(owners):
                target[owner, tile * held : (tile + 1) * held, :] = blocks[
                    owner * held : (owner + 1) * held, tile * LANES : (tile + 1) * LANES
                ]

    def spread(source, target, size, send_sem, recv_sem):
        copies = []
        for apart in range(1, owners):
            to = lax.rem(me + apart, owners)
            copy = pltpu.make_async_remote_copy(
                src_ref=source.at[to, 0:size],
                dst_ref=target.at[me, 0:size],
                send_sem=send_sem.at[apart],
                recv_sem=recv_sem.at[apart],
                device_id={"sub": to},
                device_id_type=MESH,
            )
            copies.append(copy)
            copy.start()
        target[me] = source[me]
        return copies

    put_blocks(early_out, 0)
    early_copies = spread(early_out, early_in, 2 * held, early_send, early_recv)

    @pl.when(me < owners - 1)
    def _():
        for back in backs:
            back.wait_recv()

    @pl.when(me > 0)
    def _():
        for back in backs:
            back.wait_send()

    for part in range(2):
        at = part * half_rows
        top = window + (part + 1) * half_rows
        fill = tables[0][window - 16 : window, at : at + half_rows].astype(jnp.float32)
        edge = tables[0][top - 16 : top, at : at + half_rows].astype(jnp.float32)[15:16]
        amount = table_ref[0][2:3, at : at + half_rows]
        late_edge = last_row & jnp.broadcast_to(amount > 0, (16, half_rows))
        fill = fill + jnp.where(late_edge, jnp.broadcast_to(edge, (16, half_rows)), 0.0)
        tables[0][window - 16 : window, at : at + half_rows] = fill.astype(jnp.bfloat16)
    for level_num in range(2, levels + 1):
        begins = [floor_16(needed(level_num - 1, half, early)) for half in range(2)]
        ends = [ceil_16(needed(level_num - 1, half, window)) for half in range(2)]
        for half in range(2):
            advance(level_num, half, begins[half], ends[half])
        for half in range(2):
            given = ends[1] if level_num == levels else ends[half]
            finish(
                level_num,
                half,
                floor_16(needed(level_num, half, early)),
                ceil_16(needed(level_num, half, window)),
                given,
            )
    put_blocks(late_out, early)
    rest = window - 2 * rows
    tail = tables[levels - 1][2 * rows : window, :]
    tail = turn_over(jnp.concatenate([tail] * (LANES // rest), axis=0))
    row_spot = lax.broadcasted_iota(jnp.int32, (rows, LANES), 0)
    turned = window * me // rest % (LANES // rest)
    lane_spot = lax.broadcasted_iota(jnp.int32, (rows, LANES), 1) // rest
    tail = jnp.where((row_spot + lane_spot) % (LANES // rest) == turned, tail, 0.0).astype(jnp.bfloat16)
    packed_rows = rows * rest // LANES
    gather_rows = (
        lax.broadcasted_iota(jnp.int32, (packed_rows, rows), 1) // (LANES // rest)
        == lax.broadcasted_iota(jnp.int32, (packed_rows, rows), 0)
    )
    tail = jnp.dot(
        gather_rows.astype(jnp.float32).astype(jnp.bfloat16),
        tail,
        preferred_element_type=jnp.float32,
    ).astype(jnp.bfloat16)
    extra = packed_rows // owners
    for owner in range(owners):
        late_out[owner, 2 * held : 2 * held + extra, :] = tail[
            owner * extra : (owner + 1) * extra
        ]
    late_copies = spread(late_out, late_in, 2 * held + extra, late_send, late_recv)

    wide_lane = lax.broadcasted_iota(jnp.int32, (held, LANES), 1)
    pieces = [[] for _ in range(fold_size)]
    for source in range(owners):
        for at in range(0, window, LANES):
            fold, part = divmod(window * source + at, LANES)
            count = min(LANES, window - at)
            for where, low, high in (
                (fold, part, min(LANES, part + count)),
                (fold + 1, 0, part + count - LANES),
            ):
                if where < fold_size and low < high:
                    pieces[where].append((low, high, source, at >= early, at, part))
    rolled = {}

    def rolled_tile(source, late, at, part):
        if (source, at) not in rolled:
            if at < 2 * rows:
                place = (at - early if late else at) // LANES * held
                value = (late_in if late else early_in)[source, place : place + held, :]
                value = value.astype(jnp.float32)
                if part:
                    value = pltpu.roll(value, part, axis=1)
            else:
                value = late_in[source, 2 * held : 3 * held, :].astype(jnp.float32)
                value = jnp.concatenate(
                    [
                        pltpu.roll(
                            jnp.broadcast_to(value[row : row + 1], (LANES // rest, LANES)),
                            0,
                            axis=1,
                            stride=rest,
                            stride_axis=0,
                        )
                        for row in range(extra)
                    ],
                    axis=0,
                )
            rolled[source, at] = value
        return rolled[source, at]

    def assemble(which):
        for fold in range(fold_size):
            some = [piece for piece in sorted(pieces[fold]) if piece[3] == which]
            if not some:
                continue
            where = slice(fold * FOLD_PITCH, fold * FOLD_PITCH + held)
            value = None
            if which and len(some) < len(pieces[fold]):
                value = folded[where, :]
            for low, high, source, late, at, part in some:
                piece = rolled_tile(source, late, at, part)
                if value is None:
                    value = piece
                elif high == LANES:
                    value = jnp.where(wide_lane < low, value, piece)
                elif low == 0:
                    value = jnp.where(wide_lane < high, piece, value)
                else:
                    value = jnp.where((wide_lane >= low) & (wide_lane < high), piece, value)
            folded[where, :] = value

    for copy in early_copies:
        copy.wait()
    assemble(False)
    for load in loads[3:]:
        load.wait()
    for copy in late_copies:
        copy.wait()

    assemble(True)

    cosine, sine = twist_ref[0], twist_ref[1]
    for series in range(0, held, 2):
        pair = jnp.concatenate(
            [folded[pl.ds(series + side, fold_size, stride=FOLD_PITCH), :] for side in range(2)], axis=1
        )
        spun = jnp.dot(
            first_ref[...], pair.astype(jnp.bfloat16), preferred_element_type=jnp.float32
        )
        for side in range(2):
            real = spun[0:fold_size, side * LANES : (side + 1) * LANES]
            imag = spun[fold_size:, side * LANES : (side + 1) * LANES]
            at = (series + side) * fold_size
            twisted[at : at + fold_size, 0:LANES] = (real * cosine + imag * sine).astype(
                jnp.bfloat16
            )
            twisted[at : at + fold_size, LANES:] = (imag * cosine - real * sine).astype(
                jnp.bfloat16
            )
    half = fold_size
    scale = 1.0 / (length * channels)
    small_lane = lax.broadcasted_iota(jnp.int32, (half // 2, LANES), 1)
    for series in range(0, held, 4):
        at = series * fold_size
        waves = lax.dot_general(
            third_ref[...],
            twisted[at : at + 4 * fold_size, :],
            (((1,), (1,)), ((), ())),
            preferred_element_type=jnp.float32,
        )
        power = (waves[0:half] * waves[0:half] + waves[half:] * waves[half:]) * scale
        for side in range(2):
            even = power[0 : half // 2, side * LANES : (side + 1) * LANES]
            odd = power[half // 2 :, side * LANES : (side + 1) * LANES]
            left = jnp.where(small_lane < fold_size, even, pltpu.roll(odd, fold_size, axis=1))
            right = jnp.where(small_lane < fold_size, pltpu.roll(even, fold_size, axis=1), odd)
            spot = (series + 2 * side) * POWER_PITCH
            powers[spot : spot + half // 2, :] = left
            powers[spot + POWER_PITCH : spot + POWER_PITCH + half // 2, :] = right
    for block in range(0, held, GROUP):
        for tile in range(half // 2):
            out_ref[block : block + GROUP, tile * LANES : (tile + 1) * LANES] = powers[
                pl.ds(block * POWER_PITCH + tile, GROUP, stride=POWER_PITCH), :
            ]


def in_place(*operands):
    return [pltpu.with_memory_space_constraint(operand, pltpu.HBM) for operand in operands]


def local_sliced(samples, channel_order, merge_table):
    owners = lax.axis_size("sub")
    window, channels = samples.shape
    levels, _, rows = merge_table.shape
    held = rows // owners
    length = owners * (window - held)
    fold_size = length // LANES
    whole = window + rows
    order = channel_order.reshape(1, channels)
    first_table, twist, third_table = transform_tables(fold_size, length)
    return pl.pallas_call(
        functools.partial(merge_kernel, owners, length),
        out_shape=pltpu.VMEM((held, 64 * fold_size), jnp.float32),
        in_specs=[pl.BlockSpec(memory_space=pl.ANY)] * 6,
        out_specs=pl.BlockSpec(memory_space=pltpu.VMEM),
        scratch_shapes=[
            pltpu.VMEM((1, channels), jnp.int32),
            pltpu.VMEM((levels, 3, rows), jnp.int32),
            pltpu.VMEM((window, channels), jnp.bfloat16),
            pltpu.VMEM(first_table.shape, jnp.bfloat16),
            pltpu.VMEM(twist.shape, jnp.float32),
            pltpu.VMEM(third_table.shape, jnp.bfloat16),
            pltpu.VMEM((channels, channels), jnp.bfloat16),
            pltpu.VMEM((channels, channels), jnp.bfloat16),
            pltpu.VMEM((levels - 1, 2, rows // 2, rows), jnp.bfloat16),
            pltpu.VMEM((window, channels), jnp.float32),
            [pltpu.VMEM((2, whole, rows), jnp.float32)] * (levels - 1),
            [pltpu.VMEM((whole, rows), jnp.bfloat16)] * levels,
            pltpu.VMEM((rows, rows), jnp.bfloat16),
            pltpu.VMEM((rows, rows), jnp.bfloat16),
            pltpu.VMEM((owners, 2 * held, LANES), jnp.bfloat16),
            pltpu.VMEM((owners, 3 * held, LANES), jnp.bfloat16),
            pltpu.VMEM((owners, 2 * held, LANES), jnp.bfloat16),
            pltpu.VMEM((owners, 3 * held, LANES), jnp.bfloat16),
            pltpu.VMEM((FOLD_PITCH * fold_size, LANES), jnp.float32),
            pltpu.VMEM((held * fold_size, 2 * LANES), jnp.bfloat16),
            pltpu.VMEM((POWER_PITCH * held, LANES), jnp.float32),
            pltpu.SemaphoreType.DMA((4,)),
            pltpu.SemaphoreType.DMA((owners,)),
            pltpu.SemaphoreType.DMA((owners,)),
            pltpu.SemaphoreType.DMA((owners,)),
            pltpu.SemaphoreType.DMA((owners,)),
            pltpu.SemaphoreType.DMA((6,)),
        ],
        compiler_params=pltpu.CompilerParams(
            vmem_limit_bytes=40 * 1024 * 1024, collective_id=0, has_side_effects=True
        ),
        name="merge_rows",
    )(*in_place(order, merge_table, samples, first_table, twist, third_table))


def is_sliced(window, channels, owners, rows, levels):
    held = rows // owners
    length = owners * (window - held)
    return (
        held == 16
        and window % 16 == 0
        and rows == 2 * LANES
        and channels == 2 * rows
        and rows == 2 ** (levels - 1)
        and length == 64 * LANES
        and window == 2 * rows + 16
        and owners == 16
    )


def local_any(samples, channel_order, merge_table):
    window, channels = samples.shape
    levels, _, rows = merge_table.shape
    if is_sliced(window, channels, lax.axis_size("sub"), rows, levels):
        return local_sliced(samples, channel_order, merge_table)
    return local(samples, channel_order, merge_table)


def solution(mesh):
    in_specs = (P(("groups", "sub"), None), P(), P())
    out_specs = P(("groups", "sub"), None)
    return jax.shard_map(local_any, mesh=mesh, in_specs=in_specs, out_specs=out_specs, check_vma=False)
```

```python
import functools
import math

import jax
import jax.numpy as jnp
import numpy as np
from jax import lax
from jax.experimental import pallas as pl
from jax.experimental.pallas import tpu as pltpu
from jax.sharding import PartitionSpec as P

LOCAL = 5
MESH = pl.DeviceIdType.MESH
CH_DEV = 32
SAMPLES = 8192


def from_partner(block, axis, apart):
    count = lax.axis_size(axis)
    route = []
    for low in range(count):
        high = low | 1 << apart
        if high != low and high < count:
            route += [(low, high), (high, low)]
    return lax.ppermute(block, axis, route)


def delay_rows(values, shifts, margin, time_axis):
    length = values.shape[time_axis]
    moved = values
    for bit_num in range(max(1, margin.bit_length())):
        offset = 2**bit_num
        rolled = jnp.pad(moved[:, offset:], ((0, 0), (0, offset)))
        flagged = shifts >> bit_num & 1 == 1
        flagged = flagged[:, None]
        moved = jnp.where(flagged, rolled, moved)
    return moved


def merge_level(current, entries, child_rows, span_rows, time_axis):
    outputs = jnp.arange(entries.shape[1], dtype=jnp.int32)
    starts = 2 * child_rows * (outputs // span_rows)
    lower_rows = jnp.take(current, starts + entries[0], axis=1 - time_axis)
    upper_rows = jnp.take(current, starts + child_rows + entries[1], axis=1 - time_axis)
    moved_rows = delay_rows(upper_rows, entries[2], child_rows, time_axis)
    return (lower_rows.astype(jnp.float32) + moved_rows.astype(jnp.float32)).astype(jnp.bfloat16)


def spectrum(delays, channels):
    row_count = delays.shape[0]
    length = delays.shape[1]
    fold_size = length // 128
    first_index = jnp.arange(fold_size, dtype=jnp.int32)
    lane_index = jnp.arange(128, dtype=jnp.int32)
    half_index = jnp.arange(64, dtype=jnp.int32)
    angle_one = (
        2.0
        * math.pi
        / fold_size
        * (first_index[:, None] * first_index[None, :] % fold_size).astype(jnp.float32)
    )
    cos_one = jnp.cos(angle_one).astype(jnp.bfloat16)
    sin_one = jnp.sin(angle_one).astype(jnp.bfloat16)
    angle_two = (
        2.0
        * math.pi
        / length
        * (first_index[:, None] * lane_index[None, :] % length).astype(jnp.float32)
    )
    twist_cos = jnp.cos(angle_two)
    twist_sin = jnp.sin(angle_two)
    angle_three = (
        2.0 * math.pi / 128 * (lane_index[:, None] * half_index[None, :] % 128).astype(jnp.float32)
    )
    cos_three = jnp.cos(angle_three).astype(jnp.bfloat16)
    sin_three = jnp.sin(angle_three).astype(jnp.bfloat16)
    series = delays.reshape(row_count, fold_size, 128)
    first_re = jnp.einsum("kn,rnm->rkm", cos_one, series, preferred_element_type=jnp.float32)
    first_im = -jnp.einsum("kn,rnm->rkm", sin_one, series, preferred_element_type=jnp.float32)
    twisted_re = (first_re * twist_cos + first_im * twist_sin).astype(jnp.bfloat16)
    twisted_im = (first_im * twist_cos - first_re * twist_sin).astype(jnp.bfloat16)
    out_re = jnp.einsum(
        "rkn,nj->rjk", twisted_re, cos_three, preferred_element_type=jnp.float32
    ) + jnp.einsum("rkn,nj->rjk", twisted_im, sin_three, preferred_element_type=jnp.float32)
    out_im = jnp.einsum(
        "rkn,nj->rjk", twisted_im, cos_three, preferred_element_type=jnp.float32
    ) - jnp.einsum("rkn,nj->rjk", twisted_re, sin_three, preferred_element_type=jnp.float32)
    power = (out_re * out_re + out_im * out_im) / (length * channels)
    return power.reshape(row_count, 64 * fold_size)


def local(samples, channel_order, merge_table):
    owners = lax.axis_size("sub")
    owner_index = lax.axis_index("sub")
    owned_rows = CH_DEV // 2
    quarter = CH_DEV // 4
    window = samples.shape[0]
    channels = samples.shape[1]
    ordered = jnp.take(samples, channel_order, axis=1).T.reshape(owners, CH_DEV, window)
    current = lax.all_to_all(ordered, "sub", split_axis=0, concat_axis=2, tiled=True).reshape(
        CH_DEV, window * owners
    )
    for level_num in range(1, LOCAL + 1):
        entries = lax.dynamic_slice_in_dim(
            merge_table[level_num - 1], owner_index * owned_rows, owned_rows, 1
        )
        current = merge_level(
            current, entries, max(1, 2 ** (level_num - 2)), 2 ** (level_num - 1), 1
        )
    block_index = jnp.zeros((), jnp.int32)
    for bit_num in range(owners.bit_length() - 1):
        level_num = LOCAL + bit_num + 1
        half_bit = owner_index >> bit_num & 1
        block_index = block_index * 2 + half_bit
        span_rows = owned_rows * 2 ** (bit_num + 1)
        child_rows = span_rows // 2
        subband = owner_index >> bit_num + 1
        entries = lax.dynamic_slice_in_dim(
            merge_table[level_num - 1],
            subband * span_rows + owned_rows * block_index,
            owned_rows,
            1,
        )
        kept_rows = lax.dynamic_slice_in_dim(current, half_bit * quarter, quarter, 0)
        sent_rows = lax.dynamic_slice_in_dim(current, (1 - half_bit) * quarter, quarter, 0)
        partner = from_partner(sent_rows, "sub", bit_num)
        row_base = quarter * block_index
        is_low = half_bit == 0
        lower_part = jnp.where(is_low, kept_rows, partner)
        upper_part = jnp.where(is_low, partner, kept_rows)
        lower_rows = jnp.take(lower_part, entries[0] - row_base, axis=0)
        upper_rows = jnp.take(upper_part, entries[1] - row_base, axis=0)
        moved_rows = delay_rows(upper_rows, entries[2], child_rows, 1)
        current = (lower_rows.astype(jnp.float32) + moved_rows.astype(jnp.float32)).astype(
            jnp.bfloat16
        )
    return spectrum(current[:, :SAMPLES], channels)


LANES = 128
GROUP = 8
FOLD_PITCH = 24
POWER_PITCH = 40


def widest_shift(level_num):
    return max(1, 2 ** (level_num - 2))


def still_to_come(level_num, levels):
    return sum(widest_shift(later) for later in range(level_num + 1, levels + 1))


def gathered(values, places, axis):
    other = 1 - axis
    numbers = lax.GatherDimensionNumbers(
        offset_dims=(),
        collapsed_slice_dims=(axis,),
        start_index_map=(axis,),
        operand_batching_dims=(other,),
        start_indices_batching_dims=(other,),
    )
    return lax.gather(
        values,
        places[..., None],
        numbers,
        slice_sizes=(1, 1),
        mode=lax.GatherScatterMode.PROMISE_IN_BOUNDS,
    )


def transform_tables(fold_size, length):
    first_index = np.arange(fold_size)
    lane_index = np.arange(LANES)
    half_index = np.concatenate([np.arange(0, 64, 2), np.arange(1, 64, 2)])
    unit = np.float32(2.0 * math.pi)

    def angles(left, right, period):
        turns = (left[:, None] * right[None, :]) % period
        return (unit / np.float32(period)) * turns.astype(np.float32)

    one = angles(first_index, first_index, fold_size)
    first_table = np.concatenate([np.cos(one), -np.sin(one)], axis=0)
    two = angles(first_index, lane_index, length)
    twist = np.stack([np.cos(two), np.sin(two)])
    three = angles(half_index, lane_index, LANES)
    cos_three, sin_three = np.cos(three), np.sin(three)
    third_table = np.concatenate(
        [
            np.concatenate([cos_three, sin_three], axis=1),
            np.concatenate([-sin_three, cos_three], axis=1),
        ],
        axis=0,
    )
    return (
        jnp.asarray(first_table, jnp.bfloat16),
        jnp.asarray(twist, jnp.float32),
        jnp.asarray(third_table, jnp.bfloat16),
    )


def one_hot(row_index, depth):
    rows = lax.broadcasted_iota(jnp.int32, (depth, row_index.shape[1]), 0)
    return (rows == row_index).astype(jnp.float32).astype(jnp.bfloat16)


def floor_16(count):
    return count // 16 * 16


def ceil_16(count):
    return -(-count // 16) * 16


def merge_kernel(
    owners,
    length,
    order_hbm,
    table_hbm,
    own_hbm,
    first_hbm,
    twist_hbm,
    third_hbm,
    out_ref,
    order_ref,
    table_ref,
    own_ref,
    first_ref,
    twist_ref,
    third_ref,
    split,
    choose,
    choices,
    first_picked,
    picked,
    tables,
    halo_out,
    placed,
    early_out,
    late_out,
    early_in,
    late_in,
    folded,
    twisted,
    powers,
    halo_sem,
    exchange_sem,
    load_sem,
):
    levels, _, rows = table_ref.shape
    window, channels = own_ref.shape
    held = rows // owners
    fold_size = length // LANES
    me = lax.axis_index("sub")
    bits = owners.bit_length() - 1

    loads = [
        pltpu.make_async_copy(source, target, load_sem.at[place])
        for place, (source, target) in enumerate(
            [
                (order_hbm, order_ref),
                (table_hbm, table_ref),
                (own_hbm, own_ref),
                (first_hbm, first_ref),
                (twist_hbm, twist_ref),
                (third_hbm, third_ref),
            ]
        )
    ]
    for load in loads:
        load.start()
    barrier = pltpu.get_barrier_semaphore()
    column = lax.broadcasted_iota(jnp.int32, (1, channels), 1)
    paired = jnp.where(column < rows, 2 * column, 2 * (column - rows) + 1)
    stripe = channels // owners
    for apart in range(owners):
        if apart:
            far = owners // 2 + (apart // 2 if apart % 2 else -(apart // 2))
            pl.semaphore_signal(
                barrier,
                inc=1,
                device_id={"sub": lax.rem(me + far, owners)},
                device_id_type=MESH,
            )
        split[apart * stripe : (apart + 1) * stripe, :] = one_hot(paired - apart * stripe, stripe)
    half_rows = rows // 2

    @pl.when(me == owners - 1)
    def _():
        tables[0][window:, :] = jnp.zeros((rows, rows), jnp.bfloat16)

    loads[0].wait()
    order = jnp.broadcast_to(order_ref[...], (16, channels))
    side = lax.broadcasted_iota(jnp.int32, (16, channels), 0)
    digits = jnp.where(side == 0, order >> 6, order & 63).astype(jnp.float32)
    digits = jnp.dot(
        digits.astype(jnp.bfloat16), split[...], preferred_element_type=jnp.float32
    ).astype(jnp.int32)
    choose[...] = one_hot(digits[0:1] * 64 + digits[1:2], channels)

    lane = lax.broadcasted_iota(jnp.int32, (1, LANES), 1)
    sublane = lax.broadcasted_iota(jnp.int32, (GROUP, LANES), 0)

    def combine(level_num, half, begin, end, lower_ref, upper_ref, given):
        span_rows = 2 ** (level_num - 1)
        base = half * half_rows
        count = (end - begin) // GROUP
        place = (lane + base) % span_rows // 16
        static = base % span_rows // 16
        amount = table_ref[level_num - 1][2:3, base : base + half_rows]
        reach = sublane + (amount - GROUP * place)
        inside = reach < GROUP
        turn = reach & (GROUP - 1)
        steps = max(0, min(span_rows, half_rows).bit_length() - 5)
        top = end + GROUP + GROUP * (static + 2**steps - 1)
        bottom = begin + GROUP * static
        upper = upper_ref[bottom : min(top, given), :]
        if top > given:
            filler = jnp.zeros((top - given, half_rows), jnp.float32)
            upper = jnp.concatenate([upper, filler], axis=0)
        for step in range(steps):
            offset = GROUP * 2**step
            flagged = (place - static) >> step & 1 == 1
            size = upper.shape[0]
            flagged = jnp.broadcast_to(flagged, (size - offset, half_rows))
            upper = jnp.where(flagged, upper[offset:], upper[: size - offset])
        spun = [
            gathered(upper[GROUP * part : GROUP * (part + 1)], turn, 0) for part in range(count + 1)
        ]
        moved = [jnp.where(inside, spun[part], spun[part + 1]) for part in range(count)]
        return lower_ref[begin:end, :] + jnp.concatenate(moved, axis=0)

    def combine_first(half, begin, end, given):
        at = half * half_rows
        return combine(
            1,
            half,
            begin,
            end,
            first_picked.at[:, at : at + half_rows],
            first_picked.at[:, rows + at : rows + at + half_rows],
            given,
        )

    loads[1].wait()
    lanes = lax.broadcasted_iota(jnp.int32, (1, rows), 1)

    def prepare(level_num):
        child_rows = widest_shift(level_num)
        entries = table_ref[level_num - 1]
        if level_num == levels:
            choices[level_num - 2, 0] = one_hot(entries[0:1], half_rows)
            choices[level_num - 2, 1] = one_hot(entries[1:2], half_rows)
            return
        starts = 2 * child_rows * (lanes >> (level_num - 1))
        lower = starts + entries[0:1]
        upper = starts + child_rows + entries[1:2]
        for half in range(2):
            at = half * half_rows
            choices[level_num - 2, half, :, 0:half_rows] = one_hot(
                lower[:, at : at + half_rows] - at, half_rows
            )
            choices[level_num - 2, half, :, half_rows:] = one_hot(
                upper[:, at : at + half_rows] - at, half_rows
            )

    for level_num in range(2, levels + 1):
        prepare(level_num)

    loads[2].wait()
    ahead = ceil_16(rows + GROUP)
    first_picked[0:ahead, :] = jnp.dot(
        own_ref[0:ahead, :], choose[...], preferred_element_type=jnp.float32
    )
    last_row = lax.broadcasted_iota(jnp.int32, (16, half_rows), 0) == 15
    for part in range(2):
        values = combine_first(part, 0, rows, ahead)
        at = part * half_rows
        tables[0][0:rows, at : at + half_rows] = values.astype(jnp.bfloat16)
        top = (part + 1) * half_rows
        halo_out[0 : top - 16, at : at + half_rows] = values[0 : top - 16].astype(jnp.bfloat16)
        edge = jnp.broadcast_to(first_picked[0:1, rows + at : rows + at + half_rows], (16, half_rows))
        halo_out[top - 16 : top, at : at + half_rows] = jnp.where(
            last_row, edge, values[top - 16 : top]
        ).astype(jnp.bfloat16)

    first_picked[ahead:window, :] = jnp.dot(
        own_ref[ahead:window, :], choose[...], preferred_element_type=jnp.float32
    )
    for part in range(2):
        values = combine_first(part, rows, window, window)
        at = part * half_rows
        tables[0][rows:window, at : at + half_rows] = values.astype(jnp.bfloat16)

    def advance(level_num, half, source_begin, source_end):
        at = half * half_rows
        picked[level_num - 2][half, source_begin:source_end, :] = jnp.dot(
            tables[level_num - 2][source_begin:source_end, at : at + half_rows],
            choices[level_num - 2, half],
            preferred_element_type=jnp.float32,
        )

    def finish(level_num, half, begin, end, given):
        at = half * half_rows
        lower, upper = (0, 1) if level_num == levels else (half, half)
        low_at, high_at = (at, at) if level_num == levels else (0, half_rows)
        tables[level_num - 1][begin:end, at : at + half_rows] = combine(
            level_num,
            half,
            begin,
            end,
            picked[level_num - 2].at[lower, :, low_at : low_at + half_rows],
            picked[level_num - 2].at[upper, :, high_at : high_at + half_rows],
            given,
        ).astype(jnp.bfloat16)

    def needed(level_num, half, edge):
        lag = 0 if half or level_num == levels else half_rows
        return edge + still_to_come(level_num, levels) - lag

    early = rows
    pl.semaphore_wait(barrier, owners - 1)
    backs = [
        pltpu.make_async_remote_copy(
            src_ref=halo_out.at[0:count, first : first + half_rows],
            dst_ref=tables[0].at[window : window + count, first : first + half_rows],
            send_sem=halo_sem.at[part],
            recv_sem=halo_sem.at[2 + part],
            device_id={"sub": lax.rem(me + owners - 1, owners)},
            device_id_type=MESH,
        )
        for part, (count, first) in enumerate(((rows, half_rows), (half_rows, 0)))
    ]

    @pl.when(me > 0)
    def _():
        for back in backs:
            back.start()

    for level_num in range(2, levels + 1):
        ends = [ceil_16(needed(level_num - 1, half, early)) for half in range(2)]
        for half in range(2):
            advance(level_num, half, 0, ends[half])
        for half in range(2):
            given = ends[1] if level_num == levels else ends[half]
            finish(level_num, half, 0, ceil_16(needed(level_num, half, early)), given)

    spots = lax.broadcasted_iota(jnp.int32, (rows, rows), 0)
    shift = held.bit_length() - 1
    wanted = jnp.zeros_like(spots)
    for bit_num in range(bits):
        wanted = wanted | ((spots >> (shift + bit_num) & 1) << (bits - 1 - bit_num))
    wanted = (wanted << shift) + (spots & (held - 1))
    placed[...] = (
        (lax.broadcasted_iota(jnp.int32, (rows, rows), 1) == wanted)
        .astype(jnp.float32)
        .astype(jnp.bfloat16)
    )

    def turn_over(values):
        return lax.dot_general(
            placed[...],
            values,
            (((1,), (1,)), ((), ())),
            preferred_element_type=jnp.float32,
        )

    def put_blocks(target, begin):
        blocks = turn_over(tables[levels - 1][begin : begin + rows, :]).astype(jnp.bfloat16)
        for tile in range(rows // LANES):
            for owner in range(owners):
                target[owner, tile * held : (tile + 1) * held, :] = blocks[
                    owner * held : (owner + 1) * held, tile * LANES : (tile + 1) * LANES
                ]

    def spread(source, target, size, send_sem, recv_sem):
        for apart in range(1, owners):
            to = lax.rem(me + apart, owners)
            pltpu.make_async_remote_copy(
                src_ref=source.at[to, 0:size],
                dst_ref=target.at[me, 0:size],
                send_sem=send_sem,
                recv_sem=recv_sem,
                device_id={"sub": to},
                device_id_type=MESH,
            ).start()
        target[me] = source[me]
        return pltpu.make_async_remote_copy(
            src_ref=source.at[1:owners, 0:size],
            dst_ref=target.at[1:owners, 0:size],
            send_sem=send_sem,
            recv_sem=recv_sem,
            device_id={"sub": lax.rem(me + 1, owners)},
            device_id_type=MESH,
        )

    put_blocks(early_out, 0)
    early_blocks = spread(early_out, early_in, 2 * held, exchange_sem.at[0], exchange_sem.at[1])

    @pl.when(me < owners - 1)
    def _():
        for back in backs:
            back.wait_recv()

    @pl.when(me > 0)
    def _():
        for back in backs:
            back.wait_send()

    for part in range(2):
        at = part * half_rows
        top = window + (part + 1) * half_rows
        fill = tables[0][window - 16 : window, at : at + half_rows].astype(jnp.float32)
        edge = tables[0][top - 16 : top, at : at + half_rows].astype(jnp.float32)[15:16]
        amount = table_ref[0][2:3, at : at + half_rows]
        late_edge = last_row & jnp.broadcast_to(amount > 0, (16, half_rows))
        fill = fill + jnp.where(late_edge, jnp.broadcast_to(edge, (16, half_rows)), 0.0)
        tables[0][window - 16 : window, at : at + half_rows] = fill.astype(jnp.bfloat16)
    for level_num in range(2, levels + 1):
        begins = [floor_16(needed(level_num - 1, half, early)) for half in range(2)]
        ends = [ceil_16(needed(level_num - 1, half, window)) for half in range(2)]
        for half in range(2):
            advance(level_num, half, begins[half], ends[half])
        for half in range(2):
            given = ends[1] if level_num == levels else ends[half]
            finish(
                level_num,
                half,
                floor_16(needed(level_num, half, early)),
                ceil_16(needed(level_num, half, window)),
                given,
            )
    put_blocks(late_out, early)
    rest = window - 2 * rows
    tail = tables[levels - 1][2 * rows : window, :]
    tail = turn_over(jnp.concatenate([tail] * (LANES // rest), axis=0))
    row_spot = lax.broadcasted_iota(jnp.int32, (rows, LANES), 0)
    turned = window * me // rest % (LANES // rest)
    lane_spot = lax.broadcasted_iota(jnp.int32, (rows, LANES), 1) // rest
    tail = jnp.where((row_spot + lane_spot) % (LANES // rest) == turned, tail, 0.0).astype(jnp.bfloat16)
    packed_rows = rows * rest // LANES
    gather_rows = (
        lax.broadcasted_iota(jnp.int32, (packed_rows, rows), 1) // (LANES // rest)
        == lax.broadcasted_iota(jnp.int32, (packed_rows, rows), 0)
    )
    tail = jnp.dot(
        gather_rows.astype(jnp.float32).astype(jnp.bfloat16),
        tail,
        preferred_element_type=jnp.float32,
    ).astype(jnp.bfloat16)
    extra = packed_rows // owners
    for owner in range(owners):
        late_out[owner, 2 * held : 2 * held + extra, :] = tail[
            owner * extra : (owner + 1) * extra
        ]
    late_blocks = spread(late_out, late_in, 2 * held + extra, exchange_sem.at[2], exchange_sem.at[3])

    wide_lane = lax.broadcasted_iota(jnp.int32, (held, LANES), 1)
    pieces = [[] for _ in range(fold_size)]
    for source in range(owners):
        for at in range(0, window, LANES):
            fold, part = divmod(window * source + at, LANES)
            count = min(LANES, window - at)
            for where, low, high in (
                (fold, part, min(LANES, part + count)),
                (fold + 1, 0, part + count - LANES),
            ):
                if where < fold_size and low < high:
                    pieces[where].append((low, high, source, at >= early, at, part))
    rolled = {}

    def rolled_tile(source, late, at, part):
        if (source, at) not in rolled:
            if at < 2 * rows:
                place = (at - early if late else at) // LANES * held
                value = (late_in if late else early_in)[source, place : place + held, :]
                value = value.astype(jnp.float32)
                if part:
                    value = pltpu.roll(value, part, axis=1)
            else:
                value = late_in[source, 2 * held : 3 * held, :].astype(jnp.float32)
                value = jnp.concatenate(
                    [
                        pltpu.roll(
                            jnp.broadcast_to(value[row : row + 1], (LANES // rest, LANES)),
                            0,
                            axis=1,
                            stride=rest,
                            stride_axis=0,
                        )
                        for row in range(extra)
                    ],
                    axis=0,
                )
            rolled[source, at] = value
        return rolled[source, at]

    def assemble(which):
        for fold in range(fold_size):
            some = [piece for piece in sorted(pieces[fold]) if piece[3] == which]
            if not some:
                continue
            where = slice(fold * FOLD_PITCH, fold * FOLD_PITCH + held)
            value = None
            if which and len(some) < len(pieces[fold]):
                value = folded[where, :]
            for low, high, source, late, at, part in some:
                piece = rolled_tile(source, late, at, part)
                if value is None:
                    value = piece
                elif high == LANES:
                    value = jnp.where(wide_lane < low, value, piece)
                elif low == 0:
                    value = jnp.where(wide_lane < high, piece, value)
                else:
                    value = jnp.where((wide_lane >= low) & (wide_lane < high), piece, value)
            folded[where, :] = value

    early_blocks.wait_recv()
    assemble(False)
    for load in loads[3:]:
        load.wait()
    early_blocks.wait_send()
    late_blocks.wait_send()
    late_blocks.wait_recv()

    assemble(True)

    cosine, sine = twist_ref[0], twist_ref[1]
    for series in range(0, held, 2):
        pair = jnp.concatenate(
            [folded[pl.ds(series + side, fold_size, stride=FOLD_PITCH), :] for side in range(2)], axis=1
        )
        spun = jnp.dot(
            first_ref[...], pair.astype(jnp.bfloat16), preferred_element_type=jnp.float32
        )
        for side in range(2):
            real = spun[0:fold_size, side * LANES : (side + 1) * LANES]
            imag = spun[fold_size:, side * LANES : (side + 1) * LANES]
            at = (series + side) * fold_size
            twisted[at : at + fold_size, 0:LANES] = (real * cosine + imag * sine).astype(
                jnp.bfloat16
            )
            twisted[at : at + fold_size, LANES:] = (imag * cosine - real * sine).astype(
                jnp.bfloat16
            )
    half = fold_size
    scale = 1.0 / (length * channels)
    small_lane = lax.broadcasted_iota(jnp.int32, (half // 2, LANES), 1)
    for series in range(0, held, 4):
        at = series * fold_size
        waves = lax.dot_general(
            third_ref[...],
            twisted[at : at + 4 * fold_size, :],
            (((1,), (1,)), ((), ())),
            preferred_element_type=jnp.float32,
        )
        power = (waves[0:half] * waves[0:half] + waves[half:] * waves[half:]) * scale
        for side in range(2):
            even = power[0 : half // 2, side * LANES : (side + 1) * LANES]
            odd = power[half // 2 :, side * LANES : (side + 1) * LANES]
            left = jnp.where(small_lane < fold_size, even, pltpu.roll(odd, fold_size, axis=1))
            right = jnp.where(small_lane < fold_size, pltpu.roll(even, fold_size, axis=1), odd)
            spot = (series + 2 * side) * POWER_PITCH
            powers[spot : spot + half // 2, :] = left
            powers[spot + POWER_PITCH : spot + POWER_PITCH + half // 2, :] = right
    for block in range(0, held, GROUP):
        for tile in range(half // 2):
            out_ref[block : block + GROUP, tile * LANES : (tile + 1) * LANES] = powers[
                pl.ds(block * POWER_PITCH + tile, GROUP, stride=POWER_PITCH), :
            ]


def in_place(*operands):
    return [pltpu.with_memory_space_constraint(operand, pltpu.HBM) for operand in operands]


def local_sliced(samples, channel_order, merge_table):
    owners = lax.axis_size("sub")
    window, channels = samples.shape
    levels, _, rows = merge_table.shape
    held = rows // owners
    length = owners * (window - held)
    fold_size = length // LANES
    whole = window + rows
    order = channel_order.reshape(1, channels)
    first_table, twist, third_table = transform_tables(fold_size, length)
    return pl.pallas_call(
        functools.partial(merge_kernel, owners, length),
        out_shape=pltpu.VMEM((held, 64 * fold_size), jnp.float32),
        in_specs=[pl.BlockSpec(memory_space=pl.ANY)] * 6,
        out_specs=pl.BlockSpec(memory_space=pltpu.VMEM),
        scratch_shapes=[
            pltpu.VMEM((1, channels), jnp.int32),
            pltpu.VMEM((levels, 3, rows), jnp.int32),
            pltpu.VMEM((window, channels), jnp.bfloat16),
            pltpu.VMEM(first_table.shape, jnp.bfloat16),
            pltpu.VMEM(twist.shape, jnp.float32),
            pltpu.VMEM(third_table.shape, jnp.bfloat16),
            pltpu.VMEM((channels, channels), jnp.bfloat16),
            pltpu.VMEM((channels, channels), jnp.bfloat16),
            pltpu.VMEM((levels - 1, 2, rows // 2, rows), jnp.bfloat16),
            pltpu.VMEM((window, channels), jnp.float32),
            [pltpu.VMEM((2, whole, rows), jnp.float32)] * (levels - 1),
            [pltpu.VMEM((whole, rows), jnp.bfloat16)] * levels,
            pltpu.VMEM((rows, rows), jnp.bfloat16),
            pltpu.VMEM((rows, rows), jnp.bfloat16),
            pltpu.VMEM((owners, 2 * held, LANES), jnp.bfloat16),
            pltpu.VMEM((owners, 3 * held, LANES), jnp.bfloat16),
            pltpu.VMEM((owners, 2 * held, LANES), jnp.bfloat16),
            pltpu.VMEM((owners, 3 * held, LANES), jnp.bfloat16),
            pltpu.VMEM((FOLD_PITCH * fold_size, LANES), jnp.float32),
            pltpu.VMEM((held * fold_size, 2 * LANES), jnp.bfloat16),
            pltpu.VMEM((POWER_PITCH * held, LANES), jnp.float32),
            pltpu.SemaphoreType.DMA((4,)),
            pltpu.SemaphoreType.DMA((4,)),
            pltpu.SemaphoreType.DMA((6,)),
        ],
        compiler_params=pltpu.CompilerParams(
            vmem_limit_bytes=40 * 1024 * 1024, collective_id=0, has_side_effects=True
        ),
        name="merge_rows",
    )(*in_place(order, merge_table, samples, first_table, twist, third_table))


def is_sliced(window, channels, owners, rows, levels):
    held = rows // owners
    length = owners * (window - held)
    return (
        held == 16
        and window % 16 == 0
        and rows == 2 * LANES
        and channels == 2 * rows
        and rows == 2 ** (levels - 1)
        and length == 64 * LANES
        and window == 2 * rows + 16
        and owners == 16
    )


def local_any(samples, channel_order, merge_table):
    window, channels = samples.shape
    levels, _, rows = merge_table.shape
    if is_sliced(window, channels, lax.axis_size("sub"), rows, levels):
        return local_sliced(samples, channel_order, merge_table)
    return local(samples, channel_order, merge_table)


def solution(mesh):
    in_specs = (P(("groups", "sub"), None), P(), P())
    out_specs = P(("groups", "sub"), None)
    return jax.shard_map(local_any, mesh=mesh, in_specs=in_specs, out_specs=out_specs, check_vma=False)
```

```python
import functools
import math

import jax
import jax.numpy as jnp
import numpy as np
from jax import lax
from jax.experimental import pallas as pl
from jax.experimental.pallas import tpu as pltpu
from jax.sharding import PartitionSpec as P

LOCAL = 5
MESH = pl.DeviceIdType.MESH
CH_DEV = 32
SAMPLES = 8192


def from_partner(block, axis, apart):
    count = lax.axis_size(axis)
    route = []
    for low in range(count):
        high = low | 1 << apart
        if high != low and high < count:
            route += [(low, high), (high, low)]
    return lax.ppermute(block, axis, route)


def delay_rows(values, shifts, margin, time_axis):
    length = values.shape[time_axis]
    moved = values
    for bit_num in range(max(1, margin.bit_length())):
        offset = 2**bit_num
        rolled = jnp.pad(moved[:, offset:], ((0, 0), (0, offset)))
        flagged = shifts >> bit_num & 1 == 1
        flagged = flagged[:, None]
        moved = jnp.where(flagged, rolled, moved)
    return moved


def merge_level(current, entries, child_rows, span_rows, time_axis):
    outputs = jnp.arange(entries.shape[1], dtype=jnp.int32)
    starts = 2 * child_rows * (outputs // span_rows)
    lower_rows = jnp.take(current, starts + entries[0], axis=1 - time_axis)
    upper_rows = jnp.take(current, starts + child_rows + entries[1], axis=1 - time_axis)
    moved_rows = delay_rows(upper_rows, entries[2], child_rows, time_axis)
    return (lower_rows.astype(jnp.float32) + moved_rows.astype(jnp.float32)).astype(jnp.bfloat16)


def spectrum(delays, channels):
    row_count = delays.shape[0]
    length = delays.shape[1]
    fold_size = length // 128
    first_index = jnp.arange(fold_size, dtype=jnp.int32)
    lane_index = jnp.arange(128, dtype=jnp.int32)
    half_index = jnp.arange(64, dtype=jnp.int32)
    angle_one = (
        2.0
        * math.pi
        / fold_size
        * (first_index[:, None] * first_index[None, :] % fold_size).astype(jnp.float32)
    )
    cos_one = jnp.cos(angle_one).astype(jnp.bfloat16)
    sin_one = jnp.sin(angle_one).astype(jnp.bfloat16)
    angle_two = (
        2.0
        * math.pi
        / length
        * (first_index[:, None] * lane_index[None, :] % length).astype(jnp.float32)
    )
    twist_cos = jnp.cos(angle_two)
    twist_sin = jnp.sin(angle_two)
    angle_three = (
        2.0 * math.pi / 128 * (lane_index[:, None] * half_index[None, :] % 128).astype(jnp.float32)
    )
    cos_three = jnp.cos(angle_three).astype(jnp.bfloat16)
    sin_three = jnp.sin(angle_three).astype(jnp.bfloat16)
    series = delays.reshape(row_count, fold_size, 128)
    first_re = jnp.einsum("kn,rnm->rkm", cos_one, series, preferred_element_type=jnp.float32)
    first_im = -jnp.einsum("kn,rnm->rkm", sin_one, series, preferred_element_type=jnp.float32)
    twisted_re = (first_re * twist_cos + first_im * twist_sin).astype(jnp.bfloat16)
    twisted_im = (first_im * twist_cos - first_re * twist_sin).astype(jnp.bfloat16)
    out_re = jnp.einsum(
        "rkn,nj->rjk", twisted_re, cos_three, preferred_element_type=jnp.float32
    ) + jnp.einsum("rkn,nj->rjk", twisted_im, sin_three, preferred_element_type=jnp.float32)
    out_im = jnp.einsum(
        "rkn,nj->rjk", twisted_im, cos_three, preferred_element_type=jnp.float32
    ) - jnp.einsum("rkn,nj->rjk", twisted_re, sin_three, preferred_element_type=jnp.float32)
    power = (out_re * out_re + out_im * out_im) / (length * channels)
    return power.reshape(row_count, 64 * fold_size)


def local(samples, channel_order, merge_table):
    owners = lax.axis_size("sub")
    owner_index = lax.axis_index("sub")
    owned_rows = CH_DEV // 2
    quarter = CH_DEV // 4
    window = samples.shape[0]
    channels = samples.shape[1]
    ordered = jnp.take(samples, channel_order, axis=1).T.reshape(owners, CH_DEV, window)
    current = lax.all_to_all(ordered, "sub", split_axis=0, concat_axis=2, tiled=True).reshape(
        CH_DEV, window * owners
    )
    for level_num in range(1, LOCAL + 1):
        entries = lax.dynamic_slice_in_dim(
            merge_table[level_num - 1], owner_index * owned_rows, owned_rows, 1
        )
        current = merge_level(
            current, entries, max(1, 2 ** (level_num - 2)), 2 ** (level_num - 1), 1
        )
    block_index = jnp.zeros((), jnp.int32)
    for bit_num in range(owners.bit_length() - 1):
        level_num = LOCAL + bit_num + 1
        half_bit = owner_index >> bit_num & 1
        block_index = block_index * 2 + half_bit
        span_rows = owned_rows * 2 ** (bit_num + 1)
        child_rows = span_rows // 2
        subband = owner_index >> bit_num + 1
        entries = lax.dynamic_slice_in_dim(
            merge_table[level_num - 1],
            subband * span_rows + owned_rows * block_index,
            owned_rows,
            1,
        )
        kept_rows = lax.dynamic_slice_in_dim(current, half_bit * quarter, quarter, 0)
        sent_rows = lax.dynamic_slice_in_dim(current, (1 - half_bit) * quarter, quarter, 0)
        partner = from_partner(sent_rows, "sub", bit_num)
        row_base = quarter * block_index
        is_low = half_bit == 0
        lower_part = jnp.where(is_low, kept_rows, partner)
        upper_part = jnp.where(is_low, partner, kept_rows)
        lower_rows = jnp.take(lower_part, entries[0] - row_base, axis=0)
        upper_rows = jnp.take(upper_part, entries[1] - row_base, axis=0)
        moved_rows = delay_rows(upper_rows, entries[2], child_rows, 1)
        current = (lower_rows.astype(jnp.float32) + moved_rows.astype(jnp.float32)).astype(
            jnp.bfloat16
        )
    return spectrum(current[:, :SAMPLES], channels)


LANES = 128
GROUP = 8
FOLD_PITCH = 24
POWER_PITCH = 40


def widest_shift(level_num):
    return max(1, 2 ** (level_num - 2))


def still_to_come(level_num, levels):
    return sum(widest_shift(later) for later in range(level_num + 1, levels + 1))


def gathered(values, places, axis):
    other = 1 - axis
    numbers = lax.GatherDimensionNumbers(
        offset_dims=(),
        collapsed_slice_dims=(axis,),
        start_index_map=(axis,),
        operand_batching_dims=(other,),
        start_indices_batching_dims=(other,),
    )
    return lax.gather(
        values,
        places[..., None],
        numbers,
        slice_sizes=(1, 1),
        mode=lax.GatherScatterMode.PROMISE_IN_BOUNDS,
    )


def transform_tables(fold_size, length):
    first_index = np.arange(fold_size)
    lane_index = np.arange(LANES)
    half_index = np.concatenate([np.arange(0, 64, 2), np.arange(1, 64, 2)])
    unit = np.float32(2.0 * math.pi)

    def angles(left, right, period):
        turns = (left[:, None] * right[None, :]) % period
        return (unit / np.float32(period)) * turns.astype(np.float32)

    one = angles(first_index, first_index, fold_size)
    first_table = np.concatenate([np.cos(one), -np.sin(one)], axis=0)
    two = angles(first_index, lane_index, length)
    twist = np.stack([np.cos(two), np.sin(two)])
    three = angles(half_index, lane_index, LANES)
    cos_three, sin_three = np.cos(three), np.sin(three)
    third_table = np.concatenate(
        [
            np.concatenate([cos_three, sin_three], axis=1),
            np.concatenate([-sin_three, cos_three], axis=1),
        ],
        axis=0,
    )
    return (
        jnp.asarray(first_table, jnp.bfloat16),
        jnp.asarray(twist, jnp.float32),
        jnp.asarray(third_table, jnp.bfloat16),
    )


def one_hot(row_index, depth):
    rows = lax.broadcasted_iota(jnp.int32, (depth, row_index.shape[1]), 0)
    return (rows == row_index).astype(jnp.float32).astype(jnp.bfloat16)


def one_hot_fast(row_index, depth):
    count = row_index.shape[1]
    stripes = []
    for base in range(0, depth, 2 * LANES):
        size = min(2 * LANES, depth - base)
        rows = lax.broadcasted_iota(jnp.int32, (size, LANES), 0).astype(jnp.float32)
        rows = rows.astype(jnp.bfloat16)
        wanted = jnp.broadcast_to((row_index - base).astype(jnp.float32), (16, count))
        wanted = wanted.astype(jnp.bfloat16)
        one, zero = jnp.ones((size, LANES), jnp.bfloat16), jnp.zeros((size, LANES), jnp.bfloat16)
        stripes.append(
            jnp.concatenate(
                [
                    jnp.where(
                        rows
                        == jnp.concatenate([wanted[:, at : at + LANES]] * (size // 16), axis=0),
                        one,
                        zero,
                    )
                    for at in range(0, count, LANES)
                ],
                axis=1,
            )
        )
    return stripes[0] if len(stripes) == 1 else jnp.concatenate(stripes, axis=0)


def floor_16(count):
    return count // 16 * 16


def ceil_16(count):
    return -(-count // 16) * 16


def merge_kernel(
    owners,
    length,
    order_hbm,
    table_hbm,
    own_hbm,
    first_hbm,
    twist_hbm,
    third_hbm,
    out_ref,
    order_ref,
    table_ref,
    own_ref,
    first_ref,
    twist_ref,
    third_ref,
    split,
    choose,
    choices,
    first_picked,
    picked,
    tables,
    halo_out,
    placed,
    early_out,
    late_out,
    early_in,
    late_in,
    folded,
    twisted,
    powers,
    halo_sem,
    exchange_sem,
    load_sem,
):
    levels, _, rows = table_ref.shape
    window, channels = own_ref.shape
    held = rows // owners
    fold_size = length // LANES
    me = lax.axis_index("sub")
    bits = owners.bit_length() - 1

    loads = [
        pltpu.make_async_copy(source, target, load_sem.at[place])
        for place, (source, target) in enumerate(
            [
                (order_hbm, order_ref),
                (table_hbm, table_ref),
                (own_hbm, own_ref),
                (first_hbm, first_ref),
                (twist_hbm, twist_ref),
                (third_hbm, third_ref),
            ]
        )
    ]
    for load in loads:
        load.start()
    barrier = pltpu.get_barrier_semaphore()
    column = lax.broadcasted_iota(jnp.int32, (1, channels), 1)
    paired = jnp.where(column < rows, 2 * column, 2 * (column - rows) + 1)
    stripe = channels // owners
    for apart in range(owners):
        if apart:
            far = owners // 2 + (apart // 2 if apart % 2 else -(apart // 2))
            pl.semaphore_signal(
                barrier,
                inc=1,
                device_id={"sub": lax.rem(me + far, owners)},
                device_id_type=MESH,
            )
        split[apart * stripe : (apart + 1) * stripe, :] = one_hot_fast(paired - apart * stripe, stripe)
    half_rows = rows // 2

    @pl.when(me == owners - 1)
    def _():
        tables[0][window:, :] = jnp.zeros((rows, rows), jnp.bfloat16)

    loads[0].wait()
    order = jnp.broadcast_to(order_ref[...], (16, channels))
    side = lax.broadcasted_iota(jnp.int32, (16, channels), 0)
    digits = jnp.where(side == 0, order >> 6, order & 63).astype(jnp.float32)
    digits = jnp.dot(
        digits.astype(jnp.bfloat16), split[...], preferred_element_type=jnp.float32
    ).astype(jnp.int32)
    choose[...] = one_hot_fast(digits[0:1] * 64 + digits[1:2], channels)

    lane = lax.broadcasted_iota(jnp.int32, (1, LANES), 1)
    sublane = lax.broadcasted_iota(jnp.int32, (GROUP, LANES), 0)

    def combine(level_num, half, begin, end, lower_ref, upper_ref, given):
        span_rows = 2 ** (level_num - 1)
        base = half * half_rows
        count = (end - begin) // GROUP
        place = (lane + base) % span_rows // 16
        static = base % span_rows // 16
        amount = table_ref[level_num - 1][2:3, base : base + half_rows]
        reach = sublane + (amount - GROUP * place)
        inside = reach < GROUP
        turn = reach & (GROUP - 1)
        steps = max(0, min(span_rows, half_rows).bit_length() - 5)
        top = end + GROUP + GROUP * (static + 2**steps - 1)
        bottom = begin + GROUP * static
        upper = upper_ref[bottom : min(top, given), :]
        if top > given:
            filler = jnp.zeros((top - given, half_rows), jnp.float32)
            upper = jnp.concatenate([upper, filler], axis=0)
        for step in range(steps):
            offset = GROUP * 2**step
            flagged = (place - static) >> step & 1 == 1
            size = upper.shape[0]
            flagged = jnp.broadcast_to(flagged, (size - offset, half_rows))
            upper = jnp.where(flagged, upper[offset:], upper[: size - offset])
        spun = [
            gathered(upper[GROUP * part : GROUP * (part + 1)], turn, 0) for part in range(count + 1)
        ]
        moved = [jnp.where(inside, spun[part], spun[part + 1]) for part in range(count)]
        return lower_ref[begin:end, :] + jnp.concatenate(moved, axis=0)

    def combine_first(half, begin, end, given):
        at = half * half_rows
        return combine(
            1,
            half,
            begin,
            end,
            first_picked.at[:, at : at + half_rows],
            first_picked.at[:, rows + at : rows + at + half_rows],
            given,
        )

    loads[1].wait()
    lanes = lax.broadcasted_iota(jnp.int32, (1, rows), 1)

    def prepare(level_num):
        child_rows = widest_shift(level_num)
        entries = table_ref[level_num - 1]
        if level_num == levels:
            choices[level_num - 2, 0] = one_hot(entries[0:1], half_rows)
            choices[level_num - 2, 1] = one_hot(entries[1:2], half_rows)
            return
        starts = 2 * child_rows * (lanes >> (level_num - 1))
        lower = starts + entries[0:1]
        upper = starts + child_rows + entries[1:2]
        for half in range(2):
            at = half * half_rows
            choices[level_num - 2, half, :, 0:half_rows] = one_hot(
                lower[:, at : at + half_rows] - at, half_rows
            )
            choices[level_num - 2, half, :, half_rows:] = one_hot(
                upper[:, at : at + half_rows] - at, half_rows
            )

    for level_num in range(2, levels + 1):
        prepare(level_num)

    loads[2].wait()
    ahead = ceil_16(rows + GROUP)
    first_picked[0:ahead, :] = jnp.dot(
        own_ref[0:ahead, :], choose[...], preferred_element_type=jnp.float32
    )
    last_row = lax.broadcasted_iota(jnp.int32, (16, half_rows), 0) == 15
    for part in range(2):
        values = combine_first(part, 0, rows, ahead)
        at = part * half_rows
        tables[0][0:rows, at : at + half_rows] = values.astype(jnp.bfloat16)
        top = (part + 1) * half_rows
        halo_out[0 : top - 16, at : at + half_rows] = values[0 : top - 16].astype(jnp.bfloat16)
        edge = jnp.broadcast_to(first_picked[0:1, rows + at : rows + at + half_rows], (16, half_rows))
        halo_out[top - 16 : top, at : at + half_rows] = jnp.where(
            last_row, edge, values[top - 16 : top]
        ).astype(jnp.bfloat16)

    first_picked[ahead:window, :] = jnp.dot(
        own_ref[ahead:window, :], choose[...], preferred_element_type=jnp.float32
    )
    for part in range(2):
        values = combine_first(part, rows, window, window)
        at = part * half_rows
        tables[0][rows:window, at : at + half_rows] = values.astype(jnp.bfloat16)

    def advance(level_num, half, source_begin, source_end):
        at = half * half_rows
        picked[level_num - 2][half, source_begin:source_end, :] = jnp.dot(
            tables[level_num - 2][source_begin:source_end, at : at + half_rows],
            choices[level_num - 2, half],
            preferred_element_type=jnp.float32,
        )

    def finish(level_num, half, begin, end, given):
        at = half * half_rows
        lower, upper = (0, 1) if level_num == levels else (half, half)
        low_at, high_at = (at, at) if level_num == levels else (0, half_rows)
        tables[level_num - 1][begin:end, at : at + half_rows] = combine(
            level_num,
            half,
            begin,
            end,
            picked[level_num - 2].at[lower, :, low_at : low_at + half_rows],
            picked[level_num - 2].at[upper, :, high_at : high_at + half_rows],
            given,
        ).astype(jnp.bfloat16)

    def needed(level_num, half, edge):
        lag = 0 if half or level_num == levels else half_rows
        return edge + still_to_come(level_num, levels) - lag

    early = rows
    pl.semaphore_wait(barrier, owners - 1)
    backs = [
        pltpu.make_async_remote_copy(
            src_ref=halo_out.at[0:count, first : first + half_rows],
            dst_ref=tables[0].at[window : window + count, first : first + half_rows],
            send_sem=halo_sem.at[part],
            recv_sem=halo_sem.at[2 + part],
            device_id={"sub": lax.rem(me + owners - 1, owners)},
            device_id_type=MESH,
        )
        for part, (count, first) in enumerate(((rows, half_rows), (half_rows, 0)))
    ]

    @pl.when(me > 0)
    def _():
        for back in backs:
            back.start()

    for level_num in range(2, levels + 1):
        ends = [ceil_16(needed(level_num - 1, half, early)) for half in range(2)]
        for half in range(2):
            advance(level_num, half, 0, ends[half])
        for half in range(2):
            given = ends[1] if level_num == levels else ends[half]
            finish(level_num, half, 0, ceil_16(needed(level_num, half, early)), given)

    spots = lax.broadcasted_iota(jnp.int32, (rows, rows), 0)
    shift = held.bit_length() - 1
    wanted = jnp.zeros_like(spots)
    for bit_num in range(bits):
        wanted = wanted | ((spots >> (shift + bit_num) & 1) << (bits - 1 - bit_num))
    wanted = (wanted << shift) + (spots & (held - 1))
    placed[...] = (
        (lax.broadcasted_iota(jnp.int32, (rows, rows), 1) == wanted)
        .astype(jnp.float32)
        .astype(jnp.bfloat16)
    )

    def turn_over(values):
        return lax.dot_general(
            placed[...],
            values,
            (((1,), (1,)), ((), ())),
            preferred_element_type=jnp.float32,
        )

    def put_blocks(target, begin):
        blocks = turn_over(tables[levels - 1][begin : begin + rows, :]).astype(jnp.bfloat16)
        for tile in range(rows // LANES):
            for owner in range(owners):
                target[owner, tile * held : (tile + 1) * held, :] = blocks[
                    owner * held : (owner + 1) * held, tile * LANES : (tile + 1) * LANES
                ]

    def spread(source, target, size, send_sem, recv_sem):
        for apart in range(1, owners):
            to = lax.rem(me + apart, owners)
            pltpu.make_async_remote_copy(
                src_ref=source.at[to, 0:size],
                dst_ref=target.at[me, 0:size],
                send_sem=send_sem,
                recv_sem=recv_sem,
                device_id={"sub": to},
                device_id_type=MESH,
            ).start()
        target[me] = source[me]
        return pltpu.make_async_remote_copy(
            src_ref=source.at[1:owners, 0:size],
            dst_ref=target.at[1:owners, 0:size],
            send_sem=send_sem,
            recv_sem=recv_sem,
            device_id={"sub": lax.rem(me + 1, owners)},
            device_id_type=MESH,
        )

    put_blocks(early_out, 0)
    early_blocks = spread(early_out, early_in, 2 * held, exchange_sem.at[0], exchange_sem.at[1])

    @pl.when(me < owners - 1)
    def _():
        for back in backs:
            back.wait_recv()

    @pl.when(me > 0)
    def _():
        for back in backs:
            back.wait_send()

    for part in range(2):
        at = part * half_rows
        top = window + (part + 1) * half_rows
        fill = tables[0][window - 16 : window, at : at + half_rows].astype(jnp.float32)
        edge = tables[0][top - 16 : top, at : at + half_rows].astype(jnp.float32)[15:16]
        amount = table_ref[0][2:3, at : at + half_rows]
        late_edge = last_row & jnp.broadcast_to(amount > 0, (16, half_rows))
        fill = fill + jnp.where(late_edge, jnp.broadcast_to(edge, (16, half_rows)), 0.0)
        tables[0][window - 16 : window, at : at + half_rows] = fill.astype(jnp.bfloat16)
    for level_num in range(2, levels + 1):
        begins = [floor_16(needed(level_num - 1, half, early)) for half in range(2)]
        ends = [ceil_16(needed(level_num - 1, half, window)) for half in range(2)]
        for half in range(2):
            advance(level_num, half, begins[half], ends[half])
        for half in range(2):
            given = ends[1] if level_num == levels else ends[half]
            finish(
                level_num,
                half,
                floor_16(needed(level_num, half, early)),
                ceil_16(needed(level_num, half, window)),
                given,
            )
    put_blocks(late_out, early)
    rest = window - 2 * rows
    tail = tables[levels - 1][2 * rows : window, :]
    tail = turn_over(jnp.concatenate([tail] * (LANES // rest), axis=0))
    row_spot = lax.broadcasted_iota(jnp.int32, (rows, LANES), 0)
    turned = window * me // rest % (LANES // rest)
    lane_spot = lax.broadcasted_iota(jnp.int32, (rows, LANES), 1) // rest
    tail = jnp.where((row_spot + lane_spot) % (LANES // rest) == turned, tail, 0.0).astype(jnp.bfloat16)
    packed_rows = rows * rest // LANES
    gather_rows = (
        lax.broadcasted_iota(jnp.int32, (packed_rows, rows), 1) // (LANES // rest)
        == lax.broadcasted_iota(jnp.int32, (packed_rows, rows), 0)
    )
    tail = jnp.dot(
        gather_rows.astype(jnp.float32).astype(jnp.bfloat16),
        tail,
        preferred_element_type=jnp.float32,
    ).astype(jnp.bfloat16)
    extra = packed_rows // owners
    for owner in range(owners):
        late_out[owner, 2 * held : 2 * held + extra, :] = tail[
            owner * extra : (owner + 1) * extra
        ]
    late_blocks = spread(late_out, late_in, 2 * held + extra, exchange_sem.at[2], exchange_sem.at[3])

    wide_lane = lax.broadcasted_iota(jnp.int32, (held, LANES), 1)
    pieces = [[] for _ in range(fold_size)]
    for source in range(owners):
        for at in range(0, window, LANES):
            fold, part = divmod(window * source + at, LANES)
            count = min(LANES, window - at)
            for where, low, high in (
                (fold, part, min(LANES, part + count)),
                (fold + 1, 0, part + count - LANES),
            ):
                if where < fold_size and low < high:
                    pieces[where].append((low, high, source, at >= early, at, part))
    rolled = {}

    def rolled_tile(source, late, at, part):
        if (source, at) not in rolled:
            if at < 2 * rows:
                place = (at - early if late else at) // LANES * held
                value = (late_in if late else early_in)[source, place : place + held, :]
                value = value.astype(jnp.float32)
                if part:
                    value = pltpu.roll(value, part, axis=1)
            else:
                value = late_in[source, 2 * held : 3 * held, :].astype(jnp.float32)
                value = jnp.concatenate(
                    [
                        pltpu.roll(
                            jnp.broadcast_to(value[row : row + 1], (LANES // rest, LANES)),
                            0,
                            axis=1,
                            stride=rest,
                            stride_axis=0,
                        )
                        for row in range(extra)
                    ],
                    axis=0,
                )
            rolled[source, at] = value
        return rolled[source, at]

    def assemble(which):
        for fold in range(fold_size):
            some = [piece for piece in sorted(pieces[fold]) if piece[3] == which]
            if not some:
                continue
            where = slice(fold * FOLD_PITCH, fold * FOLD_PITCH + held)
            value = None
            if which and len(some) < len(pieces[fold]):
                value = folded[where, :]
            for low, high, source, late, at, part in some:
                piece = rolled_tile(source, late, at, part)
                if value is None:
                    value = piece
                elif high == LANES:
                    value = jnp.where(wide_lane < low, value, piece)
                elif low == 0:
                    value = jnp.where(wide_lane < high, piece, value)
                else:
                    value = jnp.where((wide_lane >= low) & (wide_lane < high), piece, value)
            folded[where, :] = value

    early_blocks.wait_recv()
    assemble(False)
    for load in loads[3:]:
        load.wait()
    late_blocks.wait_recv()

    assemble(True)

    cosine, sine = twist_ref[0], twist_ref[1]
    for series in range(0, held, 2):
        pair = jnp.concatenate(
            [folded[pl.ds(series + side, fold_size, stride=FOLD_PITCH), :] for side in range(2)], axis=1
        )
        spun = jnp.dot(
            first_ref[...], pair.astype(jnp.bfloat16), preferred_element_type=jnp.float32
        )
        for side in range(2):
            real = spun[0:fold_size, side * LANES : (side + 1) * LANES]
            imag = spun[fold_size:, side * LANES : (side + 1) * LANES]
            at = (series + side) * fold_size
            twisted[at : at + fold_size, 0:LANES] = (real * cosine + imag * sine).astype(
                jnp.bfloat16
            )
            twisted[at : at + fold_size, LANES:] = (imag * cosine - real * sine).astype(
                jnp.bfloat16
            )
    half = fold_size
    scale = 1.0 / (length * channels)
    small_lane = lax.broadcasted_iota(jnp.int32, (half // 2, LANES), 1)
    for series in range(0, held, 4):
        at = series * fold_size
        waves = lax.dot_general(
            third_ref[...],
            twisted[at : at + 4 * fold_size, :],
            (((1,), (1,)), ((), ())),
            preferred_element_type=jnp.float32,
        )
        power = (waves[0:half] * waves[0:half] + waves[half:] * waves[half:]) * scale
        for side in range(2):
            even = power[0 : half // 2, side * LANES : (side + 1) * LANES]
            odd = power[half // 2 :, side * LANES : (side + 1) * LANES]
            left = jnp.where(small_lane < fold_size, even, pltpu.roll(odd, fold_size, axis=1))
            right = jnp.where(small_lane < fold_size, pltpu.roll(even, fold_size, axis=1), odd)
            spot = (series + 2 * side) * POWER_PITCH
            powers[spot : spot + half // 2, :] = left
            powers[spot + POWER_PITCH : spot + POWER_PITCH + half // 2, :] = right
    for block in range(0, held, GROUP):
        for tile in range(half // 2):
            out_ref[block : block + GROUP, tile * LANES : (tile + 1) * LANES] = powers[
                pl.ds(block * POWER_PITCH + tile, GROUP, stride=POWER_PITCH), :
            ]
    early_blocks.wait_send()
    late_blocks.wait_send()


def in_place(*operands):
    return [pltpu.with_memory_space_constraint(operand, pltpu.HBM) for operand in operands]


def local_sliced(samples, channel_order, merge_table):
    owners = lax.axis_size("sub")
    window, channels = samples.shape
    levels, _, rows = merge_table.shape
    held = rows // owners
    length = owners * (window - held)
    fold_size = length // LANES
    whole = window + rows
    order = channel_order.reshape(1, channels)
    first_table, twist, third_table = transform_tables(fold_size, length)
    return pl.pallas_call(
        functools.partial(merge_kernel, owners, length),
        out_shape=pltpu.VMEM((held, 64 * fold_size), jnp.float32),
        in_specs=[pl.BlockSpec(memory_space=pl.ANY)] * 6,
        out_specs=pl.BlockSpec(memory_space=pltpu.VMEM),
        scratch_shapes=[
            pltpu.VMEM((1, channels), jnp.int32),
            pltpu.VMEM((levels, 3, rows), jnp.int32),
            pltpu.VMEM((window, channels), jnp.bfloat16),
            pltpu.VMEM(first_table.shape, jnp.bfloat16),
            pltpu.VMEM(twist.shape, jnp.float32),
            pltpu.VMEM(third_table.shape, jnp.bfloat16),
            pltpu.VMEM((channels, channels), jnp.bfloat16),
            pltpu.VMEM((channels, channels), jnp.bfloat16),
            pltpu.VMEM((levels - 1, 2, rows // 2, rows), jnp.bfloat16),
            pltpu.VMEM((window, channels), jnp.float32),
            [pltpu.VMEM((2, whole, rows), jnp.float32)] * (levels - 1),
            [pltpu.VMEM((whole, rows), jnp.bfloat16)] * levels,
            pltpu.VMEM((rows, rows), jnp.bfloat16),
            pltpu.VMEM((rows, rows), jnp.bfloat16),
            pltpu.VMEM((owners, 2 * held, LANES), jnp.bfloat16),
            pltpu.VMEM((owners, 3 * held, LANES), jnp.bfloat16),
            pltpu.VMEM((owners, 2 * held, LANES), jnp.bfloat16),
            pltpu.VMEM((owners, 3 * held, LANES), jnp.bfloat16),
            pltpu.VMEM((FOLD_PITCH * fold_size, LANES), jnp.float32),
            pltpu.VMEM((held * fold_size, 2 * LANES), jnp.bfloat16),
            pltpu.VMEM((POWER_PITCH * held, LANES), jnp.float32),
            pltpu.SemaphoreType.DMA((4,)),
            pltpu.SemaphoreType.DMA((4,)),
            pltpu.SemaphoreType.DMA((6,)),
        ],
        compiler_params=pltpu.CompilerParams(
            vmem_limit_bytes=40 * 1024 * 1024, collective_id=0, has_side_effects=True
        ),
        name="merge_rows",
    )(*in_place(order, merge_table, samples, first_table, twist, third_table))


def is_sliced(window, channels, owners, rows, levels):
    held = rows // owners
    length = owners * (window - held)
    return (
        held == 16
        and window % 16 == 0
        and rows == 2 * LANES
        and channels == 2 * rows
        and rows == 2 ** (levels - 1)
        and length == 64 * LANES
        and window == 2 * rows + 16
        and owners == 16
    )


def local_any(samples, channel_order, merge_table):
    window, channels = samples.shape
    levels, _, rows = merge_table.shape
    if is_sliced(window, channels, lax.axis_size("sub"), rows, levels):
        return local_sliced(samples, channel_order, merge_table)
    return local(samples, channel_order, merge_table)


def solution(mesh):
    in_specs = (P(("groups", "sub"), None), P(), P())
    out_specs = P(("groups", "sub"), None)
    return jax.shard_map(local_any, mesh=mesh, in_specs=in_specs, out_specs=out_specs, check_vma=False)
```

```python
import functools
import math

import jax
import jax.numpy as jnp
import numpy as np
from jax import lax
from jax.experimental import pallas as pl
from jax.experimental.pallas import tpu as pltpu
from jax.sharding import PartitionSpec as P

LOCAL = 5
MESH = pl.DeviceIdType.MESH
CH_DEV = 32
SAMPLES = 8192


def from_partner(block, axis, apart):
    count = lax.axis_size(axis)
    route = []
    for low in range(count):
        high = low | 1 << apart
        if high != low and high < count:
            route += [(low, high), (high, low)]
    return lax.ppermute(block, axis, route)


def delay_rows(values, shifts, margin, time_axis):
    length = values.shape[time_axis]
    moved = values
    for bit_num in range(max(1, margin.bit_length())):
        offset = 2**bit_num
        rolled = jnp.pad(moved[:, offset:], ((0, 0), (0, offset)))
        flagged = shifts >> bit_num & 1 == 1
        flagged = flagged[:, None]
        moved = jnp.where(flagged, rolled, moved)
    return moved


def merge_level(current, entries, child_rows, span_rows, time_axis):
    outputs = jnp.arange(entries.shape[1], dtype=jnp.int32)
    starts = 2 * child_rows * (outputs // span_rows)
    lower_rows = jnp.take(current, starts + entries[0], axis=1 - time_axis)
    upper_rows = jnp.take(current, starts + child_rows + entries[1], axis=1 - time_axis)
    moved_rows = delay_rows(upper_rows, entries[2], child_rows, time_axis)
    return (lower_rows.astype(jnp.float32) + moved_rows.astype(jnp.float32)).astype(jnp.bfloat16)


def spectrum(delays, channels):
    row_count = delays.shape[0]
    length = delays.shape[1]
    fold_size = length // 128
    first_index = jnp.arange(fold_size, dtype=jnp.int32)
    lane_index = jnp.arange(128, dtype=jnp.int32)
    half_index = jnp.arange(64, dtype=jnp.int32)
    angle_one = (
        2.0
        * math.pi
        / fold_size
        * (first_index[:, None] * first_index[None, :] % fold_size).astype(jnp.float32)
    )
    cos_one = jnp.cos(angle_one).astype(jnp.bfloat16)
    sin_one = jnp.sin(angle_one).astype(jnp.bfloat16)
    angle_two = (
        2.0
        * math.pi
        / length
        * (first_index[:, None] * lane_index[None, :] % length).astype(jnp.float32)
    )
    twist_cos = jnp.cos(angle_two)
    twist_sin = jnp.sin(angle_two)
    angle_three = (
        2.0 * math.pi / 128 * (lane_index[:, None] * half_index[None, :] % 128).astype(jnp.float32)
    )
    cos_three = jnp.cos(angle_three).astype(jnp.bfloat16)
    sin_three = jnp.sin(angle_three).astype(jnp.bfloat16)
    series = delays.reshape(row_count, fold_size, 128)
    first_re = jnp.einsum("kn,rnm->rkm", cos_one, series, preferred_element_type=jnp.float32)
    first_im = -jnp.einsum("kn,rnm->rkm", sin_one, series, preferred_element_type=jnp.float32)
    twisted_re = (first_re * twist_cos + first_im * twist_sin).astype(jnp.bfloat16)
    twisted_im = (first_im * twist_cos - first_re * twist_sin).astype(jnp.bfloat16)
    out_re = jnp.einsum(
        "rkn,nj->rjk", twisted_re, cos_three, preferred_element_type=jnp.float32
    ) + jnp.einsum("rkn,nj->rjk", twisted_im, sin_three, preferred_element_type=jnp.float32)
    out_im = jnp.einsum(
        "rkn,nj->rjk", twisted_im, cos_three, preferred_element_type=jnp.float32
    ) - jnp.einsum("rkn,nj->rjk", twisted_re, sin_three, preferred_element_type=jnp.float32)
    power = (out_re * out_re + out_im * out_im) / (length * channels)
    return power.reshape(row_count, 64 * fold_size)


def local(samples, channel_order, merge_table):
    owners = lax.axis_size("sub")
    owner_index = lax.axis_index("sub")
    owned_rows = CH_DEV // 2
    quarter = CH_DEV // 4
    window = samples.shape[0]
    channels = samples.shape[1]
    ordered = jnp.take(samples, channel_order, axis=1).T.reshape(owners, CH_DEV, window)
    current = lax.all_to_all(ordered, "sub", split_axis=0, concat_axis=2, tiled=True).reshape(
        CH_DEV, window * owners
    )
    for level_num in range(1, LOCAL + 1):
        entries = lax.dynamic_slice_in_dim(
            merge_table[level_num - 1], owner_index * owned_rows, owned_rows, 1
        )
        current = merge_level(
            current, entries, max(1, 2 ** (level_num - 2)), 2 ** (level_num - 1), 1
        )
    block_index = jnp.zeros((), jnp.int32)
    for bit_num in range(owners.bit_length() - 1):
        level_num = LOCAL + bit_num + 1
        half_bit = owner_index >> bit_num & 1
        block_index = block_index * 2 + half_bit
        span_rows = owned_rows * 2 ** (bit_num + 1)
        child_rows = span_rows // 2
        subband = owner_index >> bit_num + 1
        entries = lax.dynamic_slice_in_dim(
            merge_table[level_num - 1],
            subband * span_rows + owned_rows * block_index,
            owned_rows,
            1,
        )
        kept_rows = lax.dynamic_slice_in_dim(current, half_bit * quarter, quarter, 0)
        sent_rows = lax.dynamic_slice_in_dim(current, (1 - half_bit) * quarter, quarter, 0)
        partner = from_partner(sent_rows, "sub", bit_num)
        row_base = quarter * block_index
        is_low = half_bit == 0
        lower_part = jnp.where(is_low, kept_rows, partner)
        upper_part = jnp.where(is_low, partner, kept_rows)
        lower_rows = jnp.take(lower_part, entries[0] - row_base, axis=0)
        upper_rows = jnp.take(upper_part, entries[1] - row_base, axis=0)
        moved_rows = delay_rows(upper_rows, entries[2], child_rows, 1)
        current = (lower_rows.astype(jnp.float32) + moved_rows.astype(jnp.float32)).astype(
            jnp.bfloat16
        )
    return spectrum(current[:, :SAMPLES], channels)


LANES = 128
GROUP = 8
FOLD_PITCH = 24
POWER_PITCH = 40


def widest_shift(level_num):
    return max(1, 2 ** (level_num - 2))


def still_to_come(level_num, levels):
    return sum(widest_shift(later) for later in range(level_num + 1, levels + 1))


def gathered(values, places, axis):
    other = 1 - axis
    numbers = lax.GatherDimensionNumbers(
        offset_dims=(),
        collapsed_slice_dims=(axis,),
        start_index_map=(axis,),
        operand_batching_dims=(other,),
        start_indices_batching_dims=(other,),
    )
    return lax.gather(
        values,
        places[..., None],
        numbers,
        slice_sizes=(1, 1),
        mode=lax.GatherScatterMode.PROMISE_IN_BOUNDS,
    )


def transform_tables(fold_size, length):
    first_index = np.arange(fold_size)
    lane_index = np.arange(LANES)
    half_index = np.concatenate([np.arange(0, 64, 2), np.arange(1, 64, 2)])
    unit = np.float32(2.0 * math.pi)

    def angles(left, right, period):
        turns = (left[:, None] * right[None, :]) % period
        return (unit / np.float32(period)) * turns.astype(np.float32)

    one = angles(first_index, first_index, fold_size)
    first_table = np.concatenate([np.cos(one), -np.sin(one)], axis=0)
    two = angles(first_index, lane_index, length)
    twist = np.stack([np.cos(two), np.sin(two)])
    three = angles(half_index, lane_index, LANES)
    cos_three, sin_three = np.cos(three), np.sin(three)
    third_table = np.concatenate(
        [
            np.concatenate([cos_three, sin_three], axis=1),
            np.concatenate([-sin_three, cos_three], axis=1),
        ],
        axis=0,
    )
    return (
        jnp.asarray(first_table, jnp.bfloat16),
        jnp.asarray(twist, jnp.float32),
        jnp.asarray(third_table, jnp.bfloat16),
    )


def one_hot(row_index, depth):
    rows = lax.broadcasted_iota(jnp.int32, (depth, row_index.shape[1]), 0)
    return (rows == row_index).astype(jnp.float32).astype(jnp.bfloat16)


def floor_16(count):
    return count // 16 * 16


def ceil_16(count):
    return -(-count // 16) * 16


def merge_kernel(
    owners,
    length,
    order_hbm,
    table_hbm,
    own_hbm,
    first_hbm,
    twist_hbm,
    third_hbm,
    out_ref,
    order_ref,
    table_ref,
    own_ref,
    first_ref,
    twist_ref,
    third_ref,
    split,
    choose,
    choices,
    first_picked,
    picked,
    tables,
    halo_out,
    placed,
    early_out,
    late_out,
    early_in,
    late_in,
    folded,
    twisted,
    powers,
    halo_sem,
    exchange_sem,
    load_sem,
):
    levels, _, rows = table_ref.shape
    window, channels = own_ref.shape
    held = rows // owners
    fold_size = length // LANES
    me = lax.axis_index("sub")
    bits = owners.bit_length() - 1

    loads = [
        pltpu.make_async_copy(source, target, load_sem.at[place])
        for place, (source, target) in enumerate(
            [
                (order_hbm, order_ref),
                (table_hbm, table_ref),
                (own_hbm, own_ref),
                (first_hbm, first_ref),
                (twist_hbm, twist_ref),
                (third_hbm, third_ref),
            ]
        )
    ]
    for load in loads:
        load.start()
    barrier = pltpu.get_barrier_semaphore()
    column = lax.broadcasted_iota(jnp.int32, (1, channels), 1)
    paired = jnp.where(column < rows, 2 * column, 2 * (column - rows) + 1)
    stripe = channels // owners
    for apart in range(owners):
        if apart:
            far = owners // 2 + (apart // 2 if apart % 2 else -(apart // 2))
            pl.semaphore_signal(
                barrier,
                inc=1,
                device_id={"sub": lax.rem(me + far, owners)},
                device_id_type=MESH,
            )
        split[apart * stripe : (apart + 1) * stripe, :] = one_hot(paired - apart * stripe, stripe)
    half_rows = rows // 2

    @pl.when(me == owners - 1)
    def _():
        tables[0][window:, :] = jnp.zeros((rows, rows), jnp.bfloat16)

    loads[0].wait()
    order = jnp.broadcast_to(order_ref[...], (16, channels))
    side = lax.broadcasted_iota(jnp.int32, (16, channels), 0)
    digits = jnp.where(side == 0, order >> 6, order & 63).astype(jnp.float32)
    digits = jnp.dot(
        digits.astype(jnp.bfloat16), split[...], preferred_element_type=jnp.float32
    ).astype(jnp.int32)
    choose[...] = one_hot(digits[0:1] * 64 + digits[1:2], channels)

    lane = lax.broadcasted_iota(jnp.int32, (1, LANES), 1)
    sublane = lax.broadcasted_iota(jnp.int32, (GROUP, LANES), 0)

    def combine(level_num, half, begin, end, lower_ref, upper_ref, given):
        span_rows = 2 ** (level_num - 1)
        base = half * half_rows
        count = (end - begin) // GROUP
        place = (lane + base) % span_rows // 16
        static = base % span_rows // 16
        amount = table_ref[level_num - 1][2:3, base : base + half_rows]
        reach = sublane + (amount - GROUP * place)
        inside = reach < GROUP
        turn = reach & (GROUP - 1)
        steps = max(0, min(span_rows, half_rows).bit_length() - 5)
        top = end + GROUP + GROUP * (static + 2**steps - 1)
        bottom = begin + GROUP * static
        upper = upper_ref[bottom : min(top, given), :]
        if top > given:
            filler = jnp.zeros((top - given, half_rows), jnp.float32)
            upper = jnp.concatenate([upper, filler], axis=0)
        for step in range(steps):
            offset = GROUP * 2**step
            flagged = (place - static) >> step & 1 == 1
            size = upper.shape[0]
            flagged = jnp.broadcast_to(flagged, (size - offset, half_rows))
            upper = jnp.where(flagged, upper[offset:], upper[: size - offset])
        spun = [
            gathered(upper[GROUP * part : GROUP * (part + 1)], turn, 0) for part in range(count + 1)
        ]
        moved = [jnp.where(inside, spun[part], spun[part + 1]) for part in range(count)]
        return lower_ref[begin:end, :] + jnp.concatenate(moved, axis=0)

    def combine_first(half, begin, end, given):
        at = half * half_rows
        return combine(
            1,
            half,
            begin,
            end,
            first_picked.at[:, at : at + half_rows],
            first_picked.at[:, rows + at : rows + at + half_rows],
            given,
        )

    loads[1].wait()
    lanes = lax.broadcasted_iota(jnp.int32, (1, rows), 1)

    def prepare(level_num):
        child_rows = widest_shift(level_num)
        entries = table_ref[level_num - 1]
        if level_num == levels:
            choices[level_num - 2, 0] = one_hot(entries[0:1], half_rows)
            choices[level_num - 2, 1] = one_hot(entries[1:2], half_rows)
            return
        starts = 2 * child_rows * (lanes >> (level_num - 1))
        lower = starts + entries[0:1]
        upper = starts + child_rows + entries[1:2]
        for half in range(2):
            at = half * half_rows
            choices[level_num - 2, half, :, 0:half_rows] = one_hot(
                lower[:, at : at + half_rows] - at, half_rows
            )
            choices[level_num - 2, half, :, half_rows:] = one_hot(
                upper[:, at : at + half_rows] - at, half_rows
            )

    for level_num in range(2, levels + 1):
        prepare(level_num)

    loads[2].wait()
    ahead = ceil_16(rows + GROUP)
    first_picked[0:ahead, :] = jnp.dot(
        own_ref[0:ahead, :], choose[...], preferred_element_type=jnp.float32
    )
    last_row = lax.broadcasted_iota(jnp.int32, (16, half_rows), 0) == 15
    for part in range(2):
        values = combine_first(part, 0, rows, ahead)
        at = part * half_rows
        tables[0][0:rows, at : at + half_rows] = values.astype(jnp.bfloat16)
        top = (part + 1) * half_rows
        halo_out[0 : top - 16, at : at + half_rows] = values[0 : top - 16].astype(jnp.bfloat16)
        edge = jnp.broadcast_to(first_picked[0:1, rows + at : rows + at + half_rows], (16, half_rows))
        halo_out[top - 16 : top, at : at + half_rows] = jnp.where(
            last_row, edge, values[top - 16 : top]
        ).astype(jnp.bfloat16)

    first_picked[ahead:window, :] = jnp.dot(
        own_ref[ahead:window, :], choose[...], preferred_element_type=jnp.float32
    )
    for part in range(2):
        values = combine_first(part, rows, window, window)
        at = part * half_rows
        tables[0][rows:window, at : at + half_rows] = values.astype(jnp.bfloat16)

    def advance(level_num, half, source_begin, source_end):
        at = half * half_rows
        picked[level_num - 2][half, source_begin:source_end, :] = jnp.dot(
            tables[level_num - 2][source_begin:source_end, at : at + half_rows],
            choices[level_num - 2, half],
            preferred_element_type=jnp.float32,
        )

    def finish(level_num, half, begin, end, given):
        at = half * half_rows
        lower, upper = (0, 1) if level_num == levels else (half, half)
        low_at, high_at = (at, at) if level_num == levels else (0, half_rows)
        tables[level_num - 1][begin:end, at : at + half_rows] = combine(
            level_num,
            half,
            begin,
            end,
            picked[level_num - 2].at[lower, :, low_at : low_at + half_rows],
            picked[level_num - 2].at[upper, :, high_at : high_at + half_rows],
            given,
        ).astype(jnp.bfloat16)

    def needed(level_num, half, edge):
        lag = 0 if half or level_num == levels else half_rows
        return edge + still_to_come(level_num, levels) - lag

    early = rows
    pl.semaphore_wait(barrier, owners - 1)
    backs = [
        pltpu.make_async_remote_copy(
            src_ref=halo_out.at[0:count, first : first + half_rows],
            dst_ref=tables[0].at[window : window + count, first : first + half_rows],
            send_sem=halo_sem.at[part],
            recv_sem=halo_sem.at[2 + part],
            device_id={"sub": lax.rem(me + owners - 1, owners)},
            device_id_type=MESH,
        )
        for part, (count, first) in enumerate(((half_rows, 0), (rows, half_rows)))
    ]

    @pl.when(me > 0)
    def _():
        for back in backs:
            back.start()

    for level_num in range(2, levels + 1):
        ends = [ceil_16(needed(level_num - 1, half, early)) for half in range(2)]
        for half in range(2):
            advance(level_num, half, 0, ends[half])
        for half in range(2):
            given = ends[1] if level_num == levels else ends[half]
            finish(level_num, half, 0, ceil_16(needed(level_num, half, early)), given)

    spots = lax.broadcasted_iota(jnp.int32, (rows, rows), 0)
    shift = held.bit_length() - 1
    wanted = jnp.zeros_like(spots)
    for bit_num in range(bits):
        wanted = wanted | ((spots >> (shift + bit_num) & 1) << (bits - 1 - bit_num))
    wanted = (wanted << shift) + (spots & (held - 1))
    placed[...] = (
        (lax.broadcasted_iota(jnp.int32, (rows, rows), 1) == wanted)
        .astype(jnp.float32)
        .astype(jnp.bfloat16)
    )

    def turn_over(values):
        return lax.dot_general(
            placed[...],
            values,
            (((1,), (1,)), ((), ())),
            preferred_element_type=jnp.float32,
        )

    def put_blocks(target, begin):
        blocks = turn_over(tables[levels - 1][begin : begin + rows, :]).astype(jnp.bfloat16)
        for tile in range(rows // LANES):
            for owner in range(owners):
                target[owner, tile * held : (tile + 1) * held, :] = blocks[
                    owner * held : (owner + 1) * held, tile * LANES : (tile + 1) * LANES
                ]

    def spread(source, target, size, send_sem, recv_sem):
        for apart in range(1, owners):
            to = lax.rem(me + apart, owners)
            pltpu.make_async_remote_copy(
                src_ref=source.at[to, 0:size],
                dst_ref=target.at[me, 0:size],
                send_sem=send_sem,
                recv_sem=recv_sem,
                device_id={"sub": to},
                device_id_type=MESH,
            ).start()
        target[me] = source[me]
        return pltpu.make_async_remote_copy(
            src_ref=source.at[1:owners, 0:size],
            dst_ref=target.at[1:owners, 0:size],
            send_sem=send_sem,
            recv_sem=recv_sem,
            device_id={"sub": lax.rem(me + 1, owners)},
            device_id_type=MESH,
        )

    put_blocks(early_out, 0)
    early_blocks = spread(early_out, early_in, 2 * held, exchange_sem.at[0], exchange_sem.at[1])

    @pl.when(me < owners - 1)
    def _():
        for back in backs:
            back.wait_recv()

    @pl.when(me > 0)
    def _():
        for back in backs:
            back.wait_send()

    for part in range(2):
        at = part * half_rows
        top = window + (part + 1) * half_rows
        fill = tables[0][window - 16 : window, at : at + half_rows].astype(jnp.float32)
        edge = tables[0][top - 16 : top, at : at + half_rows].astype(jnp.float32)[15:16]
        amount = table_ref[0][2:3, at : at + half_rows]
        late_edge = last_row & jnp.broadcast_to(amount > 0, (16, half_rows))
        fill = fill + jnp.where(late_edge, jnp.broadcast_to(edge, (16, half_rows)), 0.0)
        tables[0][window - 16 : window, at : at + half_rows] = fill.astype(jnp.bfloat16)
    for level_num in range(2, levels + 1):
        begins = [floor_16(needed(level_num - 1, half, early)) for half in range(2)]
        ends = [ceil_16(needed(level_num - 1, half, window)) for half in range(2)]
        for half in range(2):
            advance(level_num, half, begins[half], ends[half])
        for half in range(2):
            given = ends[1] if level_num == levels else ends[half]
            finish(
                level_num,
                half,
                floor_16(needed(level_num, half, early)),
                ceil_16(needed(level_num, half, window)),
                given,
            )
    put_blocks(late_out, early)
    rest = window - 2 * rows
    tail = tables[levels - 1][2 * rows : window, :]
    tail = turn_over(jnp.concatenate([tail] * (LANES // rest), axis=0))
    row_spot = lax.broadcasted_iota(jnp.int32, (rows, LANES), 0)
    turned = window * me // rest % (LANES // rest)
    lane_spot = lax.broadcasted_iota(jnp.int32, (rows, LANES), 1) // rest
    tail = jnp.where((row_spot + lane_spot) % (LANES // rest) == turned, tail, 0.0).astype(jnp.bfloat16)
    packed_rows = rows * rest // LANES
    gather_rows = (
        lax.broadcasted_iota(jnp.int32, (packed_rows, rows), 1) // (LANES // rest)
        == lax.broadcasted_iota(jnp.int32, (packed_rows, rows), 0)
    )
    tail = jnp.dot(
        gather_rows.astype(jnp.float32).astype(jnp.bfloat16),
        tail,
        preferred_element_type=jnp.float32,
    ).astype(jnp.bfloat16)
    extra = packed_rows // owners
    for owner in range(owners):
        late_out[owner, 2 * held : 2 * held + extra, :] = tail[
            owner * extra : (owner + 1) * extra
        ]
    late_blocks = spread(late_out, late_in, 2 * held + extra, exchange_sem.at[2], exchange_sem.at[3])

    wide_lane = lax.broadcasted_iota(jnp.int32, (held, LANES), 1)
    pieces = [[] for _ in range(fold_size)]
    for source in range(owners):
        for at in range(0, window, LANES):
            fold, part = divmod(window * source + at, LANES)
            count = min(LANES, window - at)
            for where, low, high in (
                (fold, part, min(LANES, part + count)),
                (fold + 1, 0, part + count - LANES),
            ):
                if where < fold_size and low < high:
                    pieces[where].append((low, high, source, at >= early, at, part))
    rolled = {}

    def rolled_tile(source, late, at, part):
        if (source, at) not in rolled:
            if at < 2 * rows:
                place = (at - early if late else at) // LANES * held
                value = (late_in if late else early_in)[source, place : place + held, :]
                value = value.astype(jnp.float32)
                if part:
                    value = pltpu.roll(value, part, axis=1)
            else:
                value = late_in[source, 2 * held : 3 * held, :].astype(jnp.float32)
                value = jnp.concatenate(
                    [
                        pltpu.roll(
                            jnp.broadcast_to(value[row : row + 1], (LANES // rest, LANES)),
                            0,
                            axis=1,
                            stride=rest,
                            stride_axis=0,
                        )
                        for row in range(extra)
                    ],
                    axis=0,
                )
            rolled[source, at] = value
        return rolled[source, at]

    def assemble(which):
        for fold in range(fold_size):
            some = [piece for piece in sorted(pieces[fold]) if piece[3] == which]
            if not some:
                continue
            where = slice(fold * FOLD_PITCH, fold * FOLD_PITCH + held)
            value = None
            if which and len(some) < len(pieces[fold]):
                value = folded[where, :]
            for low, high, source, late, at, part in some:
                piece = rolled_tile(source, late, at, part)
                if value is None:
                    value = piece
                elif high == LANES:
                    value = jnp.where(wide_lane < low, value, piece)
                elif low == 0:
                    value = jnp.where(wide_lane < high, piece, value)
                else:
                    value = jnp.where((wide_lane >= low) & (wide_lane < high), piece, value)
            folded[where, :] = value

    early_blocks.wait_recv()
    assemble(False)
    for load in loads[3:]:
        load.wait()
    early_blocks.wait_send()
    late_blocks.wait_send()
    late_blocks.wait_recv()

    assemble(True)

    cosine, sine = twist_ref[0], twist_ref[1]
    for series in range(0, held, 2):
        pair = jnp.concatenate(
            [folded[pl.ds(series + side, fold_size, stride=FOLD_PITCH), :] for side in range(2)], axis=1
        )
        spun = jnp.dot(
            first_ref[...], pair.astype(jnp.bfloat16), preferred_element_type=jnp.float32
        )
        for side in range(2):
            real = spun[0:fold_size, side * LANES : (side + 1) * LANES]
            imag = spun[fold_size:, side * LANES : (side + 1) * LANES]
            at = (series + side) * fold_size
            twisted[at : at + fold_size, 0:LANES] = (real * cosine + imag * sine).astype(
                jnp.bfloat16
            )
            twisted[at : at + fold_size, LANES:] = (imag * cosine - real * sine).astype(
                jnp.bfloat16
            )
    half = fold_size
    scale = 1.0 / (length * channels)
    small_lane = lax.broadcasted_iota(jnp.int32, (half // 2, LANES), 1)
    for series in range(0, held, 4):
        at = series * fold_size
        waves = lax.dot_general(
            third_ref[...],
            twisted[at : at + 4 * fold_size, :],
            (((1,), (1,)), ((), ())),
            preferred_element_type=jnp.float32,
        )
        power = (waves[0:half] * waves[0:half] + waves[half:] * waves[half:]) * scale
        for side in range(2):
            even = power[0 : half // 2, side * LANES : (side + 1) * LANES]
            odd = power[half // 2 :, side * LANES : (side + 1) * LANES]
            left = jnp.where(small_lane < fold_size, even, pltpu.roll(odd, fold_size, axis=1))
            right = jnp.where(small_lane < fold_size, pltpu.roll(even, fold_size, axis=1), odd)
            spot = (series + 2 * side) * POWER_PITCH
            powers[spot : spot + half // 2, :] = left
            powers[spot + POWER_PITCH : spot + POWER_PITCH + half // 2, :] = right
    for block in range(0, held, GROUP):
        for tile in range(half // 2):
            out_ref[block : block + GROUP, tile * LANES : (tile + 1) * LANES] = powers[
                pl.ds(block * POWER_PITCH + tile, GROUP, stride=POWER_PITCH), :
            ]


def in_place(*operands):
    return [pltpu.with_memory_space_constraint(operand, pltpu.HBM) for operand in operands]


def local_sliced(samples, channel_order, merge_table):
    owners = lax.axis_size("sub")
    window, channels = samples.shape
    levels, _, rows = merge_table.shape
    held = rows // owners
    length = owners * (window - held)
    fold_size = length // LANES
    whole = window + rows
    order = channel_order.reshape(1, channels)
    first_table, twist, third_table = transform_tables(fold_size, length)
    return pl.pallas_call(
        functools.partial(merge_kernel, owners, length),
        out_shape=pltpu.VMEM((held, 64 * fold_size), jnp.float32),
        in_specs=[pl.BlockSpec(memory_space=pl.ANY)] * 6,
        out_specs=pl.BlockSpec(memory_space=pltpu.VMEM),
        scratch_shapes=[
            pltpu.VMEM((1, channels), jnp.int32),
            pltpu.VMEM((levels, 3, rows), jnp.int32),
            pltpu.VMEM((window, channels), jnp.bfloat16),
            pltpu.VMEM(first_table.shape, jnp.bfloat16),
            pltpu.VMEM(twist.shape, jnp.float32),
            pltpu.VMEM(third_table.shape, jnp.bfloat16),
            pltpu.VMEM((channels, channels), jnp.bfloat16),
            pltpu.VMEM((channels, channels), jnp.bfloat16),
            pltpu.VMEM((levels - 1, 2, rows // 2, rows), jnp.bfloat16),
            pltpu.VMEM((window, channels), jnp.float32),
            [pltpu.VMEM((2, whole, rows), jnp.float32)] * (levels - 1),
            [pltpu.VMEM((whole, rows), jnp.bfloat16)] * levels,
            pltpu.VMEM((rows, rows), jnp.bfloat16),
            pltpu.VMEM((rows, rows), jnp.bfloat16),
            pltpu.VMEM((owners, 2 * held, LANES), jnp.bfloat16),
            pltpu.VMEM((owners, 3 * held, LANES), jnp.bfloat16),
            pltpu.VMEM((owners, 2 * held, LANES), jnp.bfloat16),
            pltpu.VMEM((owners, 3 * held, LANES), jnp.bfloat16),
            pltpu.VMEM((FOLD_PITCH * fold_size, LANES), jnp.float32),
            pltpu.VMEM((held * fold_size, 2 * LANES), jnp.bfloat16),
            pltpu.VMEM((POWER_PITCH * held, LANES), jnp.float32),
            pltpu.SemaphoreType.DMA((4,)),
            pltpu.SemaphoreType.DMA((4,)),
            pltpu.SemaphoreType.DMA((6,)),
        ],
        compiler_params=pltpu.CompilerParams(
            vmem_limit_bytes=40 * 1024 * 1024, collective_id=0, has_side_effects=True
        ),
        name="merge_rows",
    )(*in_place(order, merge_table, samples, first_table, twist, third_table))


def is_sliced(window, channels, owners, rows, levels):
    held = rows // owners
    length = owners * (window - held)
    return (
        held == 16
        and window % 16 == 0
        and rows == 2 * LANES
        and channels == 2 * rows
        and rows == 2 ** (levels - 1)
        and length == 64 * LANES
        and window == 2 * rows + 16
        and owners == 16
    )


def local_any(samples, channel_order, merge_table):
    window, channels = samples.shape
    levels, _, rows = merge_table.shape
    if is_sliced(window, channels, lax.axis_size("sub"), rows, levels):
        return local_sliced(samples, channel_order, merge_table)
    return local(samples, channel_order, merge_table)


def solution(mesh):
    in_specs = (P(("groups", "sub"), None), P(), P())
    out_specs = P(("groups", "sub"), None)
    return jax.shard_map(local_any, mesh=mesh, in_specs=in_specs, out_specs=out_specs, check_vma=False)
```
